32 devices in a mesh: child: 2 (over y), row: 4 (over x, core), col: 4 (over z).
Axes of the slice: x: 2, y: 2, z: 4, core: 2. Of those that a mesh axis runs over, the one named last changes fastest.
Arguments:
- child_blocks: float32 [2, 4096, 4096], P('child', 'row', 'col'), as said below
- child_panels: bfloat16 [2, 4096, 1024], P('child', 'row'), may hold values from -0.1875 to 0.1875
- child_patterns: int32 [2, 16, 16], replicated, may hold values from 0 to 1, as said below
- child_maps: int32 [2, 16], replicated, may hold values from 0 to 23, as said below
- parent_place: int32 [24], replicated, may hold values from 0 to 23, as said below
- parent_front: float32 [6144, 6144], P(('child', 'row'), 'col'), as said below
Outputs:
- factored: float32 [6144, 6144], P(('child', 'row'), 'col')
The draws below stay inside these ranges and needn't reach their ends.
Inputs may be any that keep to these rules, and one draw needn't show every extreme that they name: `parent_place`: a permutation. The entries of one child are distinct; within each aligned block of 4 entries of one child, the values parent_place[child_maps[c, i]] // 6 are distinct. `child_patterns`: symmetric in its two tile dimensions, with ones on the diagonal. `child_blocks`: each child's block is symmetric. `parent_front`: symmetric; the diagonal entries inside stored tiles (parent_place[0], parent_place[0]) and (parent_place[1], parent_place[1]) lie between 200 and 400.
All inputs are finite; a program needn't handle non-finite values.
Results may differ from the reference program's by a relative error of at most 0.0003.
Values may be sent and summed in bfloat16 or wider, within the bound.
A program may use at most 128 MiB of HBM per device.

```python
import math
import jax
import jax.numpy as jnp
from jax import lax

TILE = 256
DEPTH = 1024
CHILD_TILES_DEV = 4
PARENT_TILES_DEV = 3
PANEL = 512
CHILD_TILES = 16
PARENT_TILES = 24
CHILD_ORDER = 4096
PARENT_ORDER = 6144


def move_front(within, slot_value, group_width, index_pos):
    target_group = slot_value // group_width
    target_pos = slot_value % group_width
    group_row = within[target_group]
    positions = jnp.arange(group_width)
    current = group_row[index_pos]
    new_row = jnp.where(group_row == target_pos, current, jnp.where(positions == index_pos, target_pos, group_row))
    return within.at[target_group].set(new_row)


def layout_tables(key):
    folded = jax.random.fold_in(key, 11)
    place_key, child_key = jax.random.split(folded)
    ordering = jax.random.permutation(place_key, PARENT_TILES).astype(jnp.int32)
    inverse = jnp.argsort(ordering).astype(jnp.int32)
    blocks = CHILD_TILES // CHILD_TILES_DEV
    stride = blocks // CHILD_TILES_DEV
    group_width = 2 * PARENT_TILES_DEV
    mappings = []
    for member in range(2):
        subkeys = jax.random.split(jax.random.fold_in(child_key, member), 4)
        relabel = jax.random.permutation(subkeys[0], blocks)
        block_order = jax.random.permutation(subkeys[1], blocks)
        within = jax.vmap(lambda subkey: jax.random.permutation(subkey, group_width))(jax.random.split(subkeys[2], blocks))
        within = move_front(within, ordering[PARENT_TILES - 1], group_width, 0)
        within = move_front(within, ordering[0], group_width, 1)
        position = jax.vmap(lambda subkey: jax.random.permutation(subkey, CHILD_TILES_DEV))(jax.random.split(subkeys[3], blocks))
        block_ids = jnp.arange(blocks)[:, None]
        ranks_row = jnp.arange(CHILD_TILES_DEV)[None, :]
        groups = relabel[(block_ids + ranks_row * stride) % blocks]
        slot_ids = groups * group_width + within[groups, ranks_row]
        tile_ids = block_order[block_ids] * CHILD_TILES_DEV + position
        mapping = jnp.zeros((CHILD_TILES,), jnp.int32).at[tile_ids.reshape(-1)].set(inverse[slot_ids].reshape(-1))
        mappings.append(mapping)
    return (ordering, jnp.stack(mappings).astype(jnp.int32))


def draw_parent_place(key, part):
    return layout_tables(key)[0]


def draw_child_maps(key, part):
    return layout_tables(key)[1]


def draw_child_patterns(key, part):
    folded = jax.random.fold_in(key, 23)
    first, second = jax.random.split(folded)
    density = jax.random.randint(first, (2, 1, 1), 35, 96)
    rolls = jax.random.randint(second, (2, CHILD_TILES, CHILD_TILES), 0, 100)
    lower = jnp.tril(rolls < density)
    symmetric = jnp.logical_or(lower, jnp.swapaxes(lower, 1, 2))
    identity = jnp.eye(CHILD_TILES, dtype=bool)[None]
    return jnp.where(identity, 1, symmetric.astype(jnp.int32)).astype(jnp.int32)


def draw_child_blocks(key, part):
    folded = jax.random.fold_in(key, 31)
    dims_shape = (2, CHILD_ORDER, CHILD_ORDER)
    raw_values = jax.random.normal(folded, dims_shape, jnp.float32)
    return (raw_values + jnp.swapaxes(raw_values, 1, 2)) / math.sqrt(2.0)


def draw_parent_front(key, part):
    ordering = layout_tables(key)[0]
    folded = jax.random.fold_in(key, 37)
    first, second = jax.random.split(folded)
    dims_shape = (PARENT_ORDER, PARENT_ORDER)
    raw_values = jax.random.normal(first, dims_shape, jnp.float32)
    symmetric = (raw_values + raw_values.T) / math.sqrt(2.0)
    tile_ids = jnp.arange(PARENT_ORDER) // TILE
    pivot = jnp.logical_or(tile_ids == ordering[0], tile_ids == ordering[1])
    strip = pivot[:, None] != pivot[None, :]
    scaled = jnp.where(strip, 4.0 * symmetric, symmetric)
    diagonal = jax.random.uniform(second, (PARENT_ORDER,), jnp.float32, 200.0, 400.0)
    identity = jnp.logical_and(jnp.eye(PARENT_ORDER, dtype=bool), pivot[:, None])
    return jnp.where(identity, diagonal[None, :], scaled)


def shard_levels(own_key, shape, cuts, least, largest):
    def one(dim, parts):
        draws = jax.random.uniform(jax.random.fold_in(jax.random.fold_in(own_key, 6), dim), (parts,), jnp.float32, least / len(cuts), largest / len(cuts))
        return jnp.repeat(jnp.exp(draws), shape[dim] // parts).reshape((-1,) + (1,) * (len(shape) - dim - 1))

    factor_of = one(*cuts[0])
    for cut in cuts[1:]:
        factor_of = factor_of * one(*cut)
    return factor_of


def noise(rng, shape, spread, limit, cuts=(), kind=jnp.bfloat16):
    factor_of = shard_levels(rng, shape, cuts, -0.22, 0.18) if cuts else 1.0
    values = jax.random.normal(rng, shape, jnp.float32) * spread * factor_of
    return jnp.minimum(jnp.maximum(values, -limit), limit).astype(kind)


def setup_inputs(seed: int = 0) -> dict:
    key_list = jax.random.split(jax.random.key(seed), 7)
    return {
        "child_blocks": draw_child_blocks(jax.random.fold_in(key_list[6], 71), 0),
        "child_panels": noise(key_list[1], (2, CHILD_ORDER, DEPTH), DEPTH ** -0.5, 0.1875, ((0, 2), (1, 4))),
        "child_patterns": draw_child_patterns(jax.random.fold_in(key_list[6], 71), 0),
        "child_maps": draw_child_maps(jax.random.fold_in(key_list[6], 71), 0),
        "parent_place": draw_parent_place(jax.random.fold_in(key_list[6], 71), 0),
        "parent_front": draw_parent_front(jax.random.fold_in(key_list[6], 71), 0),
    }


def reference(child_blocks, child_panels, child_patterns, child_maps, parent_place, parent_front):
    frontal = parent_front.reshape(PARENT_TILES, TILE, PARENT_TILES, TILE)
    for member in range(2):
        panel_data = child_panels[member].astype(jnp.float32)
        product = jnp.dot(panel_data.astype(jnp.float32), panel_data.T.astype(jnp.float32), precision=lax.Precision.HIGHEST, preferred_element_type=jnp.float32)
        tile_mask = child_patterns[member].astype(jnp.float32)
        update = (child_blocks[member] - product).reshape(CHILD_TILES, TILE, CHILD_TILES, TILE) * tile_mask[:, None, :, None]
        slot_list = parent_place[child_maps[member]]
        frontal = frontal.at[slot_list[:, None], :, slot_list[None, :], :].add(update.transpose(0, 2, 1, 3))
    panel_slots = parent_place[0:2]
    diagonal_block = frontal[panel_slots[:, None], :, panel_slots[None, :], :]
    diagonal_block = diagonal_block.transpose(0, 2, 1, 3).reshape(PANEL, PANEL)
    factor = jnp.linalg.cholesky(diagonal_block)
    column = frontal[:, :, panel_slots, :].reshape(PARENT_ORDER, PANEL)
    panel_rows = lax.linalg.triangular_solve(factor, column, left_side=False, lower=True, transpose_a=True)
    flattened = frontal.reshape(PARENT_ORDER, PARENT_ORDER)
    result = flattened - jnp.dot(panel_rows.astype(jnp.float32), panel_rows.T.astype(jnp.float32), precision=lax.Precision.HIGHEST, preferred_element_type=jnp.float32)
    result_tiles = result.reshape(PARENT_TILES, TILE, PARENT_TILES, TILE)
    result_tiles = result_tiles.at[:, :, panel_slots, :].set(panel_rows.reshape(PARENT_TILES, TILE, 2, TILE))
    return result_tiles.reshape(PARENT_ORDER, PARENT_ORDER)
```

```python
import functools

import jax
import jax.numpy as jnp
from jax import lax
from jax.experimental import pallas as pl
from jax.experimental.pallas import tpu as pltpu
from jax.sharding import Mesh, PartitionSpec as P

TILE = 256
F32 = jnp.float32
BF16 = jnp.bfloat16
META = 16
CODED = TILE + META
FULL = 32767.0
NT = (((1,), (1,)), ((), ()))
NN = (((1,), (0,)), ((), ()))


def dot(a, b, dims):
    return lax.dot_general(a, b, dims, preferred_element_type=F32)


def split(x):
    hi = x.astype(BF16)
    return hi, (x - hi.astype(F32)).astype(BF16)


def tile_call(kernel, grid, tables, operands, in_specs, out_shape, out_spec, name, cost=None, scratch=()):
    return pl.pallas_call(
        kernel,
        grid_spec=pltpu.PrefetchScalarGridSpec(
            num_scalar_prefetch=len(tables), grid=grid, in_specs=in_specs, out_specs=out_spec,
            scratch_shapes=list(scratch),
        ),
        out_shape=out_shape,
        name=name,
        cost_estimate=cost,
    )(*tables, *operands)


def powers(k):
    h = jnp.floor(k * 0.5)
    return jnp.exp2(h), jnp.exp2(k - h)


def encode(x):
    top = jnp.maximum(jnp.max(jnp.abs(x), axis=0, keepdims=True), 1e-37)
    k = jnp.ceil(jnp.log2(top) + 1e-3)
    p, r = powers(-k)
    part = jnp.clip(jnp.ceil(top * p * r * FULL), 1.0, FULL)
    q = jnp.clip(x * p * (r * (FULL * FULL / part)), -FULL, FULL)
    q = jnp.floor(q + 0.5).astype(jnp.int32)
    ids = lax.broadcasted_iota(jnp.int32, (META, x.shape[1]), 0)
    meta = jnp.where(ids == 0, k.astype(jnp.int32), jnp.where(ids == 1, part.astype(jnp.int32), 0))
    return q.astype(jnp.int16), meta.astype(jnp.int16)


def decode(code):
    n = code.shape[0] - META
    meta = code[n:, :].astype(jnp.int32).astype(F32)
    p, r = powers(meta[0:1, :])
    q = code[:n, :].astype(jnp.int32).astype(F32)
    return q * (meta[1:2, :] * (1.0 / (FULL * FULL)) * p) * r


def pick_kernel(idx, src, out):
    q, meta = encode(src[...])
    out[0, 0, :TILE, :] = q
    out[0, 0, TILE:, :] = meta


def diag_kernel(t, blk, front, ea, eb, out):
    k = pl.program_id(0) * 2 + pl.program_id(1)
    x = jnp.where(t[4, k] != 0, blk[...], 0.0) + jnp.where(t[5, k] != 0, front[...], 0.0)
    out[...] = x - jnp.where(t[6, k] != 0, dot(ea[...], eb[0], NT), 0.0)


def update_kernel(rows, fac, raw, panel, partner, out, coded):
    f = fac[pl.program_id(0), pl.program_id(1)]
    u = decode(raw[0, 0]) - dot(panel[...], partner[0], NT)
    u = jnp.where(f != 0, u, 0.0)
    out[0] = u
    q, meta = encode(u)
    coded[0, 0, :TILE, :] = q
    coded[0, 0, TILE:, :] = meta


def strip_kernel(t, upd, front, out, g):
    a, q = pl.program_id(0), pl.program_id(1)
    cd = pl.num_programs(1)
    k = a * cd + q
    x = jnp.where(t[2, k] != 0, upd[0], 0.0) + jnp.where(t[4, k] != 0, front[...], 0.0)
    rows = pl.ds(pl.multiple_of(q * TILE, TILE), TILE)
    g[rows, pl.ds(pl.multiple_of(a * TILE, TILE), TILE)] = x.T

    @pl.when(jnp.logical_and(a == 1, q == cd - 1))
    def _():
        n = out.shape[1] - META
        for p in range(out.shape[0]):
            code, meta = encode(g[p * n : (p + 1) * n, :])
            out[p, :n, :] = code
            out[p, n:, :] = meta


def solve_kernel(parts, inverse, out):
    g = decode(parts[0])
    for p in range(1, parts.shape[0]):
        g = g + decode(parts[p])
    w = lax.dot_general(g, inverse[...], NT, precision=lax.Precision.HIGHEST, preferred_element_type=F32)
    n = out.shape[0] - META
    code, meta = encode(w)
    out[:n, :] = code
    out[n:, :] = meta


def final_kernel(t, front, a0, b0, a1, b1, wr, wc, out, rh, rl, ch, cl):
    i, j = pl.program_id(0), pl.program_id(1)
    k = i * pl.num_programs(1) + j
    panel = t[12, k]

    @pl.when(k == 0)
    def _():
        for src, hi, lo in ((wr, rh, rl), (wc, ch, cl)):
            n = src.shape[1] - META
            for p in range(src.shape[0]):
                at = pl.ds(p * n, n)
                hi[at, :], lo[at, :] = split(decode(src[p]))

    ri = pl.ds(pl.multiple_of(i * TILE, TILE), TILE)

    @pl.when(panel == 0)
    def _():
        cj = pl.ds(pl.multiple_of(j * TILE, TILE), TILE)
        big = dot(rh[ri, :], ch[cj, :], NT)
        out[...] = front[...] - (big + (dot(rh[ri, :], cl[cj, :], NT) + dot(rl[ri, :], ch[cj, :], NT)))
        for m, src in enumerate((a0, b0, a1, b1)):

            @pl.when(t[8 + m, k] != 0)
            def _(src=src):
                out[...] = out[...] + decode(src[0])

    @pl.when(panel == 1)
    def _():
        out[...] = rh[ri, :TILE].astype(F32) + rl[ri, :TILE].astype(F32)

    @pl.when(panel == 2)
    def _():
        out[...] = rh[ri, TILE:].astype(F32) + rl[ri, TILE:].astype(F32)


MESH = pl.DeviceIdType.MESH


class Spot:
    def __init__(self):
        self.ci, self.rx = lax.axis_index("child"), lax.axis_index("rx")
        self.core, self.col = lax.axis_index("core"), lax.axis_index("col")
        self.rxn, self.cores, self.cols = lax.axis_size("rx"), lax.axis_size("core"), lax.axis_size("col")
        self.chips = lax.axis_size("child") * self.rxn
        self.chip = self.ci * self.rxn + self.rx
        self.other = {"core": 1 - self.core}

    def id(self, chip, core=None):
        core = self.core if core is None else core
        return {"child": chip // self.rxn, "rx": lax.rem(chip, self.rxn), "core": core}

    def turn(self, at, d, n):
        return lax.rem(at + (d % n), n)


def greet(ids):
    bar = pltpu.get_barrier_semaphore()
    for i in ids:
        pl.semaphore_signal(bar, inc=1, device_id=i, device_id_type=MESH)
    pl.semaphore_wait(bar, len(ids))


def push(src, dst, send, recv, to):
    cp = pltpu.make_async_remote_copy(
        src_ref=src, dst_ref=dst, send_sem=send, recv_sem=recv, device_id=to, device_id_type=MESH
    )
    cp.start()
    return cp


def remote_call(kernel, operands, out_shape, out_specs, scratch, cid, name, flops=0):
    return pl.pallas_call(
        kernel,
        out_shape=out_shape,
        in_specs=[pl.BlockSpec(memory_space=pltpu.VMEM)] * len(operands),
        out_specs=out_specs,
        scratch_shapes=scratch,
        compiler_params=pltpu.CompilerParams(collective_id=cid, has_side_effects=True),
        cost_estimate=pl.CostEstimate(flops=flops, bytes_accessed=1 << 20, transcendentals=0),
        name=name,
    )(*operands)


ANY = pl.BlockSpec(memory_space=pl.ANY)
IN_VMEM = pl.BlockSpec(memory_space=pltpu.VMEM)


def panel_kernel(x, out, loc, ss, rs, fs, fr):
    s = Spot()
    n = s.rxn
    me = s.rx * s.cores + s.core
    peers = [{"rx": s.turn(s.rx, d, n)} for d in range(1, n)]
    greet(peers + [s.other])
    keep = pltpu.make_async_copy(x, out.at[me], loc)
    keep.start()
    cps = [push(x, out.at[me], ss.at[d], rs.at[d], to) for d, to in enumerate(peers, 1)]
    fwd = [push(x, out.at[me], fs.at[0], fr.at[0], s.other)]
    for d, cp in enumerate(cps, 1):
        cp.wait_recv()
        at = s.turn(s.rx, -d, n) * s.cores + s.core
        fwd.append(push(out.at[at], out.at[at], fs.at[d], fr.at[d], s.other))
    keep.wait()
    for cp in cps:
        cp.wait_send()
    for cp in fwd:
        cp.wait()


def panel_gather(x):
    n = lax.axis_size("rx")
    shape = (n * lax.axis_size("core"),) + x.shape
    dma = pltpu.SemaphoreType.DMA
    return remote_call(
        panel_kernel, (x,), jax.ShapeDtypeStruct(shape, x.dtype), ANY,
        [dma, dma((n,)), dma((n,)), dma((n,)), dma((n,))], 0, "panels",
    )


def sum_kernel(x, out, half, mine, got, part, zgot, ss0, rs0, ss1, rs1, ss2, rs2, ss3, rs3, ss4, rs4, ss5, rs5):
    s = Spot()
    nc, nz = s.chips, s.cols
    chips = [s.turn(s.chip, d, nc) for d in range(1, nc)]
    cols = [s.turn(s.col, d, nz) for d in range(1, nz)]
    greet([s.other] + [s.id(t) for t in chips] + [{"col": t} for t in cols])
    cp = push(x.at[1 - s.core], half, ss0, rs0, s.other)
    cp.wait()
    mine[...] = x[s.core] + half[...]
    cps = [push(mine.at[t], got.at[d], ss1.at[d], rs1.at[d], s.id(t)) for d, t in enumerate(chips)]
    for cp in cps:
        cp.wait()
    total = mine[s.chip]
    for d in range(nc - 1):
        total = total + got[d]
    part[...] = total
    cps = [push(part.at[t], zgot.at[d], ss2.at[d], rs2.at[d], {"col": t}) for d, t in enumerate(cols)]
    for cp in cps:
        cp.wait()
    total = part[s.col]
    for d in range(nz - 1):
        total = total + zgot[d]
    out[s.core, s.chip, s.col] = total
    own = out.at[s.core, s.chip, s.col]
    cps = [push(own, own, ss3.at[d], rs3.at[d], {"col": t}) for d, t in enumerate(cols)]
    for cp in cps:
        cp.wait()
    own = out.at[s.core, s.chip]
    cps = [push(own, own, ss4.at[d], rs4.at[d], s.id(t)) for d, t in enumerate(chips)]
    for cp in cps:
        cp.wait()
    own = out.at[s.core]
    push(own, own, ss5, rs5, s.other).wait()


def sum_all(x):
    n = x.shape[0]
    nc, nz = lax.axis_size(("child", "rx")), lax.axis_size("col")
    tail = (n // (2 * nc * nz), n)
    full = jax.ShapeDtypeStruct((2, nc, nz) + tail, F32)
    dma = pltpu.SemaphoreType.DMA
    sems = [dma, dma, dma((nc,)), dma((nc,)), dma((nz,)), dma((nz,)), dma((nz,)), dma((nz,)), dma((nc,)), dma((nc,)), dma, dma]
    half, part = (nc, nz) + tail, (nz,) + tail
    vm = [pltpu.VMEM(z, F32) for z in (half, half, (nc - 1,) + part, part, (nz - 1,) + tail)]
    out = remote_call(sum_kernel, (x.reshape(full.shape),), full, IN_VMEM, vm + sems, 1, "total")
    return out.reshape(n, n)


def scatter_kernel(x, out, loc, ss, rs):
    s = Spot()
    n = x.shape[0]
    me = s.chip * s.cores + s.core
    peers = [s.turn(me, d, n) for d in range(1, n)]
    ids = [s.id(t // s.cores, lax.rem(t, s.cores)) for t in peers]
    greet(ids)
    keep = pltpu.make_async_copy(x.at[me], out.at[me], loc)
    keep.start()
    cps = [push(x.at[t], out.at[me], ss.at[d], rs.at[d], i) for d, (t, i) in enumerate(zip(peers, ids))]
    keep.wait()
    for cp in cps:
        cp.wait()


def scatter(x):
    n = x.shape[0]
    dma = pltpu.SemaphoreType.DMA
    return remote_call(
        scatter_kernel, (x,), jax.ShapeDtypeStruct(x.shape, x.dtype), ANY, [dma, dma((n,)), dma((n,))], 2, "strips"
    )


def spread_kernel(x, wc, wr, zbuf, loc, zs, zr, ps, pr, fs, fr, ws, wx, wl):
    s = Spot()
    nc, nz, half = s.chips, s.cols, wr.shape[0]
    me = s.chip * s.cores + s.core
    slot = lax.rem(me, half)
    n = nc * s.cores
    chips = [s.turn(s.chip, d, nc) for d in range(1, nc)]
    cols = [s.turn(s.col, d, nz) for d in range(1, nz)]
    plane = [s.turn(me, d, n) for d in range(1, n)]
    greet([s.id(t // s.cores, lax.rem(t, s.cores)) for t in plane] + [{"col": t} for t in cols])
    keep = pltpu.make_async_copy(x, wc.at[me], loc)
    keep.start()
    zc = [push(x, zbuf.at[s.col], zs.at[d], zr.at[d], {"col": t}) for d, t in enumerate(cols, 1)]
    pc = [push(x, wc.at[me], ps.at[d], pr.at[d], s.id(t)) for d, t in enumerate(chips, 1)]
    fc = [push(x, wc.at[me], fs.at[0], fr.at[0], s.other)]

    def hand(src, z, d):
        here = jnp.logical_and(z == s.chip, s.ci == s.core)

        @pl.when(here)
        def _():
            pltpu.make_async_copy(src, wr.at[slot], wl).start()

        @pl.when(jnp.logical_not(here))
        def _():
            push(src, wr.at[slot], ws.at[d], wx.at[slot], s.id(z, s.ci))

    def handed(src, z, d):
        here = jnp.logical_and(z == s.chip, s.ci == s.core)

        @pl.when(here)
        def _():
            pltpu.make_async_copy(src, wr.at[slot], wl).wait()

        @pl.when(jnp.logical_not(here))
        def _():
            pltpu.make_async_remote_copy(
                src_ref=src, dst_ref=wr.at[slot], send_sem=ws.at[d], recv_sem=wx.at[slot],
                device_id=s.id(z, s.ci), device_id_type=MESH,
            ).wait_send()

    hand(x, s.col, 0)
    back = [s.turn(s.col, -d, nz) for d in range(nz)]
    for d in range(1, max(nz, nc)):
        if d < nz:
            zc[d - 1].wait_recv()
            hand(zbuf.at[back[d]], back[d], d)
        if d < nc:
            pc[d - 1].wait_recv()
            at = s.turn(s.chip, -d, nc) * s.cores + s.core
            fc.append(push(wc.at[at], wc.at[at], fs.at[d], fr.at[d], s.other))
    for d in range(nz):
        handed(x if d == 0 else zbuf.at[back[d]], back[d], d)
    for j in range(half):

        @pl.when(jnp.logical_or(s.ci != s.core, slot != j))
        def _(j=j):
            pltpu.make_async_remote_copy(
                src_ref=wr.at[j], dst_ref=wr.at[j], send_sem=ws.at[0], recv_sem=wx.at[j],
                device_id=s.other, device_id_type=MESH,
            ).wait_recv()

    keep.wait()
    for cp in zc + pc:
        cp.wait_send()
    for cp in fc:
        cp.wait()


def spread(x):
    nc, nz = lax.axis_size(("child", "rx")), lax.axis_size("col")
    dma = pltpu.SemaphoreType.DMA
    sems = [dma] + [dma((nz,))] * 2 + [dma((nc,))] * 4 + [dma((nz,)), dma((nc,)), dma]
    shapes = [jax.ShapeDtypeStruct((n,) + x.shape, x.dtype) for n in (2 * nc, nc)]
    return remote_call(
        spread_kernel, (x,), shapes, [ANY, ANY], [pltpu.VMEM((nz,) + x.shape, x.dtype)] + sems, 3, "spread"
    )


BASE = 128
FACTOR_WORK = 40_000_000_000
WIDE = 8


def base_inverse(a_ref, d_ref, x_ref):
    n, step = a_ref.shape[0], 8
    ids = lax.broadcasted_iota(jnp.int32, (step, n), 0)
    lanes = lax.broadcasted_iota(jnp.int32, (step, n), 1)
    a = [a_ref[i * step : (i + 1) * step, :] for i in range(n // step)]
    x = [(lanes == ids + i * step).astype(F32) for i in range(n // step)]
    for j in range(0, n, WIDE):
        c0 = j // step
        chunks = range(c0, n // step)
        cols = [[jnp.broadcast_to(a[i][:, j + t : j + t + 1], (step, n)) for i in chunks] for t in range(WIDE)]
        at = [j + t - c0 * step for t in range(WIDE)]
        rows = [a[c0][p : p + 1, :] for p in at]
        xrows = [x[c0][p : p + 1, :] for p in at]
        for t in range(WIDE):
            pivot = cols[t][0][at[t] : at[t] + 1, :]
            d_ref[j + t : j + t + 1, :] = pivot
            inv = 1.0 / pivot
            low = [c * inv for c in cols[t]]
            low[0] = jnp.where(ids > at[t], low[0], 0.0)
            for s in range(t + 1, WIDE):
                f = cols[t][0][at[s] : at[s] + 1, :]
                g = f * inv
                cols[s] = [c - l * f for c, l in zip(cols[s], low)]
                rows[s] = rows[s] - g * rows[t]
                xrows[s] = xrows[s] - g * xrows[t]
            for n_, i in enumerate(chunks):
                a[i] = a[i] - low[n_] * rows[t]
                x[i] = x[i] - low[n_] * xrows[t]
    for i in range(n // step):
        x_ref[i * step : (i + 1) * step, :] = x[i] * (1.0 / jnp.sqrt(d_ref[i * step : (i + 1) * step, :]))


def factor_kernel(a_in, y, a, blk, piv, inv):
    n = a.shape[0]
    high = functools.partial(lax.dot_general, precision=lax.Precision.HIGHEST, preferred_element_type=F32)
    ids = lax.broadcasted_iota(jnp.int32, (n, n), 0)
    a[...] = a_in[...]
    y[...] = (ids == lax.broadcasted_iota(jnp.int32, (n, n), 1)).astype(F32)

    def one(k, carry):
        at = pl.ds(pl.multiple_of(k * BASE, BASE), BASE)
        blk[...] = a[at, at]
        base_inverse(blk, piv, inv)
        low = high(a[:, at], inv[...], NT)
        low = jnp.where(ids[:, :BASE] >= (k + 1) * BASE, low, 0.0)
        yk = high(inv[...], y[at, :], (((1,), (0,)), ((), ())))
        a[...] = a[...] - high(low, low, NT)
        y[...] = y[...] - high(low, yk, (((1,), (0,)), ((), ())))
        y[at, :] = yk
        return carry

    lax.fori_loop(0, n // BASE, one, 0)


def factor_inverse(d):
    n = d.shape[0]
    return pl.pallas_call(
        factor_kernel,
        out_shape=jax.ShapeDtypeStruct(d.shape, F32),
        scratch_shapes=[pltpu.VMEM((n, n), F32)] + [pltpu.VMEM((BASE, BASE), F32)] * 3,
        name="factor",
        cost_estimate=pl.CostEstimate(flops=FACTOR_WORK, bytes_accessed=8 * n * n, transcendentals=0),
    )(d)


def body(child_blocks, child_panels, child_patterns, child_maps, parent_place, parent_front):
    ci = lax.axis_index("child")
    rx = lax.axis_index("rx")
    core = lax.axis_index("core")
    col = lax.axis_index("col")
    cores = lax.axis_size("core")
    rxn = lax.axis_size("rx")
    row = rx * cores + core
    rown = rxn * cores
    chips = lax.axis_size("child") * rxn
    chip = ci * rxn + rx
    group = ci * rown + row
    block = child_blocks[0]
    own = child_panels[0]
    depth = own.shape[1]
    width = block.shape[0]
    td = width // TILE
    blocks = child_maps.shape[1] // td
    rd = parent_front.shape[0] // TILE
    cd = parent_front.shape[1] // TILE
    slots_n = parent_place.shape[0]
    i32 = jnp.int32

    slots = jnp.sum(
        jnp.where(child_maps[:, :, None] == jnp.arange(slots_n, dtype=i32), parent_place, 0), axis=2
    )
    tiles = jnp.arange(child_maps.shape[1], dtype=i32)
    hit = slots[:, None, :] == jnp.arange(slots_n, dtype=i32)[None, :, None]
    inv = jnp.sum(jnp.where(hit, tiles + 1, 0), axis=2) - 1
    mine = lax.dynamic_index_in_dim(slots, ci, 0, keepdims=False).reshape(blocks, td)
    inv_own = lax.dynamic_index_in_dim(inv, ci, 0, keepdims=False)
    pat = lax.dynamic_index_in_dim(child_patterns, ci, 0, keepdims=False)
    m = (mine // cd)[:, None, :] == jnp.arange(chips, dtype=i32)[None, :, None]
    which = jnp.sum(jnp.where(m, jnp.arange(td, dtype=i32), 0), axis=2)
    there = jnp.any(m, axis=2).astype(i32)
    row_tile = lax.dynamic_index_in_dim(which, row, 0, keepdims=False)
    row_ok = lax.dynamic_index_in_dim(there, row, 0, keepdims=False)
    out_tile = lax.dynamic_index_in_dim(which, col, 0, keepdims=False)
    in_tile = lax.dynamic_index_in_dim(which, col, 1, keepdims=False)
    in_ok = lax.dynamic_index_in_dim(there, col, 1, keepdims=False)
    e = parent_place[:2]
    ie = inv_own[e]

    outgoing = tile_call(
        pick_kernel, (blocks, td), (out_tile,), (block,),
        [pl.BlockSpec((TILE, TILE), lambda z, r, i: (r, i[z]))],
        jax.ShapeDtypeStruct((blocks, td, CODED, TILE), jnp.int16),
        pl.BlockSpec((1, 1, CODED, TILE), lambda z, r, i: (z, r, 0, 0)), "pick",
    )
    part = lax.dynamic_slice(own, (row_tile[col] * TILE, 0), (TILE, depth))
    part = jnp.where(row_ok[col] != 0, part, jnp.zeros_like(part))

    e_here = jnp.logical_and(ie >= 0, ie // td == row)
    part, outgoing = lax.optimization_barrier((part, outgoing))
    raw = lax.all_to_all(outgoing, "col", split_axis=0, concat_axis=0, tiled=True)
    partner = panel_gather(part)
    pair_a = jnp.array([0, 0, 1, 1], i32)
    pair_b = jnp.array([0, 1, 0, 1], i32)
    ia, ib, ea, eb = ie[pair_a], ie[pair_b], e[pair_a], e[pair_b]
    live = (ia >= 0) & (ib >= 0) & (pat[jnp.maximum(ia, 0), jnp.maximum(ib, 0)] != 0)
    table = jnp.stack([
        jnp.maximum(ia, 0) % td, jnp.maximum(ib, 0) % td, ea % rd, eb % cd,
        live & (ia // td == row) & (ib // td == col),
        (ea // rd == group) & (eb // cd == col),
        live & (ia // td == row) & (eb // cd == col), jnp.maximum(ib, 0) // td,
    ]).astype(i32)
    diag_part = tile_call(
        diag_kernel, (2, 2), (table,), (block, parent_front, own, partner),
        [
            pl.BlockSpec((TILE, TILE), lambda a, b, t: (t[0, a * 2 + b], t[1, a * 2 + b])),
            pl.BlockSpec((TILE, TILE), lambda a, b, t: (t[2, a * 2 + b], t[3, a * 2 + b])),
            pl.BlockSpec((TILE, depth), lambda a, b, t: (t[0, a * 2 + b], 0)),
            pl.BlockSpec((1, TILE, depth), lambda a, b, t: (t[7, a * 2 + b], 0, 0)),
        ],
        jax.ShapeDtypeStruct((2 * TILE, 2 * TILE), F32),
        pl.BlockSpec((TILE, TILE), lambda a, b, t: (a, b)), "diag",
    )
    plane = ("child", "rx", "core")
    diagonal = sum_all(diag_part)
    inverse = factor_inverse(diagonal)

    wide = blocks // cores
    col_ids = jnp.arange(blocks, dtype=i32) * td + in_tile
    factors = pat[row * td + row_tile][:, col_ids] * row_ok[:, None] * in_ok[None, :]
    update, coded = tile_call(
        update_kernel, (chips, blocks), (row_tile, factors), (raw, own, partner),
        [
            pl.BlockSpec((1, 1, CODED, TILE), lambda p, b, r, f: (b, r[p], 0, 0)),
            pl.BlockSpec((TILE, depth), lambda p, b, r, f: (r[p], 0)),
            pl.BlockSpec((1, TILE, depth), lambda p, b, r, f: (b, 0, 0)),
        ],
        [
            jax.ShapeDtypeStruct((chips, TILE, blocks * TILE), F32),
            jax.ShapeDtypeStruct((chips, cores, CODED, wide * TILE), jnp.int16),
        ],
        [
            pl.BlockSpec((1, TILE, TILE), lambda p, b, r, f: (p, 0, b)),
            pl.BlockSpec((1, 1, CODED, TILE), lambda p, b, r, f: (p, b // wide, 0, b % wide)),
        ], "update",
    )
    coded = coded.reshape((chips * cores,) + coded.shape[2:])
    first = lax.all_to_all(coded, plane, split_axis=0, concat_axis=0, tiled=True)
    second = lax.ppermute(first, "core", [(k, (k + 1) % 2) for k in range(2)])

    my_cols = lax.dynamic_slice_in_dim(inv, col * cd, cd, 1)
    my_rows = lax.dynamic_slice_in_dim(inv, group * rd, rd, 1)
    cols_own = lax.dynamic_index_in_dim(my_cols, ci, 0, keepdims=False)
    grid_q = jnp.broadcast_to(jnp.arange(cd, dtype=i32), (2, cd))
    e2 = jnp.broadcast_to(e[:, None], (2, cd))
    cols2 = jnp.broadcast_to(cols_own[None, :], (2, cd))
    table = jnp.stack([
        e2 // cd, jnp.maximum(cols2, 0) // td,
        (e_here[:, None] & (cols2 >= 0)),
        e2 % rd, (e2 // rd == group),
    ]).astype(i32).reshape(5, 2 * cd)
    share = cd * TILE // (chips * cores)
    strip_part = tile_call(
        strip_kernel, (2, cd), (table,), (update, parent_front),
        [
            pl.BlockSpec((1, TILE, TILE), lambda a, q, t: (t[0, a * cd + q], 0, t[1, a * cd + q])),
            pl.BlockSpec((TILE, TILE), lambda a, q, t: (t[3, a * cd + q], q)),
        ],
        jax.ShapeDtypeStruct((chips * cores, share + META, 2 * TILE), jnp.int16),
        pl.BlockSpec((chips * cores, share + META, 2 * TILE), lambda a, q, t: (0, 0, 0)), "strip",
        scratch=[pltpu.VMEM((cd * TILE, 2 * TILE), F32)],
    )
    piece = pl.pallas_call(
        solve_kernel, out_shape=jax.ShapeDtypeStruct(strip_part.shape[1:], jnp.int16), name="solve"
    )(scatter(strip_part), inverse)
    wc, wr = spread(piece)

    rr = jnp.broadcast_to(my_rows[:, :, None], (2, rd, cd))
    cc = jnp.broadcast_to(my_cols[:, None, :], (2, rd, cd))
    ok = (rr >= 0) & (cc >= 0)
    send_row = jnp.maximum(rr, 0) // td
    from_b = jnp.maximum(cc, 0) // td
    same = from_b // wide == core
    send = jnp.arange(2, dtype=i32)[:, None, None] * rown + send_row
    from_b = from_b % wide
    lists = []
    for c in range(2):
        for kind in (same, ~same):
            flag = ok[c] & kind[c]
            lists.append((jnp.where(flag, send[c], 0), jnp.where(flag, from_b[c], 0), flag.astype(i32)))
    here = col * cd + jnp.arange(cd, dtype=i32)
    panel = jnp.where(here == e[0], 1, jnp.where(here == e[1], 2, 0))
    rows = [x[n] for n in (0, 1) for x in lists] + [x[2] for x in lists]
    rows.append(jnp.broadcast_to(panel, (rd, cd)))
    table = jnp.stack(rows).reshape(13, rd * cd)

    def from_list(n):
        return pl.BlockSpec(
            (1, CODED, TILE), lambda i, j, t: (t[n, i * cd + j], 0, t[4 + n, i * cd + j])
        )

    return tile_call(
        final_kernel, (rd, cd), (table,), (parent_front, first, second, first, second, wr, wc),
        [pl.BlockSpec((TILE, TILE), lambda i, j, t: (i, j))] + [from_list(n) for n in range(4)] + [
            pl.BlockSpec(wr.shape, lambda i, j, t: (0, 0, 0)),
            pl.BlockSpec(wc.shape, lambda i, j, t: (0, 0, 0)),
        ],
        jax.ShapeDtypeStruct(parent_front.shape, F32),
        pl.BlockSpec((TILE, TILE), lambda i, j, t: (i, j)), "final",
        scratch=[pltpu.VMEM((n * TILE, 2 * TILE), BF16) for n in (rd, rd, cd, cd)],
    )


def solution(mesh):
    child, row, col = mesh.devices.shape
    cores = child * row // col
    fine = Mesh(mesh.devices.reshape(child, row // cores, cores, col), ("child", "rx", "core", "col"))
    return jax.shard_map(
        body,
        mesh=fine,
        in_specs=(
            P("child", ("rx", "core"), "col"),
            P("child", ("rx", "core"), None),
            P(),
            P(),
            P(),
            P(("child", "rx", "core"), "col"),
        ),
        out_specs=P(("child", "rx", "core"), "col"),
        check_vma=False,
    )
```

```python
import functools
import math

import jax
import jax.numpy as jnp
from jax import lax
from jax.experimental import pallas as pl
from jax.experimental.pallas import tpu as pltpu
from jax.sharding import Mesh, PartitionSpec as P

TILE = 256
F32 = jnp.float32
BF16 = jnp.bfloat16
META = 16
CODED = TILE + META
FULL = 32767.0
NT = (((1,), (1,)), ((), ()))
NN = (((1,), (0,)), ((), ()))


def dot(a, b, dims):
    return lax.dot_general(a, b, dims, preferred_element_type=F32)


def split(x):
    hi = x.astype(BF16)
    return hi, (x - hi.astype(F32)).astype(BF16)


def tile_call(kernel, grid, tables, operands, in_specs, out_shape, out_spec, name, cost=None, scratch=()):
    return pl.pallas_call(
        kernel,
        grid_spec=pltpu.PrefetchScalarGridSpec(
            num_scalar_prefetch=len(tables), grid=grid, in_specs=in_specs, out_specs=out_spec,
            scratch_shapes=list(scratch),
        ),
        out_shape=out_shape,
        name=name,
        cost_estimate=cost,
    )(*tables, *operands)


def powers(k):
    h = jnp.floor(k * 0.5)
    return jnp.exp2(h), jnp.exp2(k - h)


def encode(x):
    top = jnp.maximum(jnp.max(jnp.abs(x), axis=0, keepdims=True), 1e-37)
    k = jnp.ceil(jnp.log2(top) + 1e-3)
    p, r = powers(-k)
    part = jnp.clip(jnp.ceil(top * p * r * FULL), 1.0, FULL)
    q = jnp.clip(x * p * (r * (FULL * FULL / part)), -FULL, FULL)
    q = jnp.floor(q + 0.5).astype(jnp.int32)
    ids = lax.broadcasted_iota(jnp.int32, (META, x.shape[1]), 0)
    meta = jnp.where(ids == 0, k.astype(jnp.int32), jnp.where(ids == 1, part.astype(jnp.int32), 0))
    return q.astype(jnp.int16), meta.astype(jnp.int16)


def decode(code):
    n = code.shape[0] - META
    meta = code[n:, :].astype(jnp.int32).astype(F32)
    p, r = powers(meta[0:1, :])
    q = code[:n, :].astype(jnp.int32).astype(F32)
    return q * (meta[1:2, :] * (1.0 / (FULL * FULL)) * p) * r


def find(maps, place, child, block, group, td, width):
    at = jnp.int32(0)
    ok = jnp.int32(0)
    for t in range(td):
        hit = place[maps[child, block * td + t]] // width == group
        at = jnp.where(hit, t, at)
        ok = jnp.where(hit, 1, ok)
    return at, ok


def pick_kernel(td, cd, pos, maps, place, src, panel, out, part):
    n = out.shape[1]
    for r in range(n):
        q, meta = encode(src[r * TILE : (r + 1) * TILE, :])
        out[0, r, :TILE, :] = q
        out[0, r, TILE:, :] = meta

    @pl.when(pl.program_id(0) == 0)
    def _():
        ok = find(maps, place, pos[0], pos[1], pos[2], td, cd)[1]
        part[...] = jnp.where(ok != 0, panel[...], jnp.zeros_like(panel))


def plan_kernel(dims, pos, maps, place, pat, rowt, fac, diagt, stript, fint, inv):
    td, cd, rd, chips, blocks, cores, rown = dims
    ci, row, col, core = pos[0], pos[1], pos[2], pos[3]
    group = ci * rown + row
    wide = blocks // cores
    slots_n, tiles_n = place.shape[0], maps.shape[1]

    @pl.loop(0, slots_n)
    def _(k):
        inv[0, k] = -1
        inv[1, k] = -1

    @pl.loop(0, tiles_n)
    def _(k):
        inv[0, place[maps[0, k]]] = k
        inv[1, place[maps[1, k]]] = k

    cols = [find(maps, place, ci, b, col, td, cd) for b in range(blocks)]
    for x in range(chips):
        at, ok = find(maps, place, ci, row, x, td, cd)
        rowt[x] = at
        for b, (tile, good) in enumerate(cols):
            fac[x, b] = pat[ci, row * td + at, b * td + tile] * ok * good
    e = (place[0], place[1])
    ie = (inv[ci, e[0]], inv[ci, e[1]])
    le = [jnp.maximum(i, 0) for i in ie]
    own = [((ie[a] >= 0) & (le[a] // td == row)).astype(jnp.int32) for a in range(2)]
    for a in range(2):
        rowt[chips + a] = jnp.where(own[a] != 0, e[a] // cd, -1)
        for b in range(2):
            k = a * 2 + b
            live = own[a] * (ie[b] >= 0).astype(jnp.int32) * pat[ci, le[a], le[b]]
            diagt[0, k] = le[a] % td
            diagt[1, k] = le[b] % td
            diagt[2, k] = e[a] % rd
            diagt[3, k] = e[b] % cd
            diagt[4, k] = live * (le[b] // td == col).astype(jnp.int32)
            diagt[5, k] = ((e[a] // rd == group) & (e[b] // cd == col)).astype(jnp.int32)
            diagt[6, k] = live * (e[b] // cd == col).astype(jnp.int32)
            diagt[7, k] = le[b] // td
        stript[0, a] = e[a] % rd

        for q in range(cd):
            slot = col * cd + q
            iq = inv[ci, slot]
            free = ((slot != e[0]) & (slot != e[1])).astype(jnp.int32)
            stript[1 + a, q] = jnp.maximum(iq, 0) // td
            stript[3 + a, q] = own[a] * free * (iq >= 0).astype(jnp.int32)
            stript[5 + a, q] = free * (e[a] // rd == group).astype(jnp.int32)
    for k in range(2, cd):
        stript[0, k] = 0

    @pl.loop(0, rd * cd)
    def _(k):
        slot = col * cd + k % cd
        for c in range(2):
            r, t = inv[c, group * rd + k // cd], inv[c, slot]
            ok = ((r >= 0) & (t >= 0)).astype(jnp.int32)
            b = jnp.maximum(t, 0) // td
            same = (b // wide == core).astype(jnp.int32)
            fint[3 * c, k] = c * rown + jnp.maximum(r, 0) // td
            fint[3 * c + 1, k] = b % wide
            fint[3 * c + 2, k] = ok * (2 - same)
        fint[6, k] = jnp.where(slot == e[0], 1, jnp.where(slot == e[1], 2, 0))


def diag_kernel(t, blk, front, ea, eb, out):
    k = pl.program_id(0) * 2 + pl.program_id(1)
    x = jnp.where(t[4, k] != 0, blk[...], 0.0) + jnp.where(t[5, k] != 0, front[...], 0.0)
    out[...] = x - jnp.where(t[6, k] != 0, dot(ea[...], eb[0], NT), 0.0)


def update_kernel(rowt, fac, raw, panel, partner, strip, coded):
    p = pl.program_id(0)
    chips = pl.num_programs(0)
    blocks = partner.shape[0]
    wide = coded.shape[3] // TILE

    @pl.when(p == 0)
    def _():
        strip[...] = jnp.zeros_like(strip)

    for b in range(blocks):
        u = decode(raw[b, 0]) - dot(panel[...], partner[b], NT)
        u = jnp.where(fac[p, b] != 0, u, 0.0)
        at = slice(b % wide * TILE, (b % wide + 1) * TILE)
        q, meta = encode(u)
        coded[0, b // wide, :TILE, at] = q
        coded[0, b // wide, TILE:, at] = meta
        for a in range(2):

            @pl.when(rowt[chips + a] == p)
            def _(a=a, u=u, b=b):
                strip[a, :, b * TILE : (b + 1) * TILE] = u


def strip_kernel(t, upd, f0, f1, out, g):
    cd = t.shape[1]
    some = sum(t[n, q] for n in range(3, 7) for q in range(cd))

    @pl.when(some == 0)
    def _():
        out[...] = jnp.zeros_like(out)

    @pl.when(some != 0)
    def _():
        g[...] = jnp.zeros_like(g)
        for q in range(cd):
            for a, f in enumerate((f0, f1)):

                @pl.when(t[3 + a, q] + t[5 + a, q] != 0)
                def _(q=q, a=a, f=f):
                    at = pl.ds(pl.multiple_of(t[1 + a, q] * TILE, TILE), TILE)
                    x = jnp.where(t[3 + a, q] != 0, upd[a, :, at], 0.0)
                    x = x + jnp.where(t[5 + a, q] != 0, f[:, q * TILE : (q + 1) * TILE], 0.0)
                    g[q * TILE : (q + 1) * TILE, a * TILE : (a + 1) * TILE] = x.T

        n = out.shape[2] - META
        for p in range(out.shape[1]):
            for k in range(out.shape[0]):
                m = p * out.shape[0] + k
                code, meta = encode(g[m * n : (m + 1) * n, :])
                out[k, p, :n, :] = code
                out[k, p, n:, :] = meta


def solve_kernel(pos, place, parts, diagonal, inverse, out):
    n = out.shape[0] - META
    g = decode(parts[0])
    for p in range(1, parts.shape[0]):
        g = g + decode(parts[p])
    unit = math.gcd(n, TILE)
    rows = []
    for u in range(n // unit):
        first = pos[4] * n + u * unit
        slot, off = first // TILE, first % TILE
        x = g[u * unit : (u + 1) * unit, :]
        for a in range(2):
            d = diagonal[pl.ds(pl.multiple_of(a * TILE + off, unit), unit), :]
            x = jnp.where(pos[5] + slot == place[a], d, x)
        rows.append(x)
    g = jnp.concatenate(rows, axis=0)
    w = lax.dot_general(g, inverse[...], NT, precision=lax.Precision.HIGHEST, preferred_element_type=F32)
    code, meta = encode(w)
    out[:n, :] = code
    out[n:, :] = meta


def final_kernel(t, front, first, second, wr, wc, out, rh, rl, ch, cl):
    i, j = pl.program_id(0), pl.program_id(1)
    per = out.shape[1] // TILE
    base = (i * pl.num_programs(1) + j) * per

    @pl.when(base == 0)
    def _():
        for src, hi, lo in ((wr, rh, rl), (wc, ch, cl)):
            n = src.shape[1] - META
            for p in range(src.shape[0]):
                at = pl.ds(p * n, n)
                hi[at, :], lo[at, :] = split(decode(src[p]))

    ri = pl.ds(pl.multiple_of(i * TILE, TILE), TILE)
    cj = pl.ds(pl.multiple_of(j * TILE * per, TILE), TILE * per)
    wh, wl = rh[ri, :], rl[ri, :]
    big = dot(wh, ch[cj, :], NT)
    out[...] = front[...] - (big + (dot(wh, cl[cj, :], NT) + dot(wl, ch[cj, :], NT)))
    for m in range(per):
        k = base + m
        at = slice(m * TILE, (m + 1) * TILE)
        for c in range(2):
            for n, src in enumerate((first, second)):

                @pl.when(t[3 * c + 2, k] == n + 1)
                def _(src=src, c=c, k=k, at=at):
                    lanes = pl.ds(pl.multiple_of(t[3 * c + 1, k] * TILE, TILE), TILE)
                    out[:, at] = out[:, at] + decode(src[t[3 * c, k], :, lanes])

        for n in range(2):

            @pl.when(t[6, k] == n + 1)
            def _(n=n, at=at):
                half = slice(n * TILE, (n + 1) * TILE)
                out[:, at] = rh[ri, half].astype(F32) + rl[ri, half].astype(F32)


MESH = pl.DeviceIdType.MESH


class Spot:
    def __init__(self):
        self.ci, self.rx = lax.axis_index("child"), lax.axis_index("rx")
        self.core, self.col = lax.axis_index("core"), lax.axis_index("col")
        self.rxn, self.cores, self.cols = lax.axis_size("rx"), lax.axis_size("core"), lax.axis_size("col")
        self.chips = lax.axis_size("child") * self.rxn
        self.chip = self.ci * self.rxn + self.rx
        self.other = {"core": 1 - self.core}

    def id(self, chip, core=None):
        core = self.core if core is None else core
        return {"child": chip // self.rxn, "rx": lax.rem(chip, self.rxn), "core": core}

    def turn(self, at, d, n):
        return lax.rem(at + (d % n), n)


def greet(ids):
    bar = pltpu.get_barrier_semaphore()
    for i in ids:
        pl.semaphore_signal(bar, inc=1, device_id=i, device_id_type=MESH)
    pl.semaphore_wait(bar, len(ids))


def push(src, dst, send, recv, to):
    cp = pltpu.make_async_remote_copy(
        src_ref=src, dst_ref=dst, send_sem=send, recv_sem=recv, device_id=to, device_id_type=MESH
    )
    cp.start()
    return cp


def remote_call(kernel, operands, out_shape, out_specs, scratch, cid, name, flops=0):
    return pl.pallas_call(
        kernel,
        out_shape=out_shape,
        in_specs=[pl.BlockSpec(memory_space=pltpu.VMEM)] * len(operands),
        out_specs=out_specs,
        scratch_shapes=scratch,
        compiler_params=pltpu.CompilerParams(collective_id=cid, has_side_effects=True),
        cost_estimate=pl.CostEstimate(flops=flops, bytes_accessed=1 << 20, transcendentals=0),
        name=name,
    )(*operands)


ANY = pl.BlockSpec(memory_space=pl.ANY)
IN_VMEM = pl.BlockSpec(memory_space=pltpu.VMEM)


def panel_kernel(x, out, loc, ss, rs, fs, fr):
    s = Spot()
    n = s.rxn
    me = s.rx * s.cores + s.core
    peers = [{"rx": s.turn(s.rx, d, n)} for d in range(1, n)]
    greet(peers + [s.other])
    keep = pltpu.make_async_copy(x, out.at[me], loc)
    keep.start()
    cps = [push(x, out.at[me], ss.at[d], rs.at[d], to) for d, to in enumerate(peers, 1)]
    fwd = [push(x, out.at[me], fs.at[0], fr.at[0], s.other)]
    for d, cp in enumerate(cps, 1):
        cp.wait_recv()
        at = s.turn(s.rx, -d, n) * s.cores + s.core
        fwd.append(push(out.at[at], out.at[at], fs.at[d], fr.at[d], s.other))
    keep.wait()
    for cp in cps:
        cp.wait_send()
    for cp in fwd:
        cp.wait()


def panel_gather(x):
    n = lax.axis_size("rx")
    shape = (n * lax.axis_size("core"),) + x.shape
    dma = pltpu.SemaphoreType.DMA
    return remote_call(
        panel_kernel, (x,), jax.ShapeDtypeStruct(shape, x.dtype), ANY,
        [dma, dma((n,)), dma((n,)), dma((n,)), dma((n,))], 0, "panels",
    )


def sum_kernel(x, out, half, mine, got, part, zgot, ss0, rs0, ss1, rs1, ss2, rs2, ss3, rs3, ss4, rs4, ss5, rs5):
    s = Spot()
    nc, nz = s.chips, s.cols
    chips = [s.turn(s.chip, d, nc) for d in range(1, nc)]
    cols = [s.turn(s.col, d, nz) for d in range(1, nz)]
    greet([s.other] + [s.id(t) for t in chips] + [{"col": t} for t in cols])
    cp = push(x.at[1 - s.core], half, ss0, rs0, s.other)
    cp.wait()
    mine[...] = x[s.core] + half[...]
    cps = [push(mine.at[t], got.at[d], ss1.at[d], rs1.at[d], s.id(t)) for d, t in enumerate(chips)]
    for cp in cps:
        cp.wait()
    total = mine[s.chip]
    for d in range(nc - 1):
        total = total + got[d]
    part[...] = total
    cps = [push(part.at[t], zgot.at[d], ss2.at[d], rs2.at[d], {"col": t}) for d, t in enumerate(cols)]
    for cp in cps:
        cp.wait()
    total = part[s.col]
    for d in range(nz - 1):
        total = total + zgot[d]
    out[s.core, s.chip, s.col] = total
    own = out.at[s.core, s.chip, s.col]
    cps = [push(own, own, ss3.at[d], rs3.at[d], {"col": t}) for d, t in enumerate(cols)]
    for cp in cps:
        cp.wait()
    own = out.at[s.core, s.chip]
    cps = [push(own, own, ss4.at[d], rs4.at[d], s.id(t)) for d, t in enumerate(chips)]
    for cp in cps:
        cp.wait()
    own = out.at[s.core]
    push(own, own, ss5, rs5, s.other).wait()


def sum_all(x):
    n = x.shape[0]
    nc, nz = lax.axis_size(("child", "rx")), lax.axis_size("col")
    tail = (n // (2 * nc * nz), n)
    full = jax.ShapeDtypeStruct((2, nc, nz) + tail, F32)
    dma = pltpu.SemaphoreType.DMA
    sems = [dma, dma, dma((nc,)), dma((nc,)), dma((nz,)), dma((nz,)), dma((nz,)), dma((nz,)), dma((nc,)), dma((nc,)), dma, dma]
    half, part = (nc, nz) + tail, (nz,) + tail
    vm = [pltpu.VMEM(z, F32) for z in (half, half, (nc - 1,) + part, part, (nz - 1,) + tail)]
    out = remote_call(sum_kernel, (x.reshape(full.shape),), full, IN_VMEM, vm + sems, 1, "total")
    return out.reshape(n, n)


def scatter_kernel(x, out, half, mine, ss, rs, cs, cr):
    s = Spot()
    nc = s.chips
    n = x.shape[2] - META
    order = [s.turn(s.chip, d, nc) for d in range(1, nc + 1)]
    greet([s.other] + [s.id(t) for t in order[:-1]])
    pairs = [push(x.at[1 - s.core, t], half.at[t], ss.at[d], rs.at[t], s.other) for d, t in enumerate(order)]
    cps = []
    for d, t in enumerate(order):
        pltpu.make_async_remote_copy(
            src_ref=half.at[t], dst_ref=half.at[t], send_sem=ss.at[d], recv_sem=rs.at[t],
            device_id=s.other, device_id_type=MESH,
        ).wait_recv()
        q, meta = encode(decode(x[s.core, t]) + decode(half[t]))
        if d < nc - 1:
            mine[d, :n, :] = q
            mine[d, n:, :] = meta
            cps.append(push(mine.at[d], out.at[d + 1], cs.at[d], cr.at[d], s.id(t)))
        else:
            out[0, :n, :] = q
            out[0, n:, :] = meta
    for cp in pairs:
        cp.wait_send()
    for cp in cps:
        cp.wait()


def scatter(x):
    nc = x.shape[1]
    dma = pltpu.SemaphoreType.DMA
    shape = x.shape[1:]
    return remote_call(
        scatter_kernel, (x,), jax.ShapeDtypeStruct(shape, x.dtype), IN_VMEM,
        [pltpu.VMEM(shape, x.dtype)] * 2 + [dma((nc,))] * 4, 2, "strips"
    )


def spread_kernel(x, wc, wr, zbuf, loc, zs, zr, ps, pr, fs, fr, ws, wx, wl):
    s = Spot()
    nc, nz, half = s.chips, s.cols, wr.shape[0]
    me = s.chip * s.cores + s.core
    slot = lax.rem(me, half)
    n = nc * s.cores
    chips = [s.turn(s.chip, d, nc) for d in range(1, nc)]
    plane = [s.turn(me, d, n) for d in range(1, n)]
    greet([s.id(t // s.cores, lax.rem(t, s.cores)) for t in plane] + [{"col": s.turn(s.col, d, nz)} for d in range(1, nz)])
    keep = pltpu.make_async_copy(x, wc.at[me], loc)
    keep.start()
    pc = [push(x, wc.at[me], ps.at[d], pr.at[d], s.id(t)) for d, t in enumerate(chips, 1)]
    fc = [push(x, wc.at[me], fs.at[0], fr.at[0], s.other)]

    def hand(src, z, d):
        here = jnp.logical_and(z == s.chip, s.ci == s.core)

        @pl.when(here)
        def _():
            pltpu.make_async_copy(src, wr.at[slot], wl).start()

        @pl.when(jnp.logical_not(here))
        def _():
            push(src, wr.at[slot], ws.at[d], wx.at[slot], s.id(z, s.ci))

    def handed(src, z, d):
        here = jnp.logical_and(z == s.chip, s.ci == s.core)

        @pl.when(here)
        def _():
            pltpu.make_async_copy(src, wr.at[slot], wl).wait()

        @pl.when(jnp.logical_not(here))
        def _():
            pltpu.make_async_remote_copy(
                src_ref=src, dst_ref=wr.at[slot], send_sem=ws.at[d], recv_sem=wx.at[slot],
                device_id=s.id(z, s.ci), device_id_type=MESH,
            ).wait_send()

    def hop(src, z, way, d):
        to = s.col + way

        @pl.when(jnp.logical_and(to >= 0, to < nz))
        def _():
            push(src, zbuf.at[z], zs.at[d], zr.at[z], {"col": to})

    def hopped(src, z, way, d):
        to = s.col + way

        @pl.when(jnp.logical_and(to >= 0, to < nz))
        def _():
            pltpu.make_async_remote_copy(
                src_ref=src, dst_ref=zbuf.at[z], send_sem=zs.at[d], recv_sem=zr.at[z],
                device_id={"col": to}, device_id_type=MESH,
            ).wait_send()

    hop(x, s.col, 1, 0)
    hop(x, s.col, -1, 1)
    hand(x, s.col, 0)

    def moved(d, way):
        z = s.col - way * d
        n = 2 * d + (way < 0)

        @pl.when(jnp.logical_and(z >= 0, z < nz))
        def _():
            src = zbuf.at[z]
            pltpu.make_async_remote_copy(
                src_ref=src, dst_ref=src, send_sem=zs.at[n], recv_sem=zr.at[z],
                device_id=s.other, device_id_type=MESH,
            ).wait_recv()
            hop(src, z, way, n)
            hand(src, z, n)

    def done(d, way):
        z = s.col - way * d
        n = 2 * d + (way < 0)

        @pl.when(jnp.logical_and(z >= 0, z < nz))
        def _():
            hopped(zbuf.at[z], z, way, n)
            handed(zbuf.at[z], z, n)

    for d in range(1, max(nz, nc)):
        if d < nz:
            moved(d, 1)
            moved(d, -1)
        if d < nc:
            pc[d - 1].wait_recv()
            at = s.turn(s.chip, -d, nc) * s.cores + s.core
            fc.append(push(wc.at[at], wc.at[at], fs.at[d], fr.at[d], s.other))
    hopped(x, s.col, 1, 0)
    hopped(x, s.col, -1, 1)
    handed(x, s.col, 0)
    for d in range(1, nz):
        done(d, 1)
        done(d, -1)
    for j in range(half):

        @pl.when(jnp.logical_or(s.ci != s.core, slot != j))
        def _(j=j):
            pltpu.make_async_remote_copy(
                src_ref=wr.at[j], dst_ref=wr.at[j], send_sem=ws.at[0], recv_sem=wx.at[j],
                device_id=s.other, device_id_type=MESH,
            ).wait_recv()

    keep.wait()
    for cp in pc:
        cp.wait_send()
    for cp in fc:
        cp.wait()


def spread(x):
    nc, nz = lax.axis_size(("child", "rx")), lax.axis_size("col")
    dma = pltpu.SemaphoreType.DMA
    sems = [dma, dma((2 * nz,)), dma((nz,))] + [dma((nc,))] * 4 + [dma((2 * nz,)), dma((nc,)), dma]
    shapes = [jax.ShapeDtypeStruct((n,) + x.shape, x.dtype) for n in (2 * nc, nc)]
    return remote_call(
        spread_kernel, (x,), shapes, [ANY, ANY], [pltpu.VMEM((nz,) + x.shape, x.dtype)] + sems, 3, "spread"
    )


BASE = 128
FACTOR_WORK = 40_000_000_000
WIDE = 8


def base_inverse(a_ref, d_ref, x_ref):
    n, step = a_ref.shape[0], 8
    ids = lax.broadcasted_iota(jnp.int32, (step, n), 0)
    lanes = lax.broadcasted_iota(jnp.int32, (step, n), 1)
    a = [a_ref[i * step : (i + 1) * step, :] for i in range(n // step)]
    x = [(lanes == ids + i * step).astype(F32) for i in range(n // step)]
    for j in range(0, n, WIDE):
        c0 = j // step
        chunks = range(c0, n // step)
        cols = [[jnp.broadcast_to(a[i][:, j + t : j + t + 1], (step, n)) for i in chunks] for t in range(WIDE)]
        at = [j + t - c0 * step for t in range(WIDE)]
        rows = [a[c0][p : p + 1, :] for p in at]
        xrows = [x[c0][p : p + 1, :] for p in at]
        for t in range(WIDE):
            pivot = cols[t][0][at[t] : at[t] + 1, :]
            d_ref[j + t : j + t + 1, :] = pivot
            inv = 1.0 / pivot
            low = [c * inv for c in cols[t]]
            low[0] = jnp.where(ids > at[t], low[0], 0.0)
            for s in range(t + 1, WIDE):
                f = cols[t][0][at[s] : at[s] + 1, :]
                g = f * inv
                cols[s] = [c - l * f for c, l in zip(cols[s], low)]
                rows[s] = rows[s] - g * rows[t]
                xrows[s] = xrows[s] - g * xrows[t]
            for n_, i in enumerate(chunks):
                a[i] = a[i] - low[n_] * rows[t]
                x[i] = x[i] - low[n_] * xrows[t]
    for i in range(n // step):
        x_ref[i * step : (i + 1) * step, :] = x[i] * (1.0 / jnp.sqrt(d_ref[i * step : (i + 1) * step, :]))


def factor_kernel(a_in, y, a, blk, piv, inv):
    n = a.shape[0]
    high = functools.partial(lax.dot_general, precision=lax.Precision.HIGHEST, preferred_element_type=F32)
    ids = lax.broadcasted_iota(jnp.int32, (n, n), 0)
    a[...] = a_in[...]
    y[...] = (ids == lax.broadcasted_iota(jnp.int32, (n, n), 1)).astype(F32)

    def one(k, carry):
        at = pl.ds(pl.multiple_of(k * BASE, BASE), BASE)
        blk[...] = a[at, at]
        base_inverse(blk, piv, inv)
        low = high(a[:, at], inv[...], NT)
        low = jnp.where(ids[:, :BASE] >= (k + 1) * BASE, low, 0.0)
        yk = high(inv[...], y[at, :], (((1,), (0,)), ((), ())))
        a[...] = a[...] - high(low, low, NT)
        y[...] = y[...] - high(low, yk, (((1,), (0,)), ((), ())))
        y[at, :] = yk
        return carry

    lax.fori_loop(0, n // BASE, one, 0)


def factor_inverse(d):
    n = d.shape[0]
    return pl.pallas_call(
        factor_kernel,
        out_shape=jax.ShapeDtypeStruct(d.shape, F32),
        scratch_shapes=[pltpu.VMEM((n, n), F32)] + [pltpu.VMEM((BASE, BASE), F32)] * 3,
        name="factor",
        cost_estimate=pl.CostEstimate(flops=FACTOR_WORK, bytes_accessed=8 * n * n, transcendentals=0),
    )(d)


def body(child_blocks, child_panels, child_patterns, child_maps, parent_place, parent_front):
    ci = lax.axis_index("child")
    rx = lax.axis_index("rx")
    core = lax.axis_index("core")
    col = lax.axis_index("col")
    cores = lax.axis_size("core")
    rxn = lax.axis_size("rx")
    row = rx * cores + core
    rown = rxn * cores
    chips = lax.axis_size("child") * rxn
    chip = ci * rxn + rx
    group = ci * rown + row
    block = child_blocks[0]
    own = child_panels[0]
    depth = own.shape[1]
    width = block.shape[0]
    td = width // TILE
    blocks = child_maps.shape[1] // td
    rd = parent_front.shape[0] // TILE
    cd = parent_front.shape[1] // TILE
    slots_n = parent_place.shape[0]
    i32 = jnp.int32

    share = cd * TILE // (chips * cores)
    wide = blocks // cores
    me = chip * cores + core
    pos = jnp.stack([ci, row, col, core, me, col * cd]).astype(i32)

    def tile_at(block, group, pos, maps, place):
        return find(maps, place, pos[0], block, group, td, cd)[0]

    outgoing, part = tile_call(
        functools.partial(pick_kernel, td, cd), (blocks,), (pos, child_maps, parent_place), (block, own),
        [
            pl.BlockSpec((width, TILE), lambda z, pos, maps, place: (0, tile_at(pos[2], z, pos, maps, place))),
            pl.BlockSpec((TILE, depth), lambda z, pos, maps, place: (tile_at(pos[1], pos[2], pos, maps, place), 0)),
        ],
        [
            jax.ShapeDtypeStruct((blocks, td, CODED, TILE), jnp.int16),
            jax.ShapeDtypeStruct((TILE, depth), own.dtype),
        ],
        [
            pl.BlockSpec((1, td, CODED, TILE), lambda z, *_: (z, 0, 0, 0)),
            pl.BlockSpec((TILE, depth), lambda z, *_: (0, 0)),
        ], "pick",
    )
    raw = lax.all_to_all(outgoing, "col", split_axis=0, concat_axis=0, tiled=True)

    smem = pl.BlockSpec(memory_space=pltpu.SMEM)
    dims = (td, cd, rd, chips, blocks, cores, rown)
    sizes = [(chips + 2,), (chips, blocks), (8, 4), (7, cd), (7, rd * cd)]
    rowt, fac, diagt, stript, fint = pl.pallas_call(
        functools.partial(plan_kernel, dims),
        in_specs=[smem] * 4, out_specs=[smem] * 5, name="plan",
        out_shape=[jax.ShapeDtypeStruct(z, i32) for z in sizes],
        scratch_shapes=[pltpu.SMEM((2, slots_n), i32)],
    )(pos, child_maps, parent_place, child_patterns)

    partner = panel_gather(part)
    diag_part = tile_call(
        diag_kernel, (2, 2), (diagt,), (block, parent_front, own, partner),
        [
            pl.BlockSpec((TILE, TILE), lambda a, b, t: (t[0, a * 2 + b], t[1, a * 2 + b])),
            pl.BlockSpec((TILE, TILE), lambda a, b, t: (t[2, a * 2 + b], t[3, a * 2 + b])),
            pl.BlockSpec((TILE, depth), lambda a, b, t: (t[0, a * 2 + b], 0)),
            pl.BlockSpec((1, TILE, depth), lambda a, b, t: (t[7, a * 2 + b], 0, 0)),
        ],
        jax.ShapeDtypeStruct((2 * TILE, 2 * TILE), F32),
        pl.BlockSpec((TILE, TILE), lambda a, b, t: (a, b)), "diag",
    )
    plane = ("child", "rx", "core")
    diagonal = sum_all(diag_part)
    diagonal, raw = lax.optimization_barrier((diagonal, raw))

    strip_rows, coded = tile_call(
        update_kernel, (chips,), (rowt, fac), (raw, own, partner),
        [
            pl.BlockSpec((blocks, 1, CODED, TILE), lambda p, r, f: (0, r[p], 0, 0)),
            pl.BlockSpec((TILE, depth), lambda p, r, f: (r[p], 0)),
            pl.BlockSpec((blocks, TILE, depth), lambda p, r, f: (0, 0, 0)),
        ],
        [
            jax.ShapeDtypeStruct((2, TILE, blocks * TILE), F32),
            jax.ShapeDtypeStruct((chips, cores, CODED, wide * TILE), jnp.int16),
        ],
        [
            pl.BlockSpec((2, TILE, blocks * TILE), lambda p, r, f: (0, 0, 0)),
            pl.BlockSpec((1, cores, CODED, wide * TILE), lambda p, r, f: (p, 0, 0, 0)),
        ], "update",
    )
    coded = coded.reshape((chips * cores,) + coded.shape[2:])
    first = lax.all_to_all(coded, plane, split_axis=0, concat_axis=0, tiled=True)
    diagonal, coded = lax.optimization_barrier((diagonal, coded))
    inverse = factor_inverse(diagonal)
    first, inverse = lax.optimization_barrier((first, inverse))
    second = lax.ppermute(first, "core", [(k, (k + 1) % 2) for k in range(2)])

    pieces = (cores, chips, share + META, 2 * TILE)
    strip_part = tile_call(
        strip_kernel, (1,), (stript,), (strip_rows, parent_front, parent_front),
        [
            pl.BlockSpec(strip_rows.shape, lambda k, t: (0, 0, 0)),
            pl.BlockSpec((TILE, cd * TILE), lambda k, t: (t[0, 0], 0)),
            pl.BlockSpec((TILE, cd * TILE), lambda k, t: (t[0, 1], 0)),
        ],
        jax.ShapeDtypeStruct(pieces, jnp.int16),
        pl.BlockSpec(pieces, lambda k, t: (0, 0, 0, 0)), "strip",
        scratch=[pltpu.VMEM((cd * TILE, 2 * TILE), F32)],
    )
    vm = IN_VMEM
    piece = pl.pallas_call(
        solve_kernel, out_shape=jax.ShapeDtypeStruct(pieces[2:], jnp.int16), name="solve",
        in_specs=[smem, smem, vm, vm, vm], out_specs=vm,
    )(pos, parent_place, scatter(strip_part), diagonal, inverse)
    wc, wr = spread(piece)

    per = 2
    return tile_call(
        final_kernel, (rd, cd // per), (fint,), (parent_front, first, second, wr, wc),
        [
            pl.BlockSpec((TILE, per * TILE), lambda i, j, t: (i, j)),
            pl.BlockSpec(first.shape, lambda i, j, t: (0, 0, 0)),
            pl.BlockSpec(second.shape, lambda i, j, t: (0, 0, 0)),
            pl.BlockSpec(wr.shape, lambda i, j, t: (0, 0, 0)),
            pl.BlockSpec(wc.shape, lambda i, j, t: (0, 0, 0)),
        ],
        jax.ShapeDtypeStruct(parent_front.shape, F32),
        pl.BlockSpec((TILE, per * TILE), lambda i, j, t: (i, j)), "final",
        scratch=[pltpu.VMEM((n * TILE, 2 * TILE), BF16) for n in (rd, rd, cd, cd)],
    )


def solution(mesh):
    child, row, col = mesh.devices.shape
    cores = child * row // col
    fine = Mesh(mesh.devices.reshape(child, row // cores, cores, col), ("child", "rx", "core", "col"))
    return jax.shard_map(
        body,
        mesh=fine,
        in_specs=(
            P("child", ("rx", "core"), "col"),
            P("child", ("rx", "core"), None),
            P(),
            P(),
            P(),
            P(("child", "rx", "core"), "col"),
        ),
        out_specs=P(("child", "rx", "core"), "col"),
        check_vma=False,
    )
```

```python
import functools
import math

import jax
import jax.numpy as jnp
from jax import lax
from jax.experimental import pallas as pl
from jax.experimental.pallas import tpu as pltpu
from jax.sharding import Mesh, PartitionSpec as P

TILE = 256
F32 = jnp.float32
BF16 = jnp.bfloat16
META = 16
CODED = TILE + META
FULL = 32767.0
NT = (((1,), (1,)), ((), ()))


def dot(a, b, dims):
    return lax.dot_general(a, b, dims, preferred_element_type=F32)


def split(x):
    hi = x.astype(BF16)
    return hi, (x - hi.astype(F32)).astype(BF16)


def tile_call(kernel, grid, tables, operands, in_specs, out_shape, out_spec, cost=None, scratch=()):
    return pl.pallas_call(
        kernel,
        grid_spec=pltpu.PrefetchScalarGridSpec(
            num_scalar_prefetch=len(tables), grid=grid, in_specs=in_specs, out_specs=out_spec,
            scratch_shapes=list(scratch),
        ),
        out_shape=out_shape,
        cost_estimate=cost,
    )(*tables, *operands)


def powers(k):
    h = jnp.floor(k * 0.5)
    return jnp.exp2(h), jnp.exp2(k - h)


def encode(x):
    top = jnp.maximum(jnp.max(jnp.abs(x), axis=0, keepdims=True), 1e-37)
    k = jnp.ceil(jnp.log2(top) + 1e-3)
    p, r = powers(-k)
    part = jnp.clip(jnp.ceil(top * p * r * FULL), 1.0, FULL)
    q = jnp.clip(x * p * (r * (FULL * FULL / part)), -FULL, FULL)
    q = jnp.floor(q + 0.5).astype(jnp.int32)
    ids = lax.broadcasted_iota(jnp.int32, (META, x.shape[1]), 0)
    meta = jnp.where(ids == 0, k.astype(jnp.int32), jnp.where(ids == 1, part.astype(jnp.int32), 0))
    return q.astype(jnp.int16), meta.astype(jnp.int16)


def decode(code):
    n = code.shape[0] - META
    meta = code[n:, :].astype(jnp.int32).astype(F32)
    p, r = powers(meta[0:1, :])
    q = code[:n, :].astype(jnp.int32).astype(F32)
    return q * (meta[1:2, :] * (1.0 / (FULL * FULL)) * p) * r


def find(maps, place, child, block, group, td, width):
    at = jnp.int32(0)
    ok = jnp.int32(0)
    for t in range(td):
        hit = place[maps[child, block * td + t]] // width == group
        at = jnp.where(hit, t, at)
        ok = jnp.where(hit, 1, ok)
    return at, ok


def pick_kernel(td, cd, pos, maps, place, src, panel, *outs):
    part, tmp = outs[-2:]
    z = pl.program_id(0)
    for r in range(td):
        q, meta = encode(src[r * TILE : (r + 1) * TILE, :])
        tmp[r, :TILE, :] = q
        tmp[r, TILE:, :] = meta
    for d, out in enumerate(outs[:-2]):

        @pl.when(z == d)
        def _(out=out):
            out[...] = tmp[...]

    @pl.when(z == 0)
    def _():
        ok = find(maps, place, pos[0], pos[1], pos[2], td, cd)[1]
        part[...] = jnp.where(ok != 0, panel[...], jnp.zeros_like(panel))


def plan_kernel(dims, pos, maps, place, pat, rowt, fac, diagt, stript, fint, inv):
    td, cd, rd, chips, blocks, cores, rown = dims
    ci, row, col, core = pos[0], pos[1], pos[2], pos[3]
    group = ci * rown + row
    chip = pos[6]
    rxn = chips // 2
    slots_n, tiles_n = place.shape[0], maps.shape[1]

    @pl.loop(0, slots_n)
    def _(k):
        inv[0, k] = -1
        inv[1, k] = -1

    @pl.loop(0, tiles_n)
    def _(k):
        inv[0, place[maps[0, k]]] = k
        inv[1, place[maps[1, k]]] = k

    from_col = [lax.rem(col + blocks - d, blocks) for d in range(blocks)]
    cols = [find(maps, place, ci, b, col, td, cd) for b in from_col]
    for d in range(chips):
        at, ok = find(maps, place, ci, row, lax.rem(chip + d, chips), td, cd)
        rowt[d] = at
        for n, (b, (tile, good)) in enumerate(zip(from_col, cols)):
            fac[d, n] = pat[ci, row * td + at, b * td + tile] * ok * good
    e = (place[0], place[1])
    ie = (inv[ci, e[0]], inv[ci, e[1]])
    le = [jnp.maximum(i, 0) for i in ie]
    own = [((ie[a] >= 0) & (le[a] // td == row)).astype(jnp.int32) for a in range(2)]
    for a in range(2):
        rowt[chips + a] = jnp.where(own[a] != 0, lax.rem(e[a] // cd + chips - chip, chips), -1)
        for b in range(a + 1):
            k = a + b
            live = own[a] * (ie[b] >= 0).astype(jnp.int32) * pat[ci, le[a], le[b]]
            diagt[0, k] = le[a] % td
            diagt[1, k] = le[b] % td
            diagt[2, k] = e[a] % rd
            diagt[3, k] = e[b] % cd
            diagt[4, k] = live * (le[b] // td == col).astype(jnp.int32)
            diagt[5, k] = ((e[a] // rd == group) & (e[b] // cd == col)).astype(jnp.int32)
            diagt[6, k] = live * (e[b] // cd == col).astype(jnp.int32)
            diagt[7, k] = le[b] // td
        stript[0, a] = e[a] % rd

        for q in range(cd):
            slot = col * cd + q
            iq = inv[ci, slot]
            free = ((slot != e[0]) & (slot != e[1])).astype(jnp.int32)
            stript[1 + a, q] = jnp.maximum(iq, 0) // td
            stript[3 + a, q] = own[a] * free * (iq >= 0).astype(jnp.int32)
            stript[5 + a, q] = free * (e[a] // rd == group).astype(jnp.int32)
    for k in range(2, cd):
        stript[0, k] = 0

    @pl.loop(0, rd * cd)
    def _(k):
        slot = col * cd + k % cd
        for c in range(2):
            r, t = inv[c, group * rd + k // cd], inv[c, slot]
            ok = ((r >= 0) & (t >= 0)).astype(jnp.int32)
            source = jnp.maximum(r, 0) // td
            far = (source % cores != core).astype(jnp.int32)
            fint[3 * c, k] = far * chips + lax.rem(chip + chips - (c * rxn + source // cores), chips)
            fint[3 * c + 1, k] = jnp.maximum(t, 0) // td
            fint[3 * c + 2, k] = ok
        fint[6, k] = jnp.where(slot == e[0], 1, jnp.where(slot == e[1], 2, 0))


def diag_kernel(t, blk, front, ea, eb, out):
    k = pl.program_id(0)
    x = jnp.where(t[4, k] != 0, blk[...], 0.0) + jnp.where(t[5, k] != 0, front[...], 0.0)
    out[...] = x - jnp.where(t[6, k] != 0, dot(ea[...], eb[0], NT), 0.0)


def update_kernel(rowt, fac, pos, *refs):
    blocks = fac.shape[1]
    raws, (panel, partner, strip), outs, tmp = refs[:blocks], refs[blocks : blocks + 3], refs[blocks + 3 : -1], refs[-1]
    p = pl.program_id(0)
    chips = pl.num_programs(0)

    @pl.when(p == 0)
    def _():
        strip[...] = jnp.zeros_like(strip)

    for d, raw in enumerate(raws):
        b = lax.rem(pos[2] + blocks - d, blocks)
        at = pl.ds(pl.multiple_of(b * TILE, TILE), TILE)
        u = decode(raw[0]) - dot(panel[...], partner[b], NT)
        u = jnp.where(fac[p, d] != 0, u, 0.0)
        q, meta = encode(u)
        tmp[:TILE, at] = q
        tmp[TILE:, at] = meta
        for a in range(2):

            @pl.when(rowt[chips + a] == p)
            def _(a=a, u=u, at=at):
                strip[a, :, at] = u

    for d, out in enumerate(outs):

        @pl.when(p == d)
        def _(out=out):
            out[...] = tmp[...]


def strip_kernel(t, pos, upd, f0, f1, *outs):
    g, outs = outs[-1], outs[:-1]
    cd = t.shape[1]
    some = sum(t[n, q] for n in range(3, 7) for q in range(cd))

    @pl.when(some == 0)
    def _():
        for out in outs:
            out[...] = jnp.zeros_like(out)

    @pl.when(some != 0)
    def _():
        g[...] = jnp.zeros_like(g)
        for q in range(cd):
            for a, f in enumerate((f0, f1)):

                @pl.when(t[3 + a, q] + t[5 + a, q] != 0)
                def _(q=q, a=a, f=f):
                    at = pl.ds(pl.multiple_of(t[1 + a, q] * TILE, TILE), TILE)
                    x = jnp.where(t[3 + a, q] != 0, upd[a, :, at], 0.0)
                    x = x + jnp.where(t[5 + a, q] != 0, f[:, q * TILE : (q + 1) * TILE], 0.0)
                    g[q * TILE : (q + 1) * TILE, a * TILE : (a + 1) * TILE] = x.T

        n = outs[0].shape[0] - META
        for d, out in enumerate(outs):
            m = lax.rem(pos[4] + d, len(outs))
            code, meta = encode(g[pl.ds(pl.multiple_of(m * n, 16), n), :])
            out[:n, :] = code
            out[n:, :] = meta


def solve_kernel(pos, place, diagonal, inverse, *refs):
    out = refs[-1]
    n = out.shape[0] - META
    g = decode(refs[0][...])
    for part in refs[1:-1]:
        g = g + decode(part[...])
    unit = math.gcd(n, TILE)
    rows = []
    for u in range(n // unit):
        first = pos[4] * n + u * unit
        slot, off = first // TILE, first % TILE
        x = g[u * unit : (u + 1) * unit, :]
        for a in range(2):
            d = diagonal[pl.ds(pl.multiple_of(a * TILE + off, unit), unit), :]
            x = jnp.where(pos[5] + slot == place[a], d, x)
        rows.append(x)
    g = jnp.concatenate(rows, axis=0)
    w = lax.dot_general(g, inverse[...], NT, precision=lax.Precision.HIGHEST, preferred_element_type=F32)
    code, meta = encode(w)
    out[:n, :] = code
    out[n:, :] = meta


def final_kernel(t, front, wr, wc, *refs):
    out, rh, rl, ch, cl, buf, sem = refs[-7:]
    codes = refs[:-7]
    i, j = pl.program_id(0), pl.program_id(1)
    per = out.shape[1] // TILE
    base = (i * pl.num_programs(1) + j) * per

    @pl.when(base == 0)
    def _():
        cps = [pltpu.make_async_copy(x, buf.at[n], sem.at[n]) for n, x in enumerate(codes)]
        for cp in cps:
            cp.start()
        for src, hi, lo in ((wr, rh, rl), (wc, ch, cl)):
            n = src.shape[1] - META
            for p in range(src.shape[0]):
                at = pl.ds(p * n, n)
                hi[at, :], lo[at, :] = split(decode(src[p]))
        for cp in cps:
            cp.wait()

    ri = pl.ds(pl.multiple_of(i * TILE, TILE), TILE)
    cj = pl.ds(pl.multiple_of(j * TILE * per, TILE), TILE * per)
    wh, wl = rh[ri, :], rl[ri, :]
    big = dot(wh, ch[cj, :], NT)
    out[...] = front[...] - (big + (dot(wh, cl[cj, :], NT) + dot(wl, ch[cj, :], NT)))
    for m in range(per):
        k = base + m
        at = slice(m * TILE, (m + 1) * TILE)
        for c in range(2):

            @pl.when(t[3 * c + 2, k] != 0)
            def _(c=c, k=k, at=at):
                lanes = pl.ds(pl.multiple_of(t[3 * c + 1, k] * TILE, TILE), TILE)
                out[:, at] = out[:, at] + decode(buf[t[3 * c, k], :, lanes])

        for n in range(2):

            @pl.when(t[6, k] == n + 1)
            def _(n=n, at=at):
                half = slice(n * TILE, (n + 1) * TILE)
                out[:, at] = rh[ri, half].astype(F32) + rl[ri, half].astype(F32)


MESH = pl.DeviceIdType.MESH


class Spot:
    def __init__(self):
        self.ci, self.rx = lax.axis_index("child"), lax.axis_index("rx")
        self.core, self.col = lax.axis_index("core"), lax.axis_index("col")
        self.rxn, self.cores, self.cols = lax.axis_size("rx"), lax.axis_size("core"), lax.axis_size("col")
        self.chips = lax.axis_size("child") * self.rxn
        self.chip = self.ci * self.rxn + self.rx
        self.other = {"core": 1 - self.core}

    def id(self, chip, core=None):
        core = self.core if core is None else core
        return {"child": chip // self.rxn, "rx": lax.rem(chip, self.rxn), "core": core}

    def turn(self, at, d, n):
        return lax.rem(at + (d % n), n)


def greet(ids):
    bar = pltpu.get_barrier_semaphore()
    for i in ids:
        pl.semaphore_signal(bar, inc=1, device_id=i, device_id_type=MESH)
    pl.semaphore_wait(bar, len(ids))


def push(src, dst, send, recv, to):
    cp = pltpu.make_async_remote_copy(
        src_ref=src, dst_ref=dst, send_sem=send, recv_sem=recv, device_id=to, device_id_type=MESH
    )
    cp.start()
    return cp


def remote_call(kernel, operands, out_shape, out_specs, scratch, cid, flops=0):
    return pl.pallas_call(
        kernel,
        out_shape=out_shape,
        in_specs=[pl.BlockSpec(memory_space=pltpu.VMEM)] * len(operands),
        out_specs=out_specs,
        scratch_shapes=scratch,
        compiler_params=pltpu.CompilerParams(collective_id=cid, has_side_effects=True),
        cost_estimate=pl.CostEstimate(flops=flops, bytes_accessed=1 << 20, transcendentals=0),
    )(*operands)


ANY = pl.BlockSpec(memory_space=pl.ANY)
IN_VMEM = pl.BlockSpec(memory_space=pltpu.VMEM)


def panel_kernel(x, out, loc, ss, rs, fs, fr):
    s = Spot()
    n = s.rxn
    me = s.rx * s.cores + s.core
    peers = [{"rx": s.turn(s.rx, d, n)} for d in range(1, n)]
    greet(peers + [s.other])
    keep = pltpu.make_async_copy(x, out.at[me], loc)
    keep.start()
    cps = [push(x, out.at[me], ss.at[d], rs.at[d], to) for d, to in enumerate(peers, 1)]
    fwd = [push(x, out.at[me], fs.at[0], fr.at[0], s.other)]
    for d, cp in enumerate(cps, 1):
        cp.wait_recv()
        at = s.turn(s.rx, -d, n) * s.cores + s.core
        fwd.append(push(out.at[at], out.at[at], fs.at[d], fr.at[d], s.other))
    keep.wait()
    for cp in cps:
        cp.wait_send()
    for cp in fwd:
        cp.wait()


def panel_gather(x):
    n = lax.axis_size("rx")
    shape = (n * lax.axis_size("core"),) + x.shape
    dma = pltpu.SemaphoreType.DMA
    return remote_call(
        panel_kernel, (x,), jax.ShapeDtypeStruct(shape, x.dtype), ANY,
        [dma, dma((n,)), dma((n,)), dma((n,)), dma((n,))], 0,
    )


def sum_kernel(x, out, half, mine, got, part, zgot, ss0, rs0, ss1, rs1, ss2, rs2, ss3, rs3, ss4, rs4, ss5, rs5):
    s = Spot()
    nc, nz = s.chips, s.cols
    chips = [s.turn(s.chip, d, nc) for d in range(1, nc)]
    cols = [s.turn(s.col, d, nz) for d in range(1, nz)]
    greet([s.other] + [s.id(t) for t in chips] + [{"col": t} for t in cols])
    cp = push(x.at[1 - s.core], half, ss0, rs0, s.other)
    cp.wait()
    mine[...] = x[s.core] + half[...]
    cps = [push(mine.at[t], got.at[d], ss1.at[d], rs1.at[d], s.id(t)) for d, t in enumerate(chips)]
    for cp in cps:
        cp.wait()
    total = mine[s.chip]
    for d in range(nc - 1):
        total = total + got[d]
    part[...] = total
    cps = [push(part.at[t], zgot.at[d], ss2.at[d], rs2.at[d], {"col": t}) for d, t in enumerate(cols)]
    for cp in cps:
        cp.wait()
    total = part[s.col]
    for d in range(nz - 1):
        total = total + zgot[d]
    out[s.core, s.chip, s.col] = total

    def send_z(d, t):
        own = out.at[s.core, s.chip, s.col]
        return push(own, own, ss3.at[d], rs3.at[d], {"col": t})

    def send_xy(z, n):
        own = out.at[s.core, s.chip, z]
        return [push(own, own, ss4.at[n, d], rs4.at[n, d], s.id(t)) for d, t in enumerate(chips)]

    def send_core(c, z, n, m):
        own = out.at[s.core, c, z]
        return push(own, own, ss5.at[n, m], rs5.at[n, m], s.other)

    zc = [send_z(d, t) for d, t in enumerate(cols)]
    xy = [send_xy(s.col, 0)]
    cc = [send_core(s.chip, s.col, 0, 0)]
    for n in range(nz):
        z = s.turn(s.col, -n, nz)
        if n:
            zc[n - 1].wait_recv()
            xy.append(send_xy(z, n))
            cc.append(send_core(s.chip, z, n, 0))
    for n in range(nz):
        for d in range(nc - 1):
            xy[n][d].wait_recv()
            cc.append(send_core(s.turn(s.chip, -(d + 1), nc), s.turn(s.col, -n, nz), n, d + 1))
    for cp in zc + [x for row in xy for x in row]:
        cp.wait_send()
    for cp in cc:
        cp.wait()


def sum_all(x):
    nc, nz = lax.axis_size(("child", "rx")), lax.axis_size("col")
    tail = (x.shape[0] // (2 * nc * nz), x.shape[1])
    full = jax.ShapeDtypeStruct((2, nc, nz) + tail, F32)
    dma = pltpu.SemaphoreType.DMA
    sems = [dma, dma, dma((nc,)), dma((nc,)), dma((nz,)), dma((nz,)), dma((nz,)), dma((nz,)), dma((nz, nc)), dma((nz, nc)), dma((nz, nc)), dma((nz, nc))]
    half, part = (nc, nz) + tail, (nz,) + tail
    vm = [pltpu.VMEM(z, F32) for z in (half, half, (nc - 1,) + part, part, (nz - 1,) + tail)]
    out = remote_call(sum_kernel, (x.reshape(full.shape),), full, IN_VMEM, vm + sems, 1)
    return out.reshape(x.shape)


def spread_kernel(x, wc, wr, zbuf, loc, zs, zr, ps, pr, fs, fr, ws, wx, wl):
    s = Spot()
    nc, nz, half = s.chips, s.cols, wr.shape[0]
    me = s.chip * s.cores + s.core
    slot = lax.rem(me, half)
    n = nc * s.cores
    chips = [s.turn(s.chip, d, nc) for d in range(1, nc)]
    plane = [s.turn(me, d, n) for d in range(1, n)]
    greet([s.id(t // s.cores, lax.rem(t, s.cores)) for t in plane] + [{"col": s.turn(s.col, d, nz)} for d in range(1, nz)])
    keep = pltpu.make_async_copy(x, wc.at[me], loc)
    keep.start()
    pc = [push(x, wc.at[me], ps.at[d], pr.at[d], s.id(t)) for d, t in enumerate(chips, 1)]
    fc = [push(x, wc.at[me], fs.at[0], fr.at[0], s.other)]

    def hand(src, z, d):
        here = jnp.logical_and(z == s.chip, s.ci == s.core)

        @pl.when(here)
        def _():
            pltpu.make_async_copy(src, wr.at[slot], wl).start()

        @pl.when(jnp.logical_not(here))
        def _():
            push(src, wr.at[slot], ws.at[d], wx.at[slot], s.id(z, s.ci))

    def handed(src, z, d):
        here = jnp.logical_and(z == s.chip, s.ci == s.core)

        @pl.when(here)
        def _():
            pltpu.make_async_copy(src, wr.at[slot], wl).wait()

        @pl.when(jnp.logical_not(here))
        def _():
            pltpu.make_async_remote_copy(
                src_ref=src, dst_ref=wr.at[slot], send_sem=ws.at[d], recv_sem=wx.at[slot],
                device_id=s.id(z, s.ci), device_id_type=MESH,
            ).wait_send()

    def hop(src, z, way, d):
        to = s.col + way

        @pl.when(jnp.logical_and(to >= 0, to < nz))
        def _():
            push(src, zbuf.at[z], zs.at[d], zr.at[z], {"col": to})

    def hopped(src, z, way, d):
        to = s.col + way

        @pl.when(jnp.logical_and(to >= 0, to < nz))
        def _():
            pltpu.make_async_remote_copy(
                src_ref=src, dst_ref=zbuf.at[z], send_sem=zs.at[d], recv_sem=zr.at[z],
                device_id={"col": to}, device_id_type=MESH,
            ).wait_send()

    hop(x, s.col, 1, 0)
    hop(x, s.col, -1, 1)
    hand(x, s.col, 0)

    def moved(d, way):
        z = s.col - way * d
        n = 2 * d + (way < 0)

        @pl.when(jnp.logical_and(z >= 0, z < nz))
        def _():
            src = zbuf.at[z]
            pltpu.make_async_remote_copy(
                src_ref=src, dst_ref=src, send_sem=zs.at[n], recv_sem=zr.at[z],
                device_id=s.other, device_id_type=MESH,
            ).wait_recv()
            hop(src, z, way, n)
            hand(src, z, n)

    def done(d, way):
        z = s.col - way * d
        n = 2 * d + (way < 0)

        @pl.when(jnp.logical_and(z >= 0, z < nz))
        def _():
            hopped(zbuf.at[z], z, way, n)
            handed(zbuf.at[z], z, n)

    for d in range(1, max(nz, nc)):
        if d < nz:
            moved(d, 1)
            moved(d, -1)
        if d < nc:
            pc[d - 1].wait_recv()
            at = s.turn(s.chip, -d, nc) * s.cores + s.core
            fc.append(push(wc.at[at], wc.at[at], fs.at[d], fr.at[d], s.other))
    hopped(x, s.col, 1, 0)
    hopped(x, s.col, -1, 1)
    handed(x, s.col, 0)
    for d in range(1, nz):
        done(d, 1)
        done(d, -1)
    for j in range(half):

        @pl.when(jnp.logical_or(s.ci != s.core, slot != j))
        def _(j=j):
            pltpu.make_async_remote_copy(
                src_ref=wr.at[j], dst_ref=wr.at[j], send_sem=ws.at[0], recv_sem=wx.at[j],
                device_id=s.other, device_id_type=MESH,
            ).wait_recv()

    keep.wait()
    for cp in pc:
        cp.wait_send()
    for cp in fc:
        cp.wait()


def spread(x):
    nc, nz = lax.axis_size(("child", "rx")), lax.axis_size("col")
    dma = pltpu.SemaphoreType.DMA
    sems = [dma, dma((2 * nz,)), dma((nz,))] + [dma((nc,))] * 4 + [dma((2 * nz,)), dma((nc,)), dma]
    shapes = [jax.ShapeDtypeStruct((n,) + x.shape, x.dtype) for n in (2 * nc, nc)]
    return remote_call(spread_kernel, (x,), shapes, [ANY, ANY], [pltpu.VMEM((nz,) + x.shape, x.dtype)] + sems, 3)


BASE = 128
FACTOR_WORK = 40_000_000_000
WIDE = 8


def base_inverse(a_ref, d_ref, x_ref):
    n, step = a_ref.shape[0], 8
    ids = lax.broadcasted_iota(jnp.int32, (step, n), 0)
    lanes = lax.broadcasted_iota(jnp.int32, (step, n), 1)
    a = [a_ref[i * step : (i + 1) * step, :] for i in range(n // step)]
    x = [(lanes == ids + i * step).astype(F32) for i in range(n // step)]
    for j in range(0, n, WIDE):
        c0 = j // step
        chunks = range(c0, n // step)
        cols = [[jnp.broadcast_to(a[i][:, j + t : j + t + 1], (step, n)) for i in chunks] for t in range(WIDE)]
        at = [j + t - c0 * step for t in range(WIDE)]
        rows = [a[c0][p : p + 1, :] for p in at]
        xrows = [x[c0][p : p + 1, :] for p in at]
        for t in range(WIDE):
            pivot = cols[t][0][at[t] : at[t] + 1, :]
            d_ref[j + t : j + t + 1, :] = pivot
            inv = 1.0 / pivot
            low = [c * inv for c in cols[t]]
            low[0] = jnp.where(ids > at[t], low[0], 0.0)
            for s in range(t + 1, WIDE):
                f = cols[t][0][at[s] : at[s] + 1, :]
                g = f * inv
                cols[s] = [c - l * f for c, l in zip(cols[s], low)]
                rows[s] = rows[s] - g * rows[t]
                xrows[s] = xrows[s] - g * xrows[t]
            for n_, i in enumerate(chunks):
                a[i] = a[i] - low[n_] * rows[t]
                x[i] = x[i] - low[n_] * xrows[t]
    for i in range(n // step):
        x_ref[i * step : (i + 1) * step, :] = x[i] * (1.0 / jnp.sqrt(d_ref[i * step : (i + 1) * step, :]))


def factor_kernel(a_in, y, full, a, blk, piv, inv):
    n = a.shape[0]
    high = functools.partial(lax.dot_general, precision=lax.Precision.HIGHEST, preferred_element_type=F32)
    ids = lax.broadcasted_iota(jnp.int32, (n, n), 0)
    a[:TILE, :TILE] = a_in[:TILE, :]
    a[TILE:, :TILE] = a_in[TILE : 2 * TILE, :]
    a[:TILE, TILE:] = a_in[TILE : 2 * TILE, :].T
    a[TILE:, TILE:] = a_in[2 * TILE :, :]
    full[...] = a[...]
    y[...] = (ids == lax.broadcasted_iota(jnp.int32, (n, n), 1)).astype(F32)

    def one(k, carry):
        at = pl.ds(pl.multiple_of(k * BASE, BASE), BASE)
        blk[...] = a[at, at]
        base_inverse(blk, piv, inv)
        low = high(a[:, at], inv[...], NT)
        low = jnp.where(ids[:, :BASE] >= (k + 1) * BASE, low, 0.0)
        yk = high(inv[...], y[at, :], (((1,), (0,)), ((), ())))
        a[...] = a[...] - high(low, low, NT)
        y[...] = y[...] - high(low, yk, (((1,), (0,)), ((), ())))
        y[at, :] = yk
        return carry

    lax.fori_loop(0, n // BASE, one, 0)


def factor_inverse(d):
    n = 2 * TILE
    return pl.pallas_call(
        factor_kernel,
        out_shape=[jax.ShapeDtypeStruct((n, n), F32)] * 2,
        scratch_shapes=[pltpu.VMEM((n, n), F32)] + [pltpu.VMEM((BASE, BASE), F32)] * 3,
        name="factor",
        cost_estimate=pl.CostEstimate(flops=FACTOR_WORK, bytes_accessed=8 * n * n, transcendentals=0),
    )(d)


def body(child_blocks, child_panels, child_patterns, child_maps, parent_place, parent_front):
    ci = lax.axis_index("child")
    rx = lax.axis_index("rx")
    core = lax.axis_index("core")
    col = lax.axis_index("col")
    cores = lax.axis_size("core")
    rxn = lax.axis_size("rx")
    row = rx * cores + core
    rown = rxn * cores
    chips = lax.axis_size("child") * rxn
    chip = ci * rxn + rx
    block = child_blocks[0]
    own = child_panels[0]
    depth = own.shape[1]
    width = block.shape[0]
    td = width // TILE
    blocks = child_maps.shape[1] // td
    rd = parent_front.shape[0] // TILE
    cd = parent_front.shape[1] // TILE
    slots_n = parent_place.shape[0]
    i32 = jnp.int32

    share = cd * TILE // (chips * cores)
    me = chip * cores + core
    pos = jnp.stack([ci, row, col, core, me, col * cd, chip]).astype(i32)

    def tile_at(block, group, pos, maps, place):
        return find(maps, place, pos[0], block, group, td, cd)[0]

    def shift(x, axes, d):
        n = lax.axis_size(axes)
        return lax.ppermute(x, axes, [(k, (k + d) % n) for k in range(n)])

    code = (td, CODED, TILE)
    *outgoing, part = tile_call(
        functools.partial(pick_kernel, td, cd), (blocks,), (pos, child_maps, parent_place), (block, own),
        [
            pl.BlockSpec(
                (width, TILE),
                lambda z, pos, maps, place: (0, tile_at(pos[2], lax.rem(pos[2] + z, blocks), pos, maps, place)),
            ),
            pl.BlockSpec((TILE, depth), lambda z, pos, maps, place: (tile_at(pos[1], pos[2], pos, maps, place), 0)),
        ],
        [jax.ShapeDtypeStruct(code, jnp.int16)] * blocks + [jax.ShapeDtypeStruct((TILE, depth), own.dtype)],
        [pl.BlockSpec(code, lambda z, *_: (0, 0, 0))] * blocks + [pl.BlockSpec((TILE, depth), lambda z, *_: (0, 0))],
        scratch=[pltpu.VMEM(code, jnp.int16)],
    )
    raw = [shift(x, "col", d) if d else x for d, x in enumerate(outgoing)]

    smem = pl.BlockSpec(memory_space=pltpu.SMEM)
    dims = (td, cd, rd, chips, blocks, cores, rown)
    sizes = [(chips + 2,), (chips, blocks), (8, 4), (7, cd), (7, rd * cd)]
    rowt, fac, diagt, stript, fint = pl.pallas_call(
        functools.partial(plan_kernel, dims),
        in_specs=[smem] * 4, out_specs=[smem] * 5, name="plan",
        out_shape=[jax.ShapeDtypeStruct(z, i32) for z in sizes],
        scratch_shapes=[pltpu.SMEM((2, slots_n), i32)],
    )(pos, child_maps, parent_place, child_patterns)

    partner = panel_gather(part)
    diag_part = tile_call(
        diag_kernel, (3,), (diagt,), (block, parent_front, own, partner),
        [
            pl.BlockSpec((TILE, TILE), lambda k, t: (t[0, k], t[1, k])),
            pl.BlockSpec((TILE, TILE), lambda k, t: (t[2, k], t[3, k])),
            pl.BlockSpec((TILE, depth), lambda k, t: (t[0, k], 0)),
            pl.BlockSpec((1, TILE, depth), lambda k, t: (t[7, k], 0, 0)),
        ],
        jax.ShapeDtypeStruct((3 * TILE, TILE), F32),
        pl.BlockSpec((TILE, TILE), lambda k, t: (k, 0)),
    )
    plane = ("child", "rx", "core")
    diagonal = sum_all(diag_part)
    diagonal, *raw = lax.optimization_barrier((diagonal, *raw))

    row_code = (CODED, blocks * TILE)
    strip_rows, *coded = tile_call(
        update_kernel, (chips,), (rowt, fac, pos), (*raw, own, partner),
        [pl.BlockSpec((1, CODED, TILE), lambda p, r, f, pos: (r[p], 0, 0))] * blocks + [
            pl.BlockSpec((TILE, depth), lambda p, r, f, pos: (r[p], 0)),
            pl.BlockSpec((blocks, TILE, depth), lambda p, r, f, pos: (0, 0, 0)),
        ],
        [jax.ShapeDtypeStruct((2, TILE, blocks * TILE), F32)] + [jax.ShapeDtypeStruct(row_code, jnp.int16)] * chips,
        [pl.BlockSpec((2, TILE, blocks * TILE), lambda p, *_: (0, 0, 0))]
        + [pl.BlockSpec(row_code, lambda p, *_: (0, 0))] * chips,
        scratch=[pltpu.VMEM(row_code, jnp.int16)],
    )
    piece = (share + META, 2 * TILE)
    parts = tile_call(
        strip_kernel, (1,), (stript, pos), (strip_rows, parent_front, parent_front),
        [
            pl.BlockSpec(strip_rows.shape, lambda k, t, pos: (0, 0, 0)),
            pl.BlockSpec((TILE, cd * TILE), lambda k, t, pos: (t[0, 0], 0)),
            pl.BlockSpec((TILE, cd * TILE), lambda k, t, pos: (t[0, 1], 0)),
        ],
        [jax.ShapeDtypeStruct(piece, jnp.int16)] * (chips * cores),
        [pl.BlockSpec(piece, lambda k, t, pos: (0, 0))] * (chips * cores),
        scratch=[pltpu.VMEM((cd * TILE, 2 * TILE), F32)],
    )
    diagonal, parts, coded = lax.optimization_barrier((diagonal, list(parts), coded))
    parts = [shift(x, plane, d) if d else x for d, x in enumerate(parts)]
    first = [shift(x, ("child", "rx"), d) if d else x for d, x in enumerate(coded)]
    inverse, diagonal = factor_inverse(diagonal)
    inverse, parts = lax.optimization_barrier((inverse, parts))

    vm = IN_VMEM
    piece = pl.pallas_call(
        solve_kernel, out_shape=jax.ShapeDtypeStruct(piece, jnp.int16), name="solve",
        in_specs=[smem, smem] + [vm] * (2 + len(parts)), out_specs=vm,
    )(pos, parent_place, diagonal, inverse, *parts)
    piece, first = lax.optimization_barrier((piece, first))
    second = [shift(x, "core", 1) for x in first]
    wc, wr = spread(piece)

    per = 2
    return tile_call(
        final_kernel, (rd, cd // per), (fint,), (parent_front, wr, wc, *first, *second),
        [
            pl.BlockSpec((TILE, per * TILE), lambda i, j, t: (i, j)),
            pl.BlockSpec(wr.shape, lambda i, j, t: (0, 0, 0)),
            pl.BlockSpec(wc.shape, lambda i, j, t: (0, 0, 0)),
        ] + [ANY] * (2 * chips),
        jax.ShapeDtypeStruct(parent_front.shape, F32),
        pl.BlockSpec((TILE, per * TILE), lambda i, j, t: (i, j)),
        scratch=[pltpu.VMEM((n * TILE, 2 * TILE), BF16) for n in (rd, rd, cd, cd)]
        + [pltpu.VMEM((2 * chips,) + row_code, jnp.int16), pltpu.SemaphoreType.DMA((2 * chips,))],
    )


def solution(mesh):
    child, row, col = mesh.devices.shape
    cores = child * row // col
    fine = Mesh(mesh.devices.reshape(child, row // cores, cores, col), ("child", "rx", "core", "col"))
    return jax.shard_map(
        body,
        mesh=fine,
        in_specs=(
            P("child", ("rx", "core"), "col"),
            P("child", ("rx", "core"), None),
            P(),
            P(),
            P(),
            P(("child", "rx", "core"), "col"),
        ),
        out_specs=P(("child", "rx", "core"), "col"),
        check_vma=False,
    )
```

```python
import functools
import math

import jax
import jax.numpy as jnp
from jax import lax
from jax.experimental import pallas as pl
from jax.experimental.pallas import tpu as pltpu
from jax.sharding import Mesh, PartitionSpec as P

TILE = 256
F32 = jnp.float32
BF16 = jnp.bfloat16
META = 16
CODED = TILE + META
FULL = 32767.0
NT = (((1,), (1,)), ((), ()))
NN = (((1,), (0,)), ((), ()))


def dot(a, b, dims):
    return lax.dot_general(a, b, dims, preferred_element_type=F32)


def split(x):
    hi = x.astype(BF16)
    return hi, (x - hi.astype(F32)).astype(BF16)


def tile_call(kernel, grid, tables, operands, in_specs, out_shape, out_spec, name, cost=None, scratch=()):
    return pl.pallas_call(
        kernel,
        grid_spec=pltpu.PrefetchScalarGridSpec(
            num_scalar_prefetch=len(tables), grid=grid, in_specs=in_specs, out_specs=out_spec,
            scratch_shapes=list(scratch),
        ),
        out_shape=out_shape,
        name=name,
        cost_estimate=cost,
    )(*tables, *operands)


def powers(k):
    h = jnp.floor(k * 0.5)
    return jnp.exp2(h), jnp.exp2(k - h)


def encode(x):
    top = jnp.maximum(jnp.max(jnp.abs(x), axis=0, keepdims=True), 1e-30)
    k = jnp.ceil(jnp.log2(top) + 1e-3)
    p, r = powers(-k)
    part = jnp.clip(jnp.ceil(top * p * r * FULL), 1.0, FULL)
    q = jnp.floor(x * ((FULL * FULL / part) * p * r) + 0.5).astype(jnp.int32)
    ids = lax.broadcasted_iota(jnp.int32, (META, x.shape[1]), 0)
    meta = jnp.where(ids == 0, k.astype(jnp.int32), jnp.where(ids == 1, part.astype(jnp.int32), 0))
    return q.astype(jnp.int16), meta.astype(jnp.int16)


def decode(code):
    n = code.shape[0] - META
    meta = code[n:, :].astype(jnp.int32).astype(F32)
    p, r = powers(meta[0:1, :])
    return code[:n, :].astype(jnp.int32).astype(F32) * (meta[1:2, :] * (1.0 / (FULL * FULL)) * p * r)


def find(maps, place, child, block, group, td, width):
    at = jnp.int32(0)
    ok = jnp.int32(0)
    for t in range(td):
        hit = place[maps[child, block * td + t]] // width == group
        at = jnp.where(hit, t, at)
        ok = jnp.where(hit, 1, ok)
    return at, ok


def pick_kernel(td, pos, maps, place, src, out):
    for r in range(td):
        q, meta = encode(src[r * TILE : (r + 1) * TILE, :])
        out[r, :TILE, :] = q
        out[r, TILE:, :] = meta


def part_kernel(td, cd, pos, maps, place, panel, part):
    ok = find(maps, place, pos[0], pos[1], pos[2], td, cd)[1]
    part[...] = jnp.where(ok != 0, panel[...], jnp.zeros_like(panel))


def plan_kernel(dims, pos, maps, place, pat, rowt, fac, diagt, stript, fint, inv):
    td, cd, rd, chips, blocks, cores, rown = dims
    ci, row, col, core = pos[0], pos[1], pos[2], pos[3]
    group = ci * rown + row
    chip = pos[6]
    rxn = chips // 2
    slots_n, tiles_n = place.shape[0], maps.shape[1]

    @pl.loop(0, slots_n)
    def _(k):
        inv[0, k] = -1
        inv[1, k] = -1

    @pl.loop(0, tiles_n)
    def _(k):
        inv[0, place[maps[0, k]]] = k
        inv[1, place[maps[1, k]]] = k

    from_col = [lax.rem(col + blocks - d, blocks) for d in range(blocks)]
    cols = [find(maps, place, ci, b, col, td, cd) for b in from_col]
    for d in range(chips):
        at, ok = find(maps, place, ci, row, lax.rem(chip + d, chips), td, cd)
        rowt[d] = at
        for n, (b, (tile, good)) in enumerate(zip(from_col, cols)):
            fac[d, n] = pat[ci, row * td + at, b * td + tile] * ok * good
    e = (place[0], place[1])
    ie = (inv[ci, e[0]], inv[ci, e[1]])
    le = [jnp.maximum(i, 0) for i in ie]
    own = [((ie[a] >= 0) & (le[a] // td == row)).astype(jnp.int32) for a in range(2)]
    for a in range(2):
        rowt[chips + a] = jnp.where(own[a] != 0, lax.rem(e[a] // cd + chips - chip, chips), -1)
        for b in range(a + 1):
            k = a + b
            live = own[a] * (ie[b] >= 0).astype(jnp.int32) * pat[ci, le[a], le[b]]
            diagt[0, k] = le[a] % td
            diagt[1, k] = le[b] % td
            diagt[2, k] = e[a] % rd
            diagt[3, k] = e[b] % cd
            diagt[4, k] = live * (le[b] // td == col).astype(jnp.int32)
            diagt[5, k] = ((e[a] // rd == group) & (e[b] // cd == col)).astype(jnp.int32)
            diagt[6, k] = live * (e[b] // cd == col).astype(jnp.int32)
            diagt[7, k] = le[b] // td
        stript[0, a] = e[a] % rd

        for q in range(cd):
            slot = col * cd + q
            iq = inv[ci, slot]
            free = ((slot != e[0]) & (slot != e[1])).astype(jnp.int32)
            stript[1 + a, q] = jnp.maximum(iq, 0) // td
            stript[3 + a, q] = own[a] * free * (iq >= 0).astype(jnp.int32)
            stript[5 + a, q] = free * (e[a] // rd == group).astype(jnp.int32)
    for k in range(2, cd):
        stript[0, k] = 0

    @pl.loop(0, rd * cd)
    def _(k):
        slot = col * cd + k % cd
        for c in range(2):
            r, t = inv[c, group * rd + k // cd], inv[c, slot]
            ok = ((r >= 0) & (t >= 0)).astype(jnp.int32)
            source = jnp.maximum(r, 0) // td
            far = (source % cores != core).astype(jnp.int32)
            fint[3 * c, k] = far * chips + lax.rem(chip + chips - (c * rxn + source // cores), chips)
            fint[3 * c + 1, k] = jnp.maximum(t, 0) // td
            fint[3 * c + 2, k] = ok
        fint[6, k] = jnp.where(slot == e[0], 1, jnp.where(slot == e[1], 2, 0))


def diag_kernel(t, blk, front, ea, eb, out):
    k = pl.program_id(0)
    x = jnp.where(t[4, k] != 0, blk[...], 0.0) + jnp.where(t[5, k] != 0, front[...], 0.0)
    out[...] = x - jnp.where(t[6, k] != 0, dot(ea[...], eb[0], NT), 0.0)


def update_kernel(rowt, fac, pos, *refs):
    blocks = fac.shape[1]
    raws, (panel, partner, strip), outs, tmp = refs[:blocks], refs[blocks : blocks + 3], refs[blocks + 3 : -1], refs[-1]
    p = pl.program_id(0)
    chips = pl.num_programs(0)

    @pl.when(p == 0)
    def _():
        strip[...] = jnp.zeros_like(strip)

    for d, raw in enumerate(raws):
        b = lax.rem(pos[2] + blocks - d, blocks)
        at = pl.ds(pl.multiple_of(b * TILE, TILE), TILE)
        u = decode(raw[0]) - dot(panel[...], partner[b], NT)
        u = jnp.where(fac[p, d] != 0, u, 0.0)
        q, meta = encode(u)
        tmp[:TILE, at] = q
        tmp[TILE:, at] = meta
        for a in range(2):

            @pl.when(rowt[chips + a] == p)
            def _(a=a, u=u, at=at):
                strip[a, :, at] = u

    for d, out in enumerate(outs):

        @pl.when(p == d)
        def _(out=out):
            out[...] = tmp[...]


def strip_kernel(t, upd, f0, f1, out, g):
    cd = t.shape[1]
    some = sum(t[n, q] for n in range(3, 7) for q in range(cd))

    @pl.when(some == 0)
    def _():
        out[...] = jnp.zeros_like(out)

    @pl.when(some != 0)
    def _():
        g[...] = jnp.zeros_like(g)
        for q in range(cd):
            for a, f in enumerate((f0, f1)):

                @pl.when(t[3 + a, q] + t[5 + a, q] != 0)
                def _(q=q, a=a, f=f):
                    at = pl.ds(pl.multiple_of(t[1 + a, q] * TILE, TILE), TILE)
                    x = jnp.where(t[3 + a, q] != 0, upd[a, :, at], 0.0)
                    x = x + jnp.where(t[5 + a, q] != 0, f[:, q * TILE : (q + 1) * TILE], 0.0)
                    g[q * TILE : (q + 1) * TILE, a * TILE : (a + 1) * TILE] = x.T

        n = out.shape[2] - META
        for p in range(out.shape[1]):
            for k in range(out.shape[0]):
                m = p * out.shape[0] + k
                code, meta = encode(g[m * n : (m + 1) * n, :])
                out[k, p, :n, :] = code
                out[k, p, n:, :] = meta


def final_kernel(t, front, wr, wc, codes, out, rh, rl, ch, cl, buf, sem):
    i, j = pl.program_id(0), pl.program_id(1)
    per = out.shape[1] // TILE
    base = (i * pl.num_programs(1) + j) * per

    @pl.when(base == 0)
    def _():
        cp = pltpu.make_async_copy(codes, buf, sem)
        cp.start()
        for src, hi, lo in ((wr, rh, rl), (wc, ch, cl)):
            n = src.shape[1] - META
            for p in range(src.shape[0]):
                at = pl.ds(p * n, n)
                hi[at, :], lo[at, :] = split(decode(src[p]))
        cp.wait()

    ri = pl.ds(pl.multiple_of(i * TILE, TILE), TILE)
    cj = pl.ds(pl.multiple_of(j * TILE * per, TILE), TILE * per)
    wh, wl = rh[ri, :], rl[ri, :]
    big = dot(wh, ch[cj, :], NT)
    out[...] = front[...] - (big + (dot(wh, cl[cj, :], NT) + dot(wl, ch[cj, :], NT)))
    for m in range(per):
        k = base + m
        at = slice(m * TILE, (m + 1) * TILE)
        for c in range(2):

            @pl.when(t[3 * c + 2, k] != 0)
            def _(c=c, k=k, at=at):
                lanes = pl.ds(pl.multiple_of(t[3 * c + 1, k] * TILE, TILE), TILE)
                out[:, at] = out[:, at] + decode(buf[t[3 * c, k], :, lanes])

        for n in range(2):

            @pl.when(t[6, k] == n + 1)
            def _(n=n, at=at):
                half = slice(n * TILE, (n + 1) * TILE)
                out[:, at] = rh[ri, half].astype(F32) + rl[ri, half].astype(F32)


MESH = pl.DeviceIdType.MESH


class Spot:
    def __init__(self):
        self.ci, self.rx = lax.axis_index("child"), lax.axis_index("rx")
        self.core, self.col = lax.axis_index("core"), lax.axis_index("col")
        self.rxn, self.cores, self.cols = lax.axis_size("rx"), lax.axis_size("core"), lax.axis_size("col")
        self.chips = lax.axis_size("child") * self.rxn
        self.chip = self.ci * self.rxn + self.rx
        self.other = {"core": 1 - self.core}

    def id(self, chip, core=None):
        core = self.core if core is None else core
        return {"child": chip // self.rxn, "rx": lax.rem(chip, self.rxn), "core": core}

    def turn(self, at, d, n):
        return lax.rem(at + (d % n), n)


def greet(ids):
    bar = pltpu.get_barrier_semaphore()
    for i in ids:
        pl.semaphore_signal(bar, inc=1, device_id=i, device_id_type=MESH)
    pl.semaphore_wait(bar, len(ids))


def push(src, dst, send, recv, to):
    cp = pltpu.make_async_remote_copy(
        src_ref=src, dst_ref=dst, send_sem=send, recv_sem=recv, device_id=to, device_id_type=MESH
    )
    cp.start()
    return cp


def remote_call(kernel, operands, out_shape, out_specs, scratch, cid, name, flops=0):
    return pl.pallas_call(
        kernel,
        out_shape=out_shape,
        in_specs=[pl.BlockSpec(memory_space=pltpu.VMEM)] * len(operands),
        out_specs=out_specs,
        scratch_shapes=scratch,
        compiler_params=pltpu.CompilerParams(collective_id=cid, has_side_effects=True),
        cost_estimate=pl.CostEstimate(flops=flops, bytes_accessed=1 << 20, transcendentals=0),
        name=name,
    )(*operands)


ANY = pl.BlockSpec(memory_space=pl.ANY)
IN_VMEM = pl.BlockSpec(memory_space=pltpu.VMEM)


def panel_kernel(x, out, loc, ss, rs, fs, fr):
    s = Spot()
    n = s.rxn
    me = s.rx * s.cores + s.core
    peers = [{"rx": s.turn(s.rx, d, n)} for d in range(1, n)]
    greet(peers + [s.other])
    keep = pltpu.make_async_copy(x, out.at[me], loc)
    keep.start()
    cps = [push(x, out.at[me], ss.at[d], rs.at[d], to) for d, to in enumerate(peers, 1)]
    fwd = [push(x, out.at[me], fs.at[0], fr.at[0], s.other)]
    for d, cp in enumerate(cps, 1):
        cp.wait_recv()
        at = s.turn(s.rx, -d, n) * s.cores + s.core
        fwd.append(push(out.at[at], out.at[at], fs.at[d], fr.at[d], s.other))
    keep.wait()
    for cp in cps:
        cp.wait_send()
    for cp in fwd:
        cp.wait()


def panel_gather(x):
    n = lax.axis_size("rx")
    shape = (n * lax.axis_size("core"),) + x.shape
    dma = pltpu.SemaphoreType.DMA
    return remote_call(
        panel_kernel, (x,), jax.ShapeDtypeStruct(shape, x.dtype), ANY,
        [dma, dma((n,)), dma((n,)), dma((n,)), dma((n,))], 0, "panels",
    )


def sum_kernel(x, out, half, mine, got, part, zgot, ss0, rs0, ss1, rs1, ss2, rs2, ss3, rs3, ss4, rs4, ss5, rs5):
    s = Spot()
    nc, nz = s.chips, s.cols
    chips = [s.turn(s.chip, d, nc) for d in range(1, nc)]
    cols = [s.turn(s.col, d, nz) for d in range(1, nz)]
    greet([s.other] + [s.id(t) for t in chips] + [{"col": t} for t in cols])
    cp = push(x.at[1 - s.core], half, ss0, rs0, s.other)
    cp.wait()
    mine[...] = x[s.core] + half[...]
    cps = [push(mine.at[t], got.at[d], ss1.at[d], rs1.at[d], s.id(t)) for d, t in enumerate(chips)]
    for cp in cps:
        cp.wait()
    total = mine[s.chip]
    for d in range(nc - 1):
        total = total + got[d]
    part[...] = total
    cps = [push(part.at[t], zgot.at[d], ss2.at[d], rs2.at[d], {"col": t}) for d, t in enumerate(cols)]
    for cp in cps:
        cp.wait()
    total = part[s.col]
    for d in range(nz - 1):
        total = total + zgot[d]
    out[s.core, s.chip, s.col] = total

    def send_z(d, t):
        own = out.at[s.core, s.chip, s.col]
        return push(own, own, ss3.at[d], rs3.at[d], {"col": t})

    def send_xy(z, n):
        own = out.at[s.core, s.chip, z]
        return [push(own, own, ss4.at[n, d], rs4.at[n, d], s.id(t)) for d, t in enumerate(chips)]

    def send_core(c, z, n, m):
        own = out.at[s.core, c, z]
        return push(own, own, ss5.at[n, m], rs5.at[n, m], s.other)

    zc = [send_z(d, t) for d, t in enumerate(cols)]
    xy = [send_xy(s.col, 0)]
    cc = [send_core(s.chip, s.col, 0, 0)]
    for n in range(nz):
        z = s.turn(s.col, -n, nz)
        if n:
            zc[n - 1].wait_recv()
            xy.append(send_xy(z, n))
            cc.append(send_core(s.chip, z, n, 0))
    for n in range(nz):
        for d in range(nc - 1):
            xy[n][d].wait_recv()
            cc.append(send_core(s.turn(s.chip, -(d + 1), nc), s.turn(s.col, -n, nz), n, d + 1))
    for cp in zc + [x for row in xy for x in row]:
        cp.wait_send()
    for cp in cc:
        cp.wait()


def sum_all(x):
    nc, nz = lax.axis_size(("child", "rx")), lax.axis_size("col")
    tail = (x.shape[0] // (2 * nc * nz), x.shape[1])
    full = jax.ShapeDtypeStruct((2, nc, nz) + tail, F32)
    dma = pltpu.SemaphoreType.DMA
    sems = [dma, dma, dma((nc,)), dma((nc,)), dma((nz,)), dma((nz,)), dma((nz,)), dma((nz,)), dma((nz, nc)), dma((nz, nc)), dma((nz, nc)), dma((nz, nc))]
    half, part = (nc, nz) + tail, (nz,) + tail
    vm = [pltpu.VMEM(z, F32) for z in (half, half, (nc - 1,) + part, part, (nz - 1,) + tail)]
    out = remote_call(sum_kernel, (x.reshape(full.shape),), full, IN_VMEM, vm + sems, 1, "total")
    return out.reshape(x.shape)


BASE = 128
WIDE = 8


def base_inverse(a_ref, d_ref, x_ref):
    n, step = a_ref.shape[0], 8
    ids = lax.broadcasted_iota(jnp.int32, (step, n), 0)
    lanes = lax.broadcasted_iota(jnp.int32, (step, n), 1)
    a = [a_ref[i * step : (i + 1) * step, :] for i in range(n // step)]
    x = [(lanes == ids + i * step).astype(F32) for i in range(n // step)]
    for j in range(0, n, WIDE):
        c0 = j // step
        chunks = range(c0, n // step)
        cols = [[jnp.broadcast_to(a[i][:, j + t : j + t + 1], (step, n)) for i in chunks] for t in range(WIDE)]
        at = [j + t - c0 * step for t in range(WIDE)]
        rows = [a[c0][p : p + 1, :] for p in at]
        xrows = [x[c0][p : p + 1, :] for p in at]
        for t in range(WIDE):
            pivot = cols[t][0][at[t] : at[t] + 1, :]
            d_ref[j + t : j + t + 1, :] = pivot
            inv = 1.0 / pivot
            low = [c * inv for c in cols[t]]
            low[0] = jnp.where(ids > at[t], low[0], 0.0)
            for s in range(t + 1, WIDE):
                f = cols[t][0][at[s] : at[s] + 1, :]
                g = f * inv
                cols[s] = [c - l * f for c, l in zip(cols[s], low)]
                rows[s] = rows[s] - g * rows[t]
                xrows[s] = xrows[s] - g * xrows[t]
            for n_, i in enumerate(chunks):
                a[i] = a[i] - low[n_] * rows[t]
                x[i] = x[i] - low[n_] * xrows[t]
    for i in range(n // step):
        x_ref[i * step : (i + 1) * step, :] = x[i] * (1.0 / jnp.sqrt(d_ref[i * step : (i + 1) * step, :]))


def factor_steps(a_in, y, full, a, blk, piv, inv):
    n = a.shape[0]
    high = functools.partial(lax.dot_general, precision=lax.Precision.HIGHEST, preferred_element_type=F32)
    ids = lax.broadcasted_iota(jnp.int32, (n, n), 0)
    a[:TILE, :TILE] = a_in[:TILE, :]
    a[TILE:, :TILE] = a_in[TILE : 2 * TILE, :]
    a[:TILE, TILE:] = a_in[TILE : 2 * TILE, :].T
    a[TILE:, TILE:] = a_in[2 * TILE :, :]
    full[...] = a[...]
    y[...] = (ids == lax.broadcasted_iota(jnp.int32, (n, n), 1)).astype(F32)

    def one(k, carry):
        at = pl.ds(pl.multiple_of(k * BASE, BASE), BASE)
        blk[...] = a[at, at]
        base_inverse(blk, piv, inv)
        low = high(a[:, at], inv[...], NT)
        low = jnp.where(ids[:, :BASE] >= (k + 1) * BASE, low, 0.0)
        yk = high(inv[...], y[at, :], (((1,), (0,)), ((), ())))
        a[...] = a[...] - high(low, low, NT)
        y[...] = y[...] - high(low, yk, (((1,), (0,)), ((), ())))
        y[at, :] = yk
        return carry

    lax.fori_loop(0, n // BASE, one, 0)


def front_kernel(
    place, diag, x, c0, *refs
):
    s = Spot()
    nc, nz = s.chips, s.cols
    far = refs[: nc - 1]
    buf, wc, wr = refs[nc - 1 : nc + 2]
    (y, full, a, blk, piv, inv, half_in, mine, got, piece, zbuf,
     loc, keep_sem, hs, hr, cs, cr, bs, br, es, er, zs, zr, ps, pr, fs, fr, ws, wx, wl) = refs[nc + 2 :]
    half = wr.shape[0]
    n = piece.shape[0] - META
    me = s.chip * s.cores + s.core
    slot = lax.rem(me, half)
    count = nc * s.cores
    chips = [s.turn(s.chip, d, nc) for d in range(1, nc)]
    plane = [s.turn(me, d, count) for d in range(1, count)]
    greet([s.id(t // s.cores, lax.rem(t, s.cores)) for t in plane] + [{"col": s.turn(s.col, d, nz)} for d in range(1, nz)])

    pairs = [push(x.at[1 - s.core, t], half_in.at[d], hs.at[d], hr.at[d], s.other) for d, t in enumerate(chips + [s.chip])]
    keep0 = pltpu.make_async_copy(c0, buf.at[0], keep_sem)
    keep0.start()
    sent = []
    for d, t in enumerate(chips + [s.chip]):
        pairs[d].wait_recv()
        q, meta = encode(decode(x[s.core, t]) + decode(half_in[d]))
        mine[d, :n, :] = q
        mine[d, n:, :] = meta
        if d < nc - 1:
            sent.append(push(mine.at[d], got.at[d], cs.at[d], cr.at[d], s.id(t)))
    bulk = [push(src, buf.at[d], bs.at[d], br.at[d], s.id(t)) for d, (t, src) in enumerate(zip(chips, far), 1)]
    echo = [push(c0, buf.at[nc], es.at[0], er.at[0], s.other)]

    factor_steps(diag, y, full, a, blk, piv, inv)

    g = decode(mine[nc - 1])
    for d, cp in enumerate(sent):
        cp.wait_recv()
        g = g + decode(got[d])
    unit = math.gcd(n, TILE)
    rows = []
    for u in range(n // unit):
        first = me * n + u * unit
        z = g[u * unit : (u + 1) * unit, :]
        for k in range(2):
            own = full[pl.ds(pl.multiple_of(k * TILE + lax.rem(first, TILE), unit), unit), :]
            z = jnp.where(s.col * (count * n // TILE) + first // TILE == place[k], own, z)
        rows.append(z)
    g = jnp.concatenate(rows, axis=0)
    w = lax.dot_general(g, y[...], NT, precision=lax.Precision.HIGHEST, preferred_element_type=F32)
    q, meta = encode(w)
    piece[:n, :] = q
    piece[n:, :] = meta
    x = piece

    def hand(src, z, d):
        here = jnp.logical_and(z == s.chip, s.ci == s.core)

        @pl.when(here)
        def _():
            pltpu.make_async_copy(src, wr.at[slot], wl).start()

        @pl.when(jnp.logical_not(here))
        def _():
            push(src, wr.at[slot], ws.at[d], wx.at[slot], s.id(z, s.ci))

    def handed(src, z, d):
        here = jnp.logical_and(z == s.chip, s.ci == s.core)

        @pl.when(here)
        def _():
            pltpu.make_async_copy(src, wr.at[slot], wl).wait()

        @pl.when(jnp.logical_not(here))
        def _():
            pltpu.make_async_remote_copy(
                src_ref=src, dst_ref=wr.at[slot], send_sem=ws.at[d], recv_sem=wx.at[slot],
                device_id=s.id(z, s.ci), device_id_type=MESH,
            ).wait_send()

    def hop(src, z, way, d):
        to = s.col + way

        @pl.when(jnp.logical_and(to >= 0, to < nz))
        def _():
            push(src, zbuf.at[z], zs.at[d], zr.at[z], {"col": to})

    def hopped(src, z, way, d):
        to = s.col + way

        @pl.when(jnp.logical_and(to >= 0, to < nz))
        def _():
            pltpu.make_async_remote_copy(
                src_ref=src, dst_ref=zbuf.at[z], send_sem=zs.at[d], recv_sem=zr.at[z],
                device_id={"col": to}, device_id_type=MESH,
            ).wait_send()

    hop(x, s.col, 1, 0)
    hop(x, s.col, -1, 1)
    hand(x, s.col, 0)
    keep = pltpu.make_async_copy(x, wc.at[me], loc)
    keep.start()
    pc = [push(x, wc.at[me], ps.at[d], pr.at[d], s.id(t)) for d, t in enumerate(chips, 1)]
    fc = [push(x, wc.at[me], fs.at[0], fr.at[0], s.other)]

    def moved(d, way):
        z = s.col - way * d
        n = 2 * d + (way < 0)

        @pl.when(jnp.logical_and(z >= 0, z < nz))
        def _():
            src = zbuf.at[z]
            pltpu.make_async_remote_copy(
                src_ref=src, dst_ref=src, send_sem=zs.at[n], recv_sem=zr.at[z],
                device_id=s.other, device_id_type=MESH,
            ).wait_recv()
            hop(src, z, way, n)
            hand(src, z, n)

    def done(d, way):
        z = s.col - way * d
        n = 2 * d + (way < 0)

        @pl.when(jnp.logical_and(z >= 0, z < nz))
        def _():
            hopped(zbuf.at[z], z, way, n)
            handed(zbuf.at[z], z, n)

    for d in range(1, max(nz, nc)):
        if d < nz:
            moved(d, 1)
            moved(d, -1)
        if d < nc:
            bulk[d - 1].wait_recv()
            echo.append(push(buf.at[d], buf.at[nc + d], es.at[d], er.at[d], s.other))
    for d in range(1, nc):
        pc[d - 1].wait_recv()
        at = s.turn(s.chip, -d, nc) * s.cores + s.core
        fc.append(push(wc.at[at], wc.at[at], fs.at[d], fr.at[d], s.other))
    hopped(x, s.col, 1, 0)
    hopped(x, s.col, -1, 1)
    handed(x, s.col, 0)
    for d in range(1, nz):
        done(d, 1)
        done(d, -1)
    for j in range(half):

        @pl.when(jnp.logical_or(s.ci != s.core, slot != j))
        def _(j=j):
            pltpu.make_async_remote_copy(
                src_ref=wr.at[j], dst_ref=wr.at[j], send_sem=ws.at[0], recv_sem=wx.at[j],
                device_id=s.other, device_id_type=MESH,
            ).wait_recv()

    keep.wait()
    keep0.wait()
    for cp in pairs + sent + bulk + pc:
        cp.wait_send()
    for cp in fc + echo:
        cp.wait()


def front_call(place, diag, x, coded):
    nc, nz = lax.axis_size(("child", "rx")), lax.axis_size("col")
    n = 2 * TILE
    dma = pltpu.SemaphoreType.DMA
    vm, smem = IN_VMEM, pl.BlockSpec(memory_space=pltpu.SMEM)
    piece, code = x.shape[2:], coded[0].shape
    scratch = [pltpu.VMEM((n, n), F32)] * 3 + [pltpu.VMEM((BASE, BASE), F32)] * 3
    scratch += [pltpu.VMEM((k,) + piece, x.dtype) for k in (nc, nc, nc)]
    scratch += [pltpu.VMEM(piece, x.dtype), pltpu.VMEM((nz,) + piece, x.dtype)]
    scratch += [dma, dma] + [dma((nc,))] * 8 + [dma((2 * nz,)), dma((nz,))] + [dma((nc,))] * 4
    scratch += [dma((2 * nz,)), dma((nc,)), dma]
    shapes = [(2 * nc,) + code, (2 * nc,) + piece, (nc,) + piece]
    return pl.pallas_call(
        front_kernel,
        out_shape=[jax.ShapeDtypeStruct(k, x.dtype) for k in shapes],
        in_specs=[smem, vm, vm, vm] + [ANY] * (nc - 1),
        out_specs=[ANY] * 3,
        scratch_shapes=scratch,
        compiler_params=pltpu.CompilerParams(collective_id=3, has_side_effects=True),
        name="front",
    )(place, diag, x, *coded)


def body(child_blocks, child_panels, child_patterns, child_maps, parent_place, parent_front):
    ci = lax.axis_index("child")
    rx = lax.axis_index("rx")
    core = lax.axis_index("core")
    col = lax.axis_index("col")
    cores = lax.axis_size("core")
    rxn = lax.axis_size("rx")
    row = rx * cores + core
    rown = rxn * cores
    chips = lax.axis_size("child") * rxn
    chip = ci * rxn + rx
    group = ci * rown + row
    block = child_blocks[0]
    own = child_panels[0]
    depth = own.shape[1]
    width = block.shape[0]
    td = width // TILE
    blocks = child_maps.shape[1] // td
    rd = parent_front.shape[0] // TILE
    cd = parent_front.shape[1] // TILE
    slots_n = parent_place.shape[0]
    i32 = jnp.int32

    share = cd * TILE // (chips * cores)
    me = chip * cores + core
    pos = jnp.stack([ci, row, col, core, me, col * cd, chip]).astype(i32)

    def tile_at(block, group, pos, maps, place):
        return find(maps, place, pos[0], block, group, td, cd)[0]

    def shift(x, axes, d):
        n = lax.axis_size(axes)
        return lax.ppermute(x, axes, [(k, (k + d) % n) for k in range(n)])

    code = (td, CODED, TILE)
    heads = (pos, child_maps, parent_place)

    def pick(d):
        return tile_call(
            functools.partial(pick_kernel, td), (1,), heads, (block,),
            [pl.BlockSpec(
                (width, TILE),
                lambda z, pos, maps, place: (0, tile_at(pos[2], lax.rem(pos[2] + d, blocks), pos, maps, place)),
            )],
            jax.ShapeDtypeStruct(code, jnp.int16), pl.BlockSpec(code, lambda z, *_: (0, 0, 0)), "pick",
        )

    order = sorted(range(1, blocks), key=lambda d: -min(d, blocks - d))
    raw = [None] * blocks
    for d in order + [0]:
        x = pick(d)
        raw[d] = shift(x, "col", d) if d else x
    part = tile_call(
        functools.partial(part_kernel, td, cd), (1,), heads, (own,),
        [pl.BlockSpec((TILE, depth), lambda z, pos, maps, place: (tile_at(pos[1], pos[2], pos, maps, place), 0))],
        jax.ShapeDtypeStruct((TILE, depth), own.dtype), pl.BlockSpec((TILE, depth), lambda z, *_: (0, 0)), "part",
    )

    smem = pl.BlockSpec(memory_space=pltpu.SMEM)
    dims = (td, cd, rd, chips, blocks, cores, rown)
    sizes = [(chips + 2,), (chips, blocks), (8, 4), (7, cd), (7, rd * cd)]
    rowt, fac, diagt, stript, fint = pl.pallas_call(
        functools.partial(plan_kernel, dims),
        in_specs=[smem] * 4, out_specs=[smem] * 5, name="plan",
        out_shape=[jax.ShapeDtypeStruct(z, i32) for z in sizes],
        scratch_shapes=[pltpu.SMEM((2, slots_n), i32)],
    )(pos, child_maps, parent_place, child_patterns)

    partner = panel_gather(part)
    diag_part = tile_call(
        diag_kernel, (3,), (diagt,), (block, parent_front, own, partner),
        [
            pl.BlockSpec((TILE, TILE), lambda k, t: (t[0, k], t[1, k])),
            pl.BlockSpec((TILE, TILE), lambda k, t: (t[2, k], t[3, k])),
            pl.BlockSpec((TILE, depth), lambda k, t: (t[0, k], 0)),
            pl.BlockSpec((1, TILE, depth), lambda k, t: (t[7, k], 0, 0)),
        ],
        jax.ShapeDtypeStruct((3 * TILE, TILE), F32),
        pl.BlockSpec((TILE, TILE), lambda k, t: (k, 0)), "diag",
    )
    diagonal = sum_all(diag_part)
    diagonal, *raw = lax.optimization_barrier((diagonal, *raw))

    row_code = (CODED, blocks * TILE)
    strip_rows, *coded = tile_call(
        update_kernel, (chips,), (rowt, fac, pos), (*raw, own, partner),
        [pl.BlockSpec((1, CODED, TILE), lambda p, r, f, pos: (r[p], 0, 0))] * blocks + [
            pl.BlockSpec((TILE, depth), lambda p, r, f, pos: (r[p], 0)),
            pl.BlockSpec((blocks, TILE, depth), lambda p, r, f, pos: (0, 0, 0)),
        ],
        [jax.ShapeDtypeStruct((2, TILE, blocks * TILE), F32)] + [jax.ShapeDtypeStruct(row_code, jnp.int16)] * chips,
        [pl.BlockSpec((2, TILE, blocks * TILE), lambda p, *_: (0, 0, 0))]
        + [pl.BlockSpec(row_code, lambda p, *_: (0, 0))] * chips,
        "update", scratch=[pltpu.VMEM(row_code, jnp.int16)],
    )
    pieces = (cores, chips, share + META, 2 * TILE)
    strips = tile_call(
        strip_kernel, (1,), (stript,), (strip_rows, parent_front, parent_front),
        [
            pl.BlockSpec(strip_rows.shape, lambda k, t: (0, 0, 0)),
            pl.BlockSpec((TILE, cd * TILE), lambda k, t: (t[0, 0], 0)),
            pl.BlockSpec((TILE, cd * TILE), lambda k, t: (t[0, 1], 0)),
        ],
        jax.ShapeDtypeStruct(pieces, jnp.int16),
        pl.BlockSpec(pieces, lambda k, t: (0, 0, 0, 0)), "strip",
        scratch=[pltpu.VMEM((cd * TILE, 2 * TILE), F32)],
    )
    codes, wc, wr = front_call(parent_place, diagonal, strips, coded)

    per = 2
    return tile_call(
        final_kernel, (rd, cd // per), (fint,), (parent_front, wr, wc, codes),
        [
            pl.BlockSpec((TILE, per * TILE), lambda i, j, t: (i, j)),
            pl.BlockSpec(wr.shape, lambda i, j, t: (0, 0, 0)),
            pl.BlockSpec(wc.shape, lambda i, j, t: (0, 0, 0)),
            ANY,
        ],
        jax.ShapeDtypeStruct(parent_front.shape, F32),
        pl.BlockSpec((TILE, per * TILE), lambda i, j, t: (i, j)), "final",
        scratch=[pltpu.VMEM((n * TILE, 2 * TILE), BF16) for n in (rd, rd, cd, cd)]
        + [pltpu.VMEM((2 * chips,) + row_code, jnp.int16), pltpu.SemaphoreType.DMA],
    )


def solution(mesh):
    child, row, col = mesh.devices.shape
    cores = child * row // col
    fine = Mesh(mesh.devices.reshape(child, row // cores, cores, col), ("child", "rx", "core", "col"))
    return jax.shard_map(
        body,
        mesh=fine,
        in_specs=(
            P("child", ("rx", "core"), "col"),
            P("child", ("rx", "core"), None),
            P(),
            P(),
            P(),
            P(("child", "rx", "core"), "col"),
        ),
        out_specs=P(("child", "rx", "core"), "col"),
        check_vma=False,
    )
```

```python
import functools
import math

import jax
import jax.numpy as jnp
from jax import lax
from jax.experimental import pallas as pl
from jax.experimental.pallas import tpu as pltpu
from jax.sharding import Mesh, PartitionSpec as P

TILE = 256
F32 = jnp.float32
BF16 = jnp.bfloat16
META = 16
CODED = TILE + META
FULL = 32767.0
NT = (((1,), (1,)), ((), ()))
NN = (((1,), (0,)), ((), ()))


def dot(a, b, dims):
    return lax.dot_general(a, b, dims, preferred_element_type=F32)


def split(x):
    hi = x.astype(BF16)
    return hi, (x - hi.astype(F32)).astype(BF16)


def tile_call(kernel, grid, tables, operands, in_specs, out_shape, out_spec, name, cost=None, scratch=()):
    return pl.pallas_call(
        kernel,
        grid_spec=pltpu.PrefetchScalarGridSpec(
            num_scalar_prefetch=len(tables), grid=grid, in_specs=in_specs, out_specs=out_spec,
            scratch_shapes=list(scratch),
        ),
        out_shape=out_shape,
        name=name,
        cost_estimate=cost,
    )(*tables, *operands)


def powers(k):
    h = jnp.floor(k * 0.5)
    return jnp.exp2(h), jnp.exp2(k - h)


def encode(x):
    top = jnp.maximum(jnp.max(jnp.abs(x), axis=0, keepdims=True), 1e-30)
    k = jnp.ceil(jnp.log2(top) + 1e-3)
    p, r = powers(-k)
    part = jnp.clip(jnp.ceil(top * p * r * FULL), 1.0, FULL)
    q = jnp.floor(x * ((FULL * FULL / part) * p * r) + 0.5).astype(jnp.int32)
    ids = lax.broadcasted_iota(jnp.int32, (META, x.shape[1]), 0)
    meta = jnp.where(ids == 0, k.astype(jnp.int32), jnp.where(ids == 1, part.astype(jnp.int32), 0))
    return q.astype(jnp.int16), meta.astype(jnp.int16)


def decode(code):
    n = code.shape[0] - META
    meta = code[n:, :].astype(jnp.int32).astype(F32)
    p, r = powers(meta[0:1, :])
    return code[:n, :].astype(jnp.int32).astype(F32) * (meta[1:2, :] * (1.0 / (FULL * FULL)) * p * r)


def find(maps, place, child, block, group, td, width):
    at = jnp.int32(0)
    ok = jnp.int32(0)
    for t in range(td):
        hit = place[maps[child, block * td + t]] // width == group
        at = jnp.where(hit, t, at)
        ok = jnp.where(hit, 1, ok)
    return at, ok


def pick_kernel(td, cd, count, pos, maps, place, src, *refs):
    z = pl.program_id(0)
    tmp = refs[-1]
    for r in range(td):
        q, meta = encode(src[r * TILE : (r + 1) * TILE, :])
        tmp[r, :TILE, :] = q
        tmp[r, TILE:, :] = meta
    outs = refs[-1 - count : -1] if len(refs) == count + 1 else refs[1 : 1 + count]
    for d, out in enumerate(outs):

        @pl.when(z == d)
        def _(out=out):
            out[...] = tmp[...]

    if len(refs) > count + 1:
        panel, part = refs[0], refs[-2]

        @pl.when(z == 0)
        def _():
            ok = find(maps, place, pos[0], pos[1], pos[2], td, cd)[1]
            part[...] = jnp.where(ok != 0, panel[...], jnp.zeros_like(panel))


def plan_kernel(dims, pos, maps, place, pat, rowt, fac, diagt, stript, fint, inv):
    td, cd, rd, chips, blocks, cores, rown = dims
    ci, row, col, core = pos[0], pos[1], pos[2], pos[3]
    group = ci * rown + row
    chip = pos[6]
    rxn = chips // 2
    slots_n, tiles_n = place.shape[0], maps.shape[1]

    @pl.loop(0, slots_n)
    def _(k):
        inv[0, k] = -1
        inv[1, k] = -1

    @pl.loop(0, tiles_n)
    def _(k):
        inv[0, place[maps[0, k]]] = k
        inv[1, place[maps[1, k]]] = k

    from_col = [lax.rem(col + blocks - d, blocks) for d in range(blocks)]
    cols = [find(maps, place, ci, b, col, td, cd) for b in from_col]
    for d in range(chips):
        at, ok = find(maps, place, ci, row, lax.rem(chip + d, chips), td, cd)
        rowt[d] = at
        for n, (b, (tile, good)) in enumerate(zip(from_col, cols)):
            fac[d, n] = pat[ci, row * td + at, b * td + tile] * ok * good
    rowt[chips + 2] = cols[0][0]
    e = (place[0], place[1])
    ie = (inv[ci, e[0]], inv[ci, e[1]])
    le = [jnp.maximum(i, 0) for i in ie]
    own = [((ie[a] >= 0) & (le[a] // td == row)).astype(jnp.int32) for a in range(2)]
    for a in range(2):
        rowt[chips + a] = jnp.where(own[a] != 0, lax.rem(e[a] // cd + chips - chip, chips), -1)
        for b in range(a + 1):
            k = a + b
            live = own[a] * (ie[b] >= 0).astype(jnp.int32) * pat[ci, le[a], le[b]]
            diagt[0, k] = le[a] % td
            diagt[1, k] = le[b] % td
            diagt[2, k] = e[a] % rd
            diagt[3, k] = e[b] % cd
            diagt[4, k] = live * (le[b] // td == col).astype(jnp.int32)
            diagt[5, k] = ((e[a] // rd == group) & (e[b] // cd == col)).astype(jnp.int32)
            diagt[6, k] = live * (e[b] // cd == col).astype(jnp.int32)
            diagt[7, k] = le[b] // td
        stript[0, a] = e[a] % rd

        for q in range(cd):
            slot = col * cd + q
            iq = inv[ci, slot]
            free = ((slot != e[0]) & (slot != e[1])).astype(jnp.int32)
            stript[1 + a, q] = jnp.maximum(iq, 0) // td
            stript[3 + a, q] = own[a] * free * (iq >= 0).astype(jnp.int32)
            stript[5 + a, q] = free * (e[a] // rd == group).astype(jnp.int32)
    for k in range(2, cd):
        stript[0, k] = 0

    @pl.loop(0, rd * cd)
    def _(k):
        slot = col * cd + k % cd
        for c in range(2):
            r, t = inv[c, group * rd + k // cd], inv[c, slot]
            ok = ((r >= 0) & (t >= 0)).astype(jnp.int32)
            source = jnp.maximum(r, 0) // td
            far = (source % cores != core).astype(jnp.int32)
            turn = far * chips + lax.rem(chip + chips - (c * rxn + source // cores), chips)
            fint[2 * c, k] = turn * blocks + jnp.maximum(t, 0) // td
            fint[2 * c + 1, k] = ok
        fint[4, k] = jnp.where(slot == e[0], 1, jnp.where(slot == e[1], 2, 0))


def diag_kernel(t, blk, front, ea, eb, out):
    k = pl.program_id(0)
    x = jnp.where(t[4, k] != 0, blk[...], 0.0) + jnp.where(t[5, k] != 0, front[...], 0.0)
    out[...] = x - jnp.where(t[6, k] != 0, dot(ea[...], eb[0], NT), 0.0)


def update_kernel(rowt, fac, pos, *refs):
    blocks = fac.shape[1]
    raw0, raws, (panel, partner, strip) = refs[0], refs[1:blocks], refs[blocks : blocks + 3]
    outs, tmp, wide = refs[blocks + 3 : -2], refs[-2], refs[-1]
    p = pl.program_id(0)
    chips = pl.num_programs(0)

    @pl.when(p == 0)
    def _():
        strip[...] = jnp.zeros_like(strip)

    for d in range(blocks):
        b = lax.rem(pos[2] + blocks - d, blocks)
        at = pl.ds(pl.multiple_of(b * TILE, TILE), TILE)
        u = (decode(raws[d - 1][0]) if d else raw0[...]) - dot(panel[...], partner[b], NT)
        u = jnp.where(fac[p, d] != 0, u, 0.0)
        wide[:, at] = u
        q, meta = encode(u)
        tmp[b, :TILE, :] = q
        tmp[b, TILE:, :] = meta

    for a in range(2):

        @pl.when(rowt[chips + a] == p)
        def _(a=a):
            strip[a] = wide[...]

    for d, out in enumerate(outs):

        @pl.when(p == d)
        def _(out=out):
            out[...] = tmp[...]


def strip_kernel(t, upd, f0, f1, out, g):
    cd = t.shape[1]
    some = sum(t[n, q] for n in range(3, 7) for q in range(cd))

    @pl.when(some == 0)
    def _():
        out[...] = jnp.zeros_like(out)

    @pl.when(some != 0)
    def _():
        g[...] = jnp.zeros_like(g)
        for q in range(cd):
            for a, f in enumerate((f0, f1)):

                @pl.when(t[3 + a, q] + t[5 + a, q] != 0)
                def _(q=q, a=a, f=f):
                    at = pl.ds(pl.multiple_of(t[1 + a, q] * TILE, TILE), TILE)
                    x = jnp.where(t[3 + a, q] != 0, upd[a, :, at], 0.0)
                    x = x + jnp.where(t[5 + a, q] != 0, f[:, q * TILE : (q + 1) * TILE], 0.0)
                    g[q * TILE : (q + 1) * TILE, a * TILE : (a + 1) * TILE] = x.T

        n = out.shape[2] - META
        for p in range(out.shape[1]):
            for k in range(out.shape[0]):
                m = p * out.shape[0] + k
                code, meta = encode(g[m * n : (m + 1) * n, :])
                out[k, p, :n, :] = code
                out[k, p, n:, :] = meta


def final_kernel(t, front, wr, wc, out, rh, rl, ch, cl):
    i, j = pl.program_id(0), pl.program_id(1)
    per = out.shape[1] // TILE
    base = (i * pl.num_programs(1) + j) * per

    @pl.when(base == 0)
    def _():
        for src, hi, lo in ((wr, rh, rl), (wc, ch, cl)):
            n = src.shape[1] - META
            for p in range(src.shape[0]):
                at = pl.ds(p * n, n)
                hi[at, :], lo[at, :] = split(decode(src[p]))

    ri = pl.ds(pl.multiple_of(i * TILE, TILE), TILE)
    cj = pl.ds(pl.multiple_of(j * TILE * per, TILE), TILE * per)
    wh, wl = rh[ri, :], rl[ri, :]
    big = dot(wh, ch[cj, :], NT)
    out[...] = front[...] - (big + (dot(wh, cl[cj, :], NT) + dot(wl, ch[cj, :], NT)))
    for m in range(per):
        k = base + m
        at = slice(m * TILE, (m + 1) * TILE)
        for n in range(2):

            @pl.when(t[4, k] == n + 1)
            def _(n=n, at=at):
                half = slice(n * TILE, (n + 1) * TILE)
                out[:, at] = rh[ri, half].astype(F32) + rl[ri, half].astype(F32)


MESH = pl.DeviceIdType.MESH


class Spot:
    def __init__(self):
        self.ci, self.rx = lax.axis_index("child"), lax.axis_index("rx")
        self.core, self.col = lax.axis_index("core"), lax.axis_index("col")
        self.rxn, self.cores, self.cols = lax.axis_size("rx"), lax.axis_size("core"), lax.axis_size("col")
        self.chips = lax.axis_size("child") * self.rxn
        self.chip = self.ci * self.rxn + self.rx
        self.other = {"core": 1 - self.core}

    def id(self, chip, core=None):
        core = self.core if core is None else core
        return {"child": chip // self.rxn, "rx": lax.rem(chip, self.rxn), "core": core}

    def turn(self, at, d, n):
        return lax.rem(at + (d % n), n)


def greet(ids):
    bar = pltpu.get_barrier_semaphore()
    for i in ids:
        pl.semaphore_signal(bar, inc=1, device_id=i, device_id_type=MESH)
    pl.semaphore_wait(bar, len(ids))


def push(src, dst, send, recv, to):
    cp = pltpu.make_async_remote_copy(
        src_ref=src, dst_ref=dst, send_sem=send, recv_sem=recv, device_id=to, device_id_type=MESH
    )
    cp.start()
    return cp


def remote_call(kernel, operands, out_shape, out_specs, scratch, cid, name, flops=0):
    return pl.pallas_call(
        kernel,
        out_shape=out_shape,
        in_specs=[pl.BlockSpec(memory_space=pltpu.VMEM)] * len(operands),
        out_specs=out_specs,
        scratch_shapes=scratch,
        compiler_params=pltpu.CompilerParams(collective_id=cid, has_side_effects=True),
        cost_estimate=pl.CostEstimate(flops=flops, bytes_accessed=1 << 20, transcendentals=0),
        name=name,
    )(*operands)


ANY = pl.BlockSpec(memory_space=pl.ANY)
IN_VMEM = pl.BlockSpec(memory_space=pltpu.VMEM)


def panel_kernel(x, out, loc, ss, rs, fs, fr):
    s = Spot()
    n = s.rxn
    me = s.rx * s.cores + s.core
    peers = [{"rx": s.turn(s.rx, d, n)} for d in range(1, n)]
    greet(peers + [s.other])
    keep = pltpu.make_async_copy(x, out.at[me], loc)
    keep.start()
    cps = [push(x, out.at[me], ss.at[d], rs.at[d], to) for d, to in enumerate(peers, 1)]
    fwd = [push(x, out.at[me], fs.at[0], fr.at[0], s.other)]
    for d, cp in enumerate(cps, 1):
        cp.wait_recv()
        at = s.turn(s.rx, -d, n) * s.cores + s.core
        fwd.append(push(out.at[at], out.at[at], fs.at[d], fr.at[d], s.other))
    keep.wait()
    for cp in cps:
        cp.wait_send()
    for cp in fwd:
        cp.wait()


def panel_gather(x):
    n = lax.axis_size("rx")
    shape = (n * lax.axis_size("core"),) + x.shape
    dma = pltpu.SemaphoreType.DMA
    return remote_call(
        panel_kernel, (x,), jax.ShapeDtypeStruct(shape, x.dtype), ANY,
        [dma, dma((n,)), dma((n,)), dma((n,)), dma((n,))], 0, "panels",
    )


def sum_kernel(x, out, half, mine, got, part, zgot, ss0, rs0, ss1, rs1, ss2, rs2, ss3, rs3, ss4, rs4, ss5, rs5):
    s = Spot()
    nc, nz = s.chips, s.cols
    chips = [s.turn(s.chip, d, nc) for d in range(1, nc)]
    cols = [s.turn(s.col, d, nz) for d in range(1, nz)]
    greet([s.other] + [s.id(t) for t in chips] + [{"col": t} for t in cols])
    cp = push(x.at[1 - s.core], half, ss0, rs0, s.other)
    cp.wait()
    mine[...] = x[s.core] + half[...]
    cps = [push(mine.at[t], got.at[d], ss1.at[d], rs1.at[d], s.id(t)) for d, t in enumerate(chips)]
    for cp in cps:
        cp.wait()
    total = mine[s.chip]
    for d in range(nc - 1):
        total = total + got[d]
    part[...] = total
    cps = [push(part.at[t], zgot.at[d], ss2.at[d], rs2.at[d], {"col": t}) for d, t in enumerate(cols)]
    for cp in cps:
        cp.wait()
    total = part[s.col]
    for d in range(nz - 1):
        total = total + zgot[d]
    out[s.core, s.chip, s.col] = total

    def send_z(d, t):
        own = out.at[s.core, s.chip, s.col]
        return push(own, own, ss3.at[d], rs3.at[d], {"col": t})

    def send_xy(z, n):
        own = out.at[s.core, s.chip, z]
        return [push(own, own, ss4.at[n, d], rs4.at[n, d], s.id(t)) for d, t in enumerate(chips)]

    def send_core(c, z, n, m):
        own = out.at[s.core, c, z]
        return push(own, own, ss5.at[n, m], rs5.at[n, m], s.other)

    zc = [send_z(d, t) for d, t in enumerate(cols)]
    xy = [send_xy(s.col, 0)]
    cc = [send_core(s.chip, s.col, 0, 0)]
    for n in range(nz):
        z = s.turn(s.col, -n, nz)
        if n:
            zc[n - 1].wait_recv()
            xy.append(send_xy(z, n))
            cc.append(send_core(s.chip, z, n, 0))
    for n in range(nz):
        for d in range(nc - 1):
            xy[n][d].wait_recv()
            cc.append(send_core(s.turn(s.chip, -(d + 1), nc), s.turn(s.col, -n, nz), n, d + 1))
    for cp in zc + [x for row in xy for x in row]:
        cp.wait_send()
    for cp in cc:
        cp.wait()


def sum_all(x):
    nc, nz = lax.axis_size(("child", "rx")), lax.axis_size("col")
    tail = (x.shape[0] // (2 * nc * nz), x.shape[1])
    full = jax.ShapeDtypeStruct((2, nc, nz) + tail, F32)
    dma = pltpu.SemaphoreType.DMA
    sems = [dma, dma, dma((nc,)), dma((nc,)), dma((nz,)), dma((nz,)), dma((nz,)), dma((nz,)), dma((nz, nc)), dma((nz, nc)), dma((nz, nc)), dma((nz, nc))]
    half, part = (nc, nz) + tail, (nz,) + tail
    vm = [pltpu.VMEM(z, F32) for z in (half, half, (nc - 1,) + part, part, (nz - 1,) + tail)]
    out = remote_call(sum_kernel, (x.reshape(full.shape),), full, IN_VMEM, vm + sems, 1, "total")
    return out.reshape(x.shape)


BASE = 128
WIDE = 8


def base_inverse(a_ref, d_ref, x_ref):
    n, step = a_ref.shape[0], 8
    ids = lax.broadcasted_iota(jnp.int32, (step, n), 0)
    lanes = lax.broadcasted_iota(jnp.int32, (step, n), 1)
    a = [a_ref[i * step : (i + 1) * step, :] for i in range(n // step)]
    x = [(lanes == ids + i * step).astype(F32) for i in range(n // step)]
    for j in range(0, n, WIDE):
        c0 = j // step
        chunks = range(c0, n // step)
        cols = [[jnp.broadcast_to(a[i][:, j + t : j + t + 1], (step, n)) for i in chunks] for t in range(WIDE)]
        at = [j + t - c0 * step for t in range(WIDE)]
        rows = [a[c0][p : p + 1, :] for p in at]
        xrows = [x[c0][p : p + 1, :] for p in at]
        for t in range(WIDE):
            pivot = cols[t][0][at[t] : at[t] + 1, :]
            d_ref[j + t : j + t + 1, :] = pivot
            inv = 1.0 / pivot
            low = [c * inv for c in cols[t]]
            low[0] = jnp.where(ids > at[t], low[0], 0.0)
            for s in range(t + 1, WIDE):
                f = cols[t][0][at[s] : at[s] + 1, :]
                g = f * inv
                cols[s] = [c - l * f for c, l in zip(cols[s], low)]
                rows[s] = rows[s] - g * rows[t]
                xrows[s] = xrows[s] - g * xrows[t]
            for n_, i in enumerate(chunks):
                a[i] = a[i] - low[n_] * rows[t]
                x[i] = x[i] - low[n_] * xrows[t]
    for i in range(n // step):
        x_ref[i * step : (i + 1) * step, :] = x[i] * (1.0 / jnp.sqrt(d_ref[i * step : (i + 1) * step, :]))


def factor_steps(a_in, y, full, a, blk, piv, inv):
    n = a.shape[0]
    high = functools.partial(lax.dot_general, precision=lax.Precision.HIGHEST, preferred_element_type=F32)
    ids = lax.broadcasted_iota(jnp.int32, (n, n), 0)
    a[:TILE, :TILE] = a_in[:TILE, :]
    a[TILE:, :TILE] = a_in[TILE : 2 * TILE, :]
    a[:TILE, TILE:] = a_in[TILE : 2 * TILE, :].T
    a[TILE:, TILE:] = a_in[2 * TILE :, :]
    full[...] = a[...]
    y[...] = (ids == lax.broadcasted_iota(jnp.int32, (n, n), 1)).astype(F32)

    def one(k, carry):
        at = pl.ds(pl.multiple_of(k * BASE, BASE), BASE)
        blk[...] = a[at, at]
        base_inverse(blk, piv, inv)
        low = high(a[:, at], inv[...], NT)
        low = jnp.where(ids[:, :BASE] >= (k + 1) * BASE, low, 0.0)
        yk = high(inv[...], y[at, :], (((1,), (0,)), ((), ())))
        a[...] = a[...] - high(low, low, NT)
        y[...] = y[...] - high(low, yk, (((1,), (0,)), ((), ())))
        y[at, :] = yk
        return carry

    lax.fori_loop(0, n // BASE, one, 0)


def front_kernel(
    place, tab, diag, x, c0, base, *refs
):
    s = Spot()
    nc, nz = s.chips, s.cols
    far = refs[: nc - 1]
    acc, wc, wr = refs[nc - 1 : nc + 2]
    (y, full, a, blk, piv, inv, half_in, mine, got, piece, zbuf, buf, sums,
     load, store, loc, keep_sem, hs, hr, cs, cr, bs, br, es, er, zs, zr, ps, pr, fs, fr, ws, wx, wl) = refs[nc + 2 :]
    half = wr.shape[0]
    n = piece.shape[0] - META
    me = s.chip * s.cores + s.core
    slot = lax.rem(me, half)
    count = nc * s.cores
    chips = [s.turn(s.chip, d, nc) for d in range(1, nc)]
    plane = [s.turn(me, d, count) for d in range(1, count)]
    greet([s.id(t // s.cores, lax.rem(t, s.cores)) for t in plane] + [{"col": s.turn(s.col, d, nz)} for d in range(1, nz)])

    def spot(n):
        return buf.at[pl.ds(n * c0.shape[0], c0.shape[0])]

    pairs = [push(x.at[1 - s.core, t], half_in.at[d], hs.at[d], hr.at[d], s.other) for d, t in enumerate(chips + [s.chip])]
    fetch = pltpu.make_async_copy(base, sums, load)
    fetch.start()
    keep0 = pltpu.make_async_copy(c0, spot(0), keep_sem)
    keep0.start()
    sent = []
    for d, t in enumerate(chips + [s.chip]):
        pairs[d].wait_recv()
        q, meta = encode(decode(x[s.core, t]) + decode(half_in[d]))
        mine[d, :n, :] = q
        mine[d, n:, :] = meta
        if d < nc - 1:
            sent.append(push(mine.at[d], got.at[d], cs.at[d], cr.at[d], s.id(t)))
    bulk = [push(src, spot(d), bs.at[d], br.at[d], s.id(t)) for d, (t, src) in enumerate(zip(chips, far), 1)]
    echo = [push(c0, spot(nc), es.at[0], er.at[0], s.other)]

    factor_steps(diag, y, full, a, blk, piv, inv)

    g = decode(mine[nc - 1])
    for d, cp in enumerate(sent):
        cp.wait_recv()
        g = g + decode(got[d])
    unit = math.gcd(n, TILE)
    rows = []
    for u in range(n // unit):
        first = me * n + u * unit
        z = g[u * unit : (u + 1) * unit, :]
        for k in range(2):
            own = full[pl.ds(pl.multiple_of(k * TILE + lax.rem(first, TILE), unit), unit), :]
            z = jnp.where(s.col * (count * n // TILE) + first // TILE == place[k], own, z)
        rows.append(z)
    g = jnp.concatenate(rows, axis=0)
    w = lax.dot_general(g, y[...], NT, precision=lax.Precision.HIGHEST, preferred_element_type=F32)
    q, meta = encode(w)
    piece[:n, :] = q
    piece[n:, :] = meta
    x = piece

    def hand(src, z, d):
        here = jnp.logical_and(z == s.chip, s.ci == s.core)

        @pl.when(here)
        def _():
            pltpu.make_async_copy(src, wr.at[slot], wl).start()

        @pl.when(jnp.logical_not(here))
        def _():
            push(src, wr.at[slot], ws.at[d], wx.at[slot], s.id(z, s.ci))

    def handed(src, z, d):
        here = jnp.logical_and(z == s.chip, s.ci == s.core)

        @pl.when(here)
        def _():
            pltpu.make_async_copy(src, wr.at[slot], wl).wait()

        @pl.when(jnp.logical_not(here))
        def _():
            pltpu.make_async_remote_copy(
                src_ref=src, dst_ref=wr.at[slot], send_sem=ws.at[d], recv_sem=wx.at[slot],
                device_id=s.id(z, s.ci), device_id_type=MESH,
            ).wait_send()

    def hop(src, z, way, d):
        to = s.col + way

        @pl.when(jnp.logical_and(to >= 0, to < nz))
        def _():
            push(src, zbuf.at[z], zs.at[d], zr.at[z], {"col": to})

    def hopped(src, z, way, d):
        to = s.col + way

        @pl.when(jnp.logical_and(to >= 0, to < nz))
        def _():
            pltpu.make_async_remote_copy(
                src_ref=src, dst_ref=zbuf.at[z], send_sem=zs.at[d], recv_sem=zr.at[z],
                device_id={"col": to}, device_id_type=MESH,
            ).wait_send()

    hop(x, s.col, 1, 0)
    hop(x, s.col, -1, 1)
    hand(x, s.col, 0)
    keep = pltpu.make_async_copy(x, wc.at[me], loc)
    keep.start()
    pc = [push(x, wc.at[me], ps.at[d], pr.at[d], s.id(t)) for d, t in enumerate(chips, 1)]
    fc = [push(x, wc.at[me], fs.at[0], fr.at[0], s.other)]

    def moved(d, way):
        z = s.col - way * d
        n = 2 * d + (way < 0)

        @pl.when(jnp.logical_and(z >= 0, z < nz))
        def _():
            src = zbuf.at[z]
            pltpu.make_async_remote_copy(
                src_ref=src, dst_ref=src, send_sem=zs.at[n], recv_sem=zr.at[z],
                device_id=s.other, device_id_type=MESH,
            ).wait_recv()
            hop(src, z, way, n)
            hand(src, z, n)

    def done(d, way):
        z = s.col - way * d
        n = 2 * d + (way < 0)

        @pl.when(jnp.logical_and(z >= 0, z < nz))
        def _():
            hopped(zbuf.at[z], z, way, n)
            handed(zbuf.at[z], z, n)

    rd, cd = base.shape[0] // TILE, base.shape[1] // TILE
    for d in range(1, nc):
        bulk[d - 1].wait_recv()
        echo.append(push(spot(d), spot(nc + d), es.at[d], er.at[d], s.other))

    def place_rows(i):
        def one(j, carry):
            k = i * cd + j
            at = pl.ds(pl.multiple_of(j * TILE, TILE), TILE)
            z = sums[i * TILE : (i + 1) * TILE, at]
            for c in range(2):
                z = z + jnp.where(tab[2 * c + 1, k] != 0, decode(buf[tab[2 * c, k]]), 0.0)
            sums[i * TILE : (i + 1) * TILE, at] = z
            return carry

        lax.fori_loop(0, cd, one, 0)
        rows = pl.ds(i * TILE, TILE)
        cp = pltpu.make_async_copy(sums.at[rows], acc.at[rows], store.at[i])
        cp.start()
        return cp

    steps = max(nz, nc, 2)
    stores = []
    for d in range(1, steps):
        if d < nz:
            moved(d, 1)
            moved(d, -1)
        if d < nc:
            pc[d - 1].wait_recv()
            at = s.turn(s.chip, -d, nc) * s.cores + s.core
            fc.append(push(wc.at[at], wc.at[at], fs.at[d], fr.at[d], s.other))
        if d == 1:
            fetch.wait()
            keep0.wait()
            for cp in echo:
                cp.wait_recv()
        stores += [place_rows(i) for i in range(rd) if i % (steps - 1) == d - 1]
    hopped(x, s.col, 1, 0)
    hopped(x, s.col, -1, 1)
    handed(x, s.col, 0)
    for d in range(1, nz):
        done(d, 1)
        done(d, -1)
    for j in range(half):

        @pl.when(jnp.logical_or(s.ci != s.core, slot != j))
        def _(j=j):
            pltpu.make_async_remote_copy(
                src_ref=wr.at[j], dst_ref=wr.at[j], send_sem=ws.at[0], recv_sem=wx.at[j],
                device_id=s.other, device_id_type=MESH,
            ).wait_recv()

    keep.wait()
    for cp in stores:
        cp.wait()
    for cp in pairs + sent + bulk + pc + echo:
        cp.wait_send()
    for cp in fc:
        cp.wait()


def front_call(place, t, diag, x, base, coded):
    nc, nz = lax.axis_size(("child", "rx")), lax.axis_size("col")
    n = 2 * TILE
    dma = pltpu.SemaphoreType.DMA
    vm, smem = IN_VMEM, pl.BlockSpec(memory_space=pltpu.SMEM)
    piece, code = x.shape[2:], coded[0].shape
    scratch = [pltpu.VMEM((n, n), F32)] * 3 + [pltpu.VMEM((BASE, BASE), F32)] * 3
    scratch += [pltpu.VMEM((k,) + piece, x.dtype) for k in (nc, nc, nc)]
    scratch += [pltpu.VMEM(piece, x.dtype), pltpu.VMEM((nz,) + piece, x.dtype)]
    scratch += [pltpu.VMEM((2 * nc * code[0],) + code[1:], x.dtype), pltpu.VMEM(base.shape, F32)]
    scratch += [dma, dma((base.shape[0] // TILE,)), dma, dma] + [dma((nc,))] * 8 + [dma((2 * nz,)), dma((nz,))] + [dma((nc,))] * 4
    scratch += [dma((2 * nz,)), dma((nc,)), dma]
    shapes = [(2 * nc,) + piece, (nc,) + piece]
    return pl.pallas_call(
        front_kernel,
        out_shape=[jax.ShapeDtypeStruct(base.shape, F32)] + [jax.ShapeDtypeStruct(k, x.dtype) for k in shapes],
        in_specs=[smem, smem, vm, vm, vm, ANY] + [ANY] * (nc - 1),
        out_specs=[ANY] * 3,
        scratch_shapes=scratch,
        compiler_params=pltpu.CompilerParams(collective_id=3, has_side_effects=True),
        name="front",
    )(place, t, diag, x, coded[0], base, *coded[1:])


def body(child_blocks, child_panels, child_patterns, child_maps, parent_place, parent_front):
    ci = lax.axis_index("child")
    rx = lax.axis_index("rx")
    core = lax.axis_index("core")
    col = lax.axis_index("col")
    cores = lax.axis_size("core")
    rxn = lax.axis_size("rx")
    row = rx * cores + core
    rown = rxn * cores
    chips = lax.axis_size("child") * rxn
    chip = ci * rxn + rx
    group = ci * rown + row
    block = child_blocks[0]
    own = child_panels[0]
    depth = own.shape[1]
    width = block.shape[0]
    td = width // TILE
    blocks = child_maps.shape[1] // td
    rd = parent_front.shape[0] // TILE
    cd = parent_front.shape[1] // TILE
    slots_n = parent_place.shape[0]
    i32 = jnp.int32

    share = cd * TILE // (chips * cores)
    me = chip * cores + core
    pos = jnp.stack([ci, row, col, core, me, col * cd, chip]).astype(i32)

    def tile_at(block, group, pos, maps, place):
        return find(maps, place, pos[0], block, group, td, cd)[0]

    def shift(x, axes, d):
        n = lax.axis_size(axes)
        return lax.ppermute(x, axes, [(k, (k + d) % n) for k in range(n)])

    code = (td, CODED, TILE)
    heads = (pos, child_maps, parent_place)

    def pick(ds, extra):
        def column(z, pos, maps, place):
            d = sum(jnp.where(z == n, d, 0) for n, d in enumerate(ds))
            return 0, tile_at(pos[2], lax.rem(pos[2] + d, blocks), pos, maps, place)

        part = [pl.BlockSpec((TILE, depth), lambda z, pos, maps, place: (tile_at(pos[1], pos[2], pos, maps, place), 0))]
        return tile_call(
            functools.partial(pick_kernel, td, cd, len(ds)), (len(ds),), heads, (block, own) if extra else (block,),
            [pl.BlockSpec((width, TILE), column)] + part * extra,
            [jax.ShapeDtypeStruct(code, jnp.int16)] * len(ds) + [jax.ShapeDtypeStruct((TILE, depth), own.dtype)] * extra,
            [pl.BlockSpec(code, lambda z, *_: (0, 0, 0))] * len(ds)
            + [pl.BlockSpec((TILE, depth), lambda z, *_: (0, 0))] * extra,
            "pick", scratch=[pltpu.VMEM(code, jnp.int16)],
        )

    order = sorted(range(1, blocks), key=lambda d: -min(d, blocks - d))
    (x,) = pick(order[:1], False)
    *rest, part = pick(order[1:], True)
    raw = [None] * blocks
    for d, x in zip(order, [x] + rest):
        raw[d] = shift(x, "col", d)
    raw = raw[1:]

    smem = pl.BlockSpec(memory_space=pltpu.SMEM)
    dims = (td, cd, rd, chips, blocks, cores, rown)
    sizes = [(chips + 3,), (chips, blocks), (8, 4), (7, cd), (5, rd * cd)]
    rowt, fac, diagt, stript, fint = pl.pallas_call(
        functools.partial(plan_kernel, dims),
        in_specs=[smem] * 4, out_specs=[smem] * 5, name="plan",
        out_shape=[jax.ShapeDtypeStruct(z, i32) for z in sizes],
        scratch_shapes=[pltpu.SMEM((2, slots_n), i32)],
    )(pos, child_maps, parent_place, child_patterns)

    partner = panel_gather(part)
    diag_part = tile_call(
        diag_kernel, (3,), (diagt,), (block, parent_front, own, partner),
        [
            pl.BlockSpec((TILE, TILE), lambda k, t: (t[0, k], t[1, k])),
            pl.BlockSpec((TILE, TILE), lambda k, t: (t[2, k], t[3, k])),
            pl.BlockSpec((TILE, depth), lambda k, t: (t[0, k], 0)),
            pl.BlockSpec((1, TILE, depth), lambda k, t: (t[7, k], 0, 0)),
        ],
        jax.ShapeDtypeStruct((3 * TILE, TILE), F32),
        pl.BlockSpec((TILE, TILE), lambda k, t: (k, 0)), "diag",
    )
    diagonal = sum_all(diag_part)
    diagonal, *raw = lax.optimization_barrier((diagonal, *raw))

    row_code = (blocks, CODED, TILE)
    strip_rows, *coded = tile_call(
        update_kernel, (chips,), (rowt, fac, pos), (block, *raw, own, partner),
        [pl.BlockSpec((TILE, TILE), lambda p, r, f, pos: (r[p], r[chips + 2]))]
        + [pl.BlockSpec((1, CODED, TILE), lambda p, r, f, pos: (r[p], 0, 0))] * (blocks - 1) + [
            pl.BlockSpec((TILE, depth), lambda p, r, f, pos: (r[p], 0)),
            pl.BlockSpec((blocks, TILE, depth), lambda p, r, f, pos: (0, 0, 0)),
        ],
        [jax.ShapeDtypeStruct((2, TILE, blocks * TILE), F32)] + [jax.ShapeDtypeStruct(row_code, jnp.int16)] * chips,
        [pl.BlockSpec((2, TILE, blocks * TILE), lambda p, *_: (0, 0, 0))]
        + [pl.BlockSpec(row_code, lambda p, *_: (0, 0, 0))] * chips,
        "update", scratch=[pltpu.VMEM(row_code, jnp.int16), pltpu.VMEM((TILE, blocks * TILE), F32)],
    )
    pieces = (cores, chips, share + META, 2 * TILE)
    strips = tile_call(
        strip_kernel, (1,), (stript,), (strip_rows, parent_front, parent_front),
        [
            pl.BlockSpec(strip_rows.shape, lambda k, t: (0, 0, 0)),
            pl.BlockSpec((TILE, cd * TILE), lambda k, t: (t[0, 0], 0)),
            pl.BlockSpec((TILE, cd * TILE), lambda k, t: (t[0, 1], 0)),
        ],
        jax.ShapeDtypeStruct(pieces, jnp.int16),
        pl.BlockSpec(pieces, lambda k, t: (0, 0, 0, 0)), "strip",
        scratch=[pltpu.VMEM((cd * TILE, 2 * TILE), F32)],
    )
    acc, wc, wr = front_call(parent_place, fint, diagonal, strips, parent_front, coded)

    per = 2
    return tile_call(
        final_kernel, (rd, cd // per), (fint,), (acc, wr, wc),
        [
            pl.BlockSpec((TILE, per * TILE), lambda i, j, t: (i, j)),
            pl.BlockSpec(wr.shape, lambda i, j, t: (0, 0, 0)),
            pl.BlockSpec(wc.shape, lambda i, j, t: (0, 0, 0)),
        ],
        jax.ShapeDtypeStruct(parent_front.shape, F32),
        pl.BlockSpec((TILE, per * TILE), lambda i, j, t: (i, j)), "final",
        scratch=[pltpu.VMEM((n * TILE, 2 * TILE), BF16) for n in (rd, rd, cd, cd)],
    )


def solution(mesh):
    child, row, col = mesh.devices.shape
    cores = child * row // col
    fine = Mesh(mesh.devices.reshape(child, row // cores, cores, col), ("child", "rx", "core", "col"))
    return jax.shard_map(
        body,
        mesh=fine,
        in_specs=(
            P("child", ("rx", "core"), "col"),
            P("child", ("rx", "core"), None),
            P(),
            P(),
            P(),
            P(("child", "rx", "core"), "col"),
        ),
        out_specs=P(("child", "rx", "core"), "col"),
        check_vma=False,
    )
```

```python
import functools
import math

import jax
import jax.numpy as jnp
from jax import lax
from jax.experimental import pallas as pl
from jax.experimental.pallas import tpu as pltpu
from jax.sharding import Mesh, PartitionSpec as P

TILE = 256
F32 = jnp.float32
BF16 = jnp.bfloat16
META = 16
CODED = TILE + META
FULL = 32767.0
NT = (((1,), (1,)), ((), ()))
NN = (((1,), (0,)), ((), ()))


def dot(a, b, dims):
    return lax.dot_general(a, b, dims, preferred_element_type=F32)


def split(x):
    hi = x.astype(BF16)
    return hi, (x - hi.astype(F32)).astype(BF16)


def tile_call(kernel, grid, tables, operands, in_specs, out_shape, out_spec, name, cost=None, scratch=()):
    return pl.pallas_call(
        kernel,
        grid_spec=pltpu.PrefetchScalarGridSpec(
            num_scalar_prefetch=len(tables), grid=grid, in_specs=in_specs, out_specs=out_spec,
            scratch_shapes=list(scratch),
        ),
        out_shape=out_shape,
        name=name,
        cost_estimate=cost,
    )(*tables, *operands)


def powers(k):
    h = jnp.floor(k * 0.5)
    return jnp.exp2(h), jnp.exp2(k - h)


def encode(x):
    top = jnp.maximum(jnp.max(jnp.abs(x), axis=0, keepdims=True), 1e-30)
    k = jnp.ceil(jnp.log2(top) + 1e-3)
    p, r = powers(-k)
    part = jnp.clip(jnp.ceil(top * p * r * FULL), 1.0, FULL)
    q = jnp.floor(x * ((FULL * FULL / part) * p * r) + 0.5).astype(jnp.int32)
    ids = lax.broadcasted_iota(jnp.int32, (META, x.shape[1]), 0)
    meta = jnp.where(ids == 0, k.astype(jnp.int32), jnp.where(ids == 1, part.astype(jnp.int32), 0))
    return q.astype(jnp.int16), meta.astype(jnp.int16)


def decode(code):
    n = code.shape[0] - META
    meta = code[n:, :].astype(jnp.int32).astype(F32)
    p, r = powers(meta[0:1, :])
    return code[:n, :].astype(jnp.int32).astype(F32) * (meta[1:2, :] * (1.0 / (FULL * FULL)) * p * r)


def find(maps, place, child, block, group, td, width):
    at = jnp.int32(0)
    ok = jnp.int32(0)
    for t in range(td):
        hit = place[maps[child, block * td + t]] // width == group
        at = jnp.where(hit, t, at)
        ok = jnp.where(hit, 1, ok)
    return at, ok


def pick_kernel(td, cd, count, pos, maps, place, src, *refs):
    z = pl.program_id(0)
    tmp = refs[-1]
    for r in range(td):
        q, meta = encode(src[r * TILE : (r + 1) * TILE, :])
        tmp[r, :TILE, :] = q
        tmp[r, TILE:, :] = meta
    outs = refs[-1 - count : -1] if len(refs) == count + 1 else refs[1 : 1 + count]
    for d, out in enumerate(outs):

        @pl.when(z == d)
        def _(out=out):
            out[...] = tmp[...]

    if len(refs) > count + 1:
        panel, part = refs[0], refs[-2]

        @pl.when(z == 0)
        def _():
            ok = find(maps, place, pos[0], pos[1], pos[2], td, cd)[1]
            part[...] = jnp.where(ok != 0, panel[...], jnp.zeros_like(panel))


def plan_kernel(dims, pos, maps, place, pat, rowt, fac, diagt, stript, fint, inv):
    td, cd, rd, chips, blocks, cores, rown = dims
    ci, row, col, core = pos[0], pos[1], pos[2], pos[3]
    group = ci * rown + row
    chip = pos[6]
    rxn = chips // 2
    slots_n, tiles_n = place.shape[0], maps.shape[1]

    @pl.loop(0, slots_n)
    def _(k):
        inv[0, k] = -1
        inv[1, k] = -1

    @pl.loop(0, tiles_n)
    def _(k):
        inv[0, place[maps[0, k]]] = k
        inv[1, place[maps[1, k]]] = k

    from_col = [lax.rem(col + blocks - d, blocks) for d in range(blocks)]
    cols = [find(maps, place, ci, b, col, td, cd) for b in from_col]
    for d in range(chips):
        at, ok = find(maps, place, ci, row, lax.rem(chip + d, chips), td, cd)
        rowt[d] = at
        for n, (b, (tile, good)) in enumerate(zip(from_col, cols)):
            fac[d, n] = pat[ci, row * td + at, b * td + tile] * ok * good
    e = (place[0], place[1])
    ie = (inv[ci, e[0]], inv[ci, e[1]])
    le = [jnp.maximum(i, 0) for i in ie]
    own = [((ie[a] >= 0) & (le[a] // td == row)).astype(jnp.int32) for a in range(2)]
    for a in range(2):
        rowt[chips + a] = jnp.where(own[a] != 0, lax.rem(e[a] // cd + chips - chip, chips), -1)
        for b in range(a + 1):
            k = a + b
            live = own[a] * (ie[b] >= 0).astype(jnp.int32) * pat[ci, le[a], le[b]]
            diagt[0, k] = le[a] % td
            diagt[1, k] = le[b] % td
            diagt[2, k] = e[a] % rd
            diagt[3, k] = e[b] % cd
            diagt[4, k] = live * (le[b] // td == col).astype(jnp.int32)
            diagt[5, k] = ((e[a] // rd == group) & (e[b] // cd == col)).astype(jnp.int32)
            diagt[6, k] = live * (e[b] // cd == col).astype(jnp.int32)
            diagt[7, k] = le[b] // td
        stript[0, a] = e[a] % rd

        for q in range(cd):
            slot = col * cd + q
            iq = inv[ci, slot]
            free = ((slot != e[0]) & (slot != e[1])).astype(jnp.int32)
            stript[1 + a, q] = jnp.maximum(iq, 0) // td
            stript[3 + a, q] = own[a] * free * (iq >= 0).astype(jnp.int32)
            stript[5 + a, q] = free * (e[a] // rd == group).astype(jnp.int32)
    for k in range(2, cd):
        stript[0, k] = 0

    @pl.loop(0, rd * cd)
    def _(k):
        slot = col * cd + k % cd
        for c in range(2):
            r, t = inv[c, group * rd + k // cd], inv[c, slot]
            ok = ((r >= 0) & (t >= 0)).astype(jnp.int32)
            source = jnp.maximum(r, 0) // td
            far = (source % cores != core).astype(jnp.int32)
            turn = far * chips + lax.rem(chip + chips - (c * rxn + source // cores), chips)
            fint[2 * c, k] = turn * blocks + jnp.maximum(t, 0) // td
            fint[2 * c + 1, k] = ok
        fint[4, k] = jnp.where(slot == e[0], 1, jnp.where(slot == e[1], 2, 0))


def diag_kernel(t, blk, front, ea, eb, out):
    k = pl.program_id(0)
    x = jnp.where(t[4, k] != 0, blk[...], 0.0) + jnp.where(t[5, k] != 0, front[...], 0.0)
    out[...] = x - jnp.where(t[6, k] != 0, dot(ea[...], eb[0], NT), 0.0)


def column_kernel(pos, maps, place, src, out):
    for r in range(out.shape[0]):
        out[r] = src[r * TILE : (r + 1) * TILE, :]


def strip_kernel(t, upd, f0, f1, out, g):
    cd = t.shape[1]
    some = sum(t[n, q] for n in range(3, 7) for q in range(cd))

    @pl.when(some == 0)
    def _():
        out[...] = jnp.zeros_like(out)

    @pl.when(some != 0)
    def _():
        g[...] = jnp.zeros_like(g)
        for q in range(cd):
            for a, f in enumerate((f0, f1)):

                @pl.when(t[3 + a, q] + t[5 + a, q] != 0)
                def _(q=q, a=a, f=f):
                    at = pl.ds(pl.multiple_of(t[1 + a, q] * TILE, TILE), TILE)
                    x = jnp.where(t[3 + a, q] != 0, upd[a, :, at], 0.0)
                    x = x + jnp.where(t[5 + a, q] != 0, f[:, q * TILE : (q + 1) * TILE], 0.0)
                    g[q * TILE : (q + 1) * TILE, a * TILE : (a + 1) * TILE] = x.T

        n = out.shape[2] - META
        for p in range(out.shape[1]):
            for k in range(out.shape[0]):
                m = p * out.shape[0] + k
                code, meta = encode(g[m * n : (m + 1) * n, :])
                out[k, p, :n, :] = code
                out[k, p, n:, :] = meta


def final_kernel(t, front, wr, wc, out, rows, cols):
    i, j = pl.program_id(0), pl.program_id(1)
    per = out.shape[1] // TILE
    base = (i * pl.num_programs(1) + j) * per
    width = 2 * TILE

    @pl.when(base == 0)
    def _():
        for src, dst, low in ((wr, rows, 2), (wc, cols, 1)):
            n = src.shape[1] - META
            for p in range(src.shape[0]):
                at = pl.ds(p * n, n)
                hi, lo = split(decode(src[p]))
                for m in range(3):
                    dst[at, m * width : (m + 1) * width] = lo if m == low else hi

    ri = pl.ds(pl.multiple_of(i * TILE, TILE), TILE)
    cj = pl.ds(pl.multiple_of(j * TILE * per, TILE), TILE * per)
    out[...] = front[...] - dot(rows[ri, :], cols[cj, :], NT)
    for m in range(per):
        at = slice(m * TILE, (m + 1) * TILE)
        for n in range(2):

            @pl.when(t[4, base + m] == n + 1)
            def _(n=n, at=at):
                hi = rows[ri, n * TILE : (n + 1) * TILE]
                lo = rows[ri, 2 * width + n * TILE : 2 * width + (n + 1) * TILE]
                out[:, at] = hi.astype(F32) + lo.astype(F32)


MESH = pl.DeviceIdType.MESH


class Spot:
    def __init__(self):
        self.ci, self.rx = lax.axis_index("child"), lax.axis_index("rx")
        self.core, self.col = lax.axis_index("core"), lax.axis_index("col")
        self.rxn, self.cores, self.cols = lax.axis_size("rx"), lax.axis_size("core"), lax.axis_size("col")
        self.chips = lax.axis_size("child") * self.rxn
        self.chip = self.ci * self.rxn + self.rx
        self.other = {"core": 1 - self.core}

    def id(self, chip, core=None):
        core = self.core if core is None else core
        return {"child": chip // self.rxn, "rx": lax.rem(chip, self.rxn), "core": core}

    def turn(self, at, d, n):
        return lax.rem(at + (d % n), n)


def greet(ids):
    bar = pltpu.get_barrier_semaphore()
    for i in ids:
        pl.semaphore_signal(bar, inc=1, device_id=i, device_id_type=MESH)
    pl.semaphore_wait(bar, len(ids))


def push(src, dst, send, recv, to):
    cp = pltpu.make_async_remote_copy(
        src_ref=src, dst_ref=dst, send_sem=send, recv_sem=recv, device_id=to, device_id_type=MESH
    )
    cp.start()
    return cp


def remote_call(kernel, operands, out_shape, out_specs, scratch, cid, name, flops=0):
    return pl.pallas_call(
        kernel,
        out_shape=out_shape,
        in_specs=[pl.BlockSpec(memory_space=pltpu.VMEM)] * len(operands),
        out_specs=out_specs,
        scratch_shapes=scratch,
        compiler_params=pltpu.CompilerParams(collective_id=cid, has_side_effects=True),
        cost_estimate=pl.CostEstimate(flops=flops, bytes_accessed=1 << 20, transcendentals=0),
        name=name,
    )(*operands)


ANY = pl.BlockSpec(memory_space=pl.ANY)
IN_VMEM = pl.BlockSpec(memory_space=pltpu.VMEM)


def panel_kernel(x, out, loc, ss, rs, fs, fr):
    s = Spot()
    n = s.rxn
    me = s.rx * s.cores + s.core
    peers = [{"rx": s.turn(s.rx, d, n)} for d in range(1, n)]
    greet(peers + [s.other])
    keep = pltpu.make_async_copy(x, out.at[me], loc)
    keep.start()
    cps = [push(x, out.at[me], ss.at[d], rs.at[d], to) for d, to in enumerate(peers, 1)]
    fwd = [push(x, out.at[me], fs.at[0], fr.at[0], s.other)]
    for d, cp in enumerate(cps, 1):
        cp.wait_recv()
        at = s.turn(s.rx, -d, n) * s.cores + s.core
        fwd.append(push(out.at[at], out.at[at], fs.at[d], fr.at[d], s.other))
    keep.wait()
    for cp in cps:
        cp.wait_send()
    for cp in fwd:
        cp.wait()


def panel_gather(x):
    n = lax.axis_size("rx")
    shape = (n * lax.axis_size("core"),) + x.shape
    dma = pltpu.SemaphoreType.DMA
    return remote_call(
        panel_kernel, (x,), jax.ShapeDtypeStruct(shape, x.dtype), ANY,
        [dma, dma((n,)), dma((n,)), dma((n,)), dma((n,))], 0, "panels",
    )


def sum_kernel(x, part, half, mine, got, ss0, rs0, ss1, rs1):
    s = Spot()
    nc = s.chips
    chips = [s.turn(s.chip, d, nc) for d in range(1, nc)]
    greet([s.other] + [s.id(t) for t in chips])
    cp = push(x.at[1 - s.core], half, ss0, rs0, s.other)
    cp.wait()
    mine[...] = x[s.core] + half[...]
    cps = [push(mine.at[t], got.at[d], ss1.at[d], rs1.at[d], s.id(t)) for d, t in enumerate(chips)]
    for cp in cps:
        cp.wait()
    total = mine[s.chip]
    for d in range(nc - 1):
        total = total + got[d]
    part[...] = total


def sum_plane(x):
    nc, nz = lax.axis_size(("child", "rx")), lax.axis_size("col")
    part = (nz, x.shape[0] // (2 * nc * nz), x.shape[1])
    half = (nc,) + part
    dma = pltpu.SemaphoreType.DMA
    vm = [pltpu.VMEM(z, F32) for z in (half, half, (nc - 1,) + part)]
    return remote_call(
        sum_kernel, (x.reshape((2,) + half),), jax.ShapeDtypeStruct(part, F32), IN_VMEM,
        vm + [dma, dma, dma((nc,)), dma((nc,))], 1, "total"
    )


def update_kernel(rowt, fac, part, own, partner, raw0, *refs):
    s = Spot()
    nc, nz = s.chips, s.cols
    raws = refs[: nz - 1]
    out, strip, coded, zgot, ss2, rs2, ss3, rs3, ss4, rs4, ss5, rs5 = refs[nz - 1 :]
    chips = [s.turn(s.chip, d, nc) for d in range(1, nc)]
    cols = [s.turn(s.col, d, nz) for d in range(1, nz)]

    def one(p, carry):
        r = rowt[p]
        panel = own[r]
        for d in range(nz):
            b = s.turn(s.col, -d, nz)
            at = pl.ds(pl.multiple_of(b * TILE, TILE), TILE)
            u = (decode(raws[d - 1][r]) if d else raw0[r]) - dot(panel, partner[b], NT)
            u = jnp.where(fac[p, d] != 0, u, 0.0)
            for a in range(2):
                strip[a, :, at] = jnp.where(rowt[nc + a] == p, u, strip[a, :, at])
            q, meta = encode(u)
            coded[p, b, :TILE, :] = q
            coded[p, b, TILE:, :] = meta
        return carry

    def work(n):
        lax.fori_loop(nc * n // 4, nc * (n + 1) // 4, one, 0)

    greet([s.other] + [s.id(t) for t in chips] + [{"col": t} for t in cols])
    cps = [push(part.at[t], zgot.at[d], ss2.at[d], rs2.at[d], {"col": t}) for d, t in enumerate(cols)]
    strip[...] = jnp.zeros_like(strip)
    work(0)
    for cp in cps:
        cp.wait()
    total = part[s.col]
    for d in range(nz - 1):
        total = total + zgot[d]
    out[s.core, s.chip, s.col] = total

    def send_z(d, t):
        own = out.at[s.core, s.chip, s.col]
        return push(own, own, ss3.at[d], rs3.at[d], {"col": t})

    def send_xy(z, n):
        own = out.at[s.core, s.chip, z]
        return [push(own, own, ss4.at[n, d], rs4.at[n, d], s.id(t)) for d, t in enumerate(chips)]

    def send_core(c, z, n, m):
        own = out.at[s.core, c, z]
        return push(own, own, ss5.at[n, m], rs5.at[n, m], s.other)

    zc = [send_z(d, t) for d, t in enumerate(cols)]
    xy = [send_xy(s.col, 0)]
    cc = [send_core(s.chip, s.col, 0, 0)]
    work(1)
    for n in range(1, nz):
        z = s.turn(s.col, -n, nz)
        zc[n - 1].wait_recv()
        xy.append(send_xy(z, n))
        cc.append(send_core(s.chip, z, n, 0))
    work(2)
    for n in range(nz):
        for d in range(nc - 1):
            xy[n][d].wait_recv()
            cc.append(send_core(s.turn(s.chip, -(d + 1), nc), s.turn(s.col, -n, nz), n, d + 1))
    work(3)
    for cp in zc + [x for row in xy for x in row]:
        cp.wait_send()
    for cp in cc:
        cp.wait()


def update_call(rowt, fac, part, own, partner, raw):
    nc, nz = lax.axis_size(("child", "rx")), lax.axis_size("col")
    dma, vm, smem = pltpu.SemaphoreType.DMA, IN_VMEM, pl.BlockSpec(memory_space=pltpu.SMEM)
    out, strip, coded = pl.pallas_call(
        update_kernel,
        out_shape=[
            jax.ShapeDtypeStruct((2, nc) + part.shape, F32),
            jax.ShapeDtypeStruct((2, TILE, nz * TILE), F32),
            jax.ShapeDtypeStruct((nc, nz, CODED, TILE), jnp.int16),
        ],
        in_specs=[smem, smem] + [vm] * (3 + nz),
        out_specs=[vm] * 3,
        scratch_shapes=[pltpu.VMEM((nz - 1,) + part.shape[1:], F32)] + [dma((nz,))] * 4 + [dma((nz, nc))] * 4,
        compiler_params=pltpu.CompilerParams(collective_id=2, has_side_effects=True),
        name="update",
    )(rowt, fac, part, own.reshape((-1, TILE) + own.shape[1:]), partner, *raw)
    return out.reshape(-1, TILE), strip, coded


BASE = 128
WIDE = 8


def base_inverse(a_ref, d_ref, x_ref):
    n, step = a_ref.shape[0], 8
    ids = lax.broadcasted_iota(jnp.int32, (step, n), 0)
    lanes = lax.broadcasted_iota(jnp.int32, (step, n), 1)
    a = [a_ref[i * step : (i + 1) * step, :] for i in range(n // step)]
    x = [(lanes == ids + i * step).astype(F32) for i in range(n // step)]
    for j in range(0, n, WIDE):
        c0 = j // step
        chunks = range(c0, n // step)
        cols = [[jnp.broadcast_to(a[i][:, j + t : j + t + 1], (step, n)) for i in chunks] for t in range(WIDE)]
        at = [j + t - c0 * step for t in range(WIDE)]
        rows = [a[c0][p : p + 1, :] for p in at]
        xrows = [x[c0][p : p + 1, :] for p in at]
        for t in range(WIDE):
            pivot = cols[t][0][at[t] : at[t] + 1, :]
            d_ref[j + t : j + t + 1, :] = pivot
            inv = 1.0 / pivot
            low = [c * inv for c in cols[t]]
            low[0] = jnp.where(ids > at[t], low[0], 0.0)
            for s in range(t + 1, WIDE):
                f = cols[t][0][at[s] : at[s] + 1, :]
                g = f * inv
                cols[s] = [c - l * f for c, l in zip(cols[s], low)]
                rows[s] = rows[s] - g * rows[t]
                xrows[s] = xrows[s] - g * xrows[t]
            for n_, i in enumerate(chunks):
                a[i] = a[i] - low[n_] * rows[t]
                x[i] = x[i] - low[n_] * xrows[t]
    for i in range(n // step):
        x_ref[i * step : (i + 1) * step, :] = x[i] * (1.0 / jnp.sqrt(d_ref[i * step : (i + 1) * step, :]))


def factor_steps(a_in, y, full, a, blk, piv, inv):
    n = a.shape[0]
    high = functools.partial(lax.dot_general, precision=lax.Precision.HIGHEST, preferred_element_type=F32)
    ids = lax.broadcasted_iota(jnp.int32, (n, n), 0)
    a[:TILE, :TILE] = a_in[:TILE, :]
    a[TILE:, :TILE] = a_in[TILE : 2 * TILE, :]
    a[:TILE, TILE:] = a_in[TILE : 2 * TILE, :].T
    a[TILE:, TILE:] = a_in[2 * TILE :, :]
    full[...] = a[...]
    y[...] = (ids == lax.broadcasted_iota(jnp.int32, (n, n), 1)).astype(F32)

    def one(k, carry):
        at = pl.ds(pl.multiple_of(k * BASE, BASE), BASE)
        blk[...] = a[at, at]
        base_inverse(blk, piv, inv)
        low = high(a[:, at], inv[...], NT)
        low = jnp.where(ids[:, :BASE] >= (k + 1) * BASE, low, 0.0)
        yk = high(inv[...], y[at, :], (((1,), (0,)), ((), ())))
        a[...] = a[...] - high(low, low, NT)
        y[...] = y[...] - high(low, yk, (((1,), (0,)), ((), ())))
        y[at, :] = yk
        return carry

    lax.fori_loop(0, n // BASE, one, 0)


def front_kernel(
    place, tab, diag, x, coded, base, *refs
):
    s = Spot()
    nc, nz = s.chips, s.cols
    acc, wc, wr = refs[:3]
    c0, far = coded.at[0], [coded.at[d] for d in range(1, nc)]
    blocks = coded.shape[1]
    (y, full, a, blk, piv, inv, half_in, mine, got, piece, zbuf, buf, sums,
     load, store, loc, keep_sem, hs, hr, cs, cr, bs, br, es, er, zs, zr, ps, pr, fs, fr, ws, wx, wl) = refs[3:]
    half = wr.shape[0]
    n = piece.shape[0] - META
    me = s.chip * s.cores + s.core
    slot = lax.rem(me, half)
    count = nc * s.cores
    chips = [s.turn(s.chip, d, nc) for d in range(1, nc)]
    plane = [s.turn(me, d, count) for d in range(1, count)]
    greet([s.id(t // s.cores, lax.rem(t, s.cores)) for t in plane] + [{"col": s.turn(s.col, d, nz)} for d in range(1, nz)])

    def spot(n):
        return buf.at[pl.ds(n * blocks, blocks)]

    pairs = [push(x.at[1 - s.core, t], half_in.at[d], hs.at[d], hr.at[d], s.other) for d, t in enumerate(chips + [s.chip])]
    fetch = pltpu.make_async_copy(base, sums, load)
    fetch.start()
    keep0 = pltpu.make_async_copy(c0, spot(0), keep_sem)
    keep0.start()
    sent = []
    for d, t in enumerate(chips + [s.chip]):
        pairs[d].wait_recv()
        q, meta = encode(decode(x[s.core, t]) + decode(half_in[d]))
        mine[d, :n, :] = q
        mine[d, n:, :] = meta
        if d < nc - 1:
            sent.append(push(mine.at[d], got.at[d], cs.at[d], cr.at[d], s.id(t)))
    bulk = [push(src, spot(d), bs.at[d], br.at[d], s.id(t)) for d, (t, src) in enumerate(zip(chips, far), 1)]
    echo = [push(c0, spot(nc), es.at[0], er.at[0], s.other)]

    factor_steps(diag, y, full, a, blk, piv, inv)

    g = decode(mine[nc - 1])
    for d, cp in enumerate(sent):
        cp.wait_recv()
        g = g + decode(got[d])
    unit = math.gcd(n, TILE)
    rows = []
    for u in range(n // unit):
        first = me * n + u * unit
        z = g[u * unit : (u + 1) * unit, :]
        for k in range(2):
            own = full[pl.ds(pl.multiple_of(k * TILE + lax.rem(first, TILE), unit), unit), :]
            z = jnp.where(s.col * (count * n // TILE) + first // TILE == place[k], own, z)
        rows.append(z)
    g = jnp.concatenate(rows, axis=0)
    w = lax.dot_general(g, y[...], NT, precision=lax.Precision.HIGHEST, preferred_element_type=F32)
    q, meta = encode(w)
    piece[:n, :] = q
    piece[n:, :] = meta
    x = piece

    def hand(src, z, d):
        here = jnp.logical_and(z == s.chip, s.ci == s.core)

        @pl.when(here)
        def _():
            pltpu.make_async_copy(src, wr.at[slot], wl).start()

        @pl.when(jnp.logical_not(here))
        def _():
            push(src, wr.at[slot], ws.at[d], wx.at[slot], s.id(z, s.ci))

    def handed(src, z, d):
        here = jnp.logical_and(z == s.chip, s.ci == s.core)

        @pl.when(here)
        def _():
            pltpu.make_async_copy(src, wr.at[slot], wl).wait()

        @pl.when(jnp.logical_not(here))
        def _():
            pltpu.make_async_remote_copy(
                src_ref=src, dst_ref=wr.at[slot], send_sem=ws.at[d], recv_sem=wx.at[slot],
                device_id=s.id(z, s.ci), device_id_type=MESH,
            ).wait_send()

    def hop(src, z, way, d):
        to = s.col + way

        @pl.when(jnp.logical_and(to >= 0, to < nz))
        def _():
            push(src, zbuf.at[z], zs.at[d], zr.at[z], {"col": to})

    def hopped(src, z, way, d):
        to = s.col + way

        @pl.when(jnp.logical_and(to >= 0, to < nz))
        def _():
            pltpu.make_async_remote_copy(
                src_ref=src, dst_ref=zbuf.at[z], send_sem=zs.at[d], recv_sem=zr.at[z],
                device_id={"col": to}, device_id_type=MESH,
            ).wait_send()

    hop(x, s.col, 1, 0)
    hop(x, s.col, -1, 1)
    hand(x, s.col, 0)
    keep = pltpu.make_async_copy(x, wc.at[me], loc)
    keep.start()
    pc = [push(x, wc.at[me], ps.at[d], pr.at[d], s.id(t)) for d, t in enumerate(chips, 1)]
    fc = [push(x, wc.at[me], fs.at[0], fr.at[0], s.other)]

    def moved(d, way):
        z = s.col - way * d
        n = 2 * d + (way < 0)

        @pl.when(jnp.logical_and(z >= 0, z < nz))
        def _():
            src = zbuf.at[z]
            pltpu.make_async_remote_copy(
                src_ref=src, dst_ref=src, send_sem=zs.at[n], recv_sem=zr.at[z],
                device_id=s.other, device_id_type=MESH,
            ).wait_recv()
            hop(src, z, way, n)
            hand(src, z, n)

    def done(d, way):
        z = s.col - way * d
        n = 2 * d + (way < 0)

        @pl.when(jnp.logical_and(z >= 0, z < nz))
        def _():
            hopped(zbuf.at[z], z, way, n)
            handed(zbuf.at[z], z, n)

    rd, cd = base.shape[0] // TILE, base.shape[1] // TILE
    for d in range(1, nc):
        bulk[d - 1].wait_recv()
        echo.append(push(spot(d), spot(nc + d), es.at[d], er.at[d], s.other))

    def place_rows(i):
        def one(j, carry):
            k = i * cd + j
            at = pl.ds(pl.multiple_of(j * TILE, TILE), TILE)
            z = sums[i * TILE : (i + 1) * TILE, at]
            for c in range(2):
                z = z + jnp.where(tab[2 * c + 1, k] != 0, decode(buf[tab[2 * c, k]]), 0.0)
            sums[i * TILE : (i + 1) * TILE, at] = z
            return carry

        lax.fori_loop(0, cd, one, 0)
        rows = pl.ds(i * TILE, TILE)
        cp = pltpu.make_async_copy(sums.at[rows], acc.at[rows], store.at[i])
        cp.start()
        return cp

    steps = max(nz, nc, 2)
    stores = []
    for d in range(1, steps):
        if d < nz:
            moved(d, 1)
            moved(d, -1)
        if d < nc:
            pc[d - 1].wait_recv()
            at = s.turn(s.chip, -d, nc) * s.cores + s.core
            fc.append(push(wc.at[at], wc.at[at], fs.at[d], fr.at[d], s.other))
        if d == 1:
            fetch.wait()
            keep0.wait()
            for cp in echo:
                cp.wait_recv()
        stores += [place_rows(i) for i in range(rd) if i % (steps - 1) == d - 1]
    hopped(x, s.col, 1, 0)
    hopped(x, s.col, -1, 1)
    handed(x, s.col, 0)
    for d in range(1, nz):
        done(d, 1)
        done(d, -1)
    for j in range(half):

        @pl.when(jnp.logical_or(s.ci != s.core, slot != j))
        def _(j=j):
            pltpu.make_async_remote_copy(
                src_ref=wr.at[j], dst_ref=wr.at[j], send_sem=ws.at[0], recv_sem=wx.at[j],
                device_id=s.other, device_id_type=MESH,
            ).wait_recv()

    keep.wait()
    for cp in stores:
        cp.wait()
    for cp in pairs + sent + bulk + pc + echo:
        cp.wait_send()
    for cp in fc:
        cp.wait()


def front_call(place, t, diag, x, base, coded):
    nc, nz = lax.axis_size(("child", "rx")), lax.axis_size("col")
    n = 2 * TILE
    dma = pltpu.SemaphoreType.DMA
    vm, smem = IN_VMEM, pl.BlockSpec(memory_space=pltpu.SMEM)
    piece, code = x.shape[2:], coded.shape[1:]
    scratch = [pltpu.VMEM((n, n), F32)] * 3 + [pltpu.VMEM((BASE, BASE), F32)] * 3
    scratch += [pltpu.VMEM((k,) + piece, x.dtype) for k in (nc, nc, nc)]
    scratch += [pltpu.VMEM(piece, x.dtype), pltpu.VMEM((nz,) + piece, x.dtype)]
    scratch += [pltpu.VMEM((2 * nc * code[0],) + code[1:], x.dtype), pltpu.VMEM(base.shape, F32)]
    scratch += [dma, dma((base.shape[0] // TILE,)), dma, dma] + [dma((nc,))] * 8 + [dma((2 * nz,)), dma((nz,))] + [dma((nc,))] * 4
    scratch += [dma((2 * nz,)), dma((nc,)), dma]
    shapes = [(2 * nc,) + piece, (nc,) + piece]
    return pl.pallas_call(
        front_kernel,
        out_shape=[jax.ShapeDtypeStruct(base.shape, F32)] + [jax.ShapeDtypeStruct(k, x.dtype) for k in shapes],
        in_specs=[smem, smem, vm, vm, ANY, ANY],
        out_specs=[ANY] * 3,
        scratch_shapes=scratch,
        compiler_params=pltpu.CompilerParams(collective_id=3, has_side_effects=True),
        name="front",
    )(place, t, diag, x, coded, base)


def body(child_blocks, child_panels, child_patterns, child_maps, parent_place, parent_front):
    ci = lax.axis_index("child")
    rx = lax.axis_index("rx")
    core = lax.axis_index("core")
    col = lax.axis_index("col")
    cores = lax.axis_size("core")
    rxn = lax.axis_size("rx")
    row = rx * cores + core
    rown = rxn * cores
    chips = lax.axis_size("child") * rxn
    chip = ci * rxn + rx
    group = ci * rown + row
    block = child_blocks[0]
    own = child_panels[0]
    depth = own.shape[1]
    width = block.shape[0]
    td = width // TILE
    blocks = child_maps.shape[1] // td
    rd = parent_front.shape[0] // TILE
    cd = parent_front.shape[1] // TILE
    slots_n = parent_place.shape[0]
    i32 = jnp.int32

    share = cd * TILE // (chips * cores)
    me = chip * cores + core
    pos = jnp.stack([ci, row, col, core, me, col * cd, chip]).astype(i32)

    def tile_at(block, group, pos, maps, place):
        return find(maps, place, pos[0], block, group, td, cd)[0]

    def shift(x, axes, d):
        n = lax.axis_size(axes)
        return lax.ppermute(x, axes, [(k, (k + d) % n) for k in range(n)])

    code = (td, CODED, TILE)
    heads = (pos, child_maps, parent_place)

    def pick(ds, extra):
        def column(z, pos, maps, place):
            d = sum(jnp.where(z == n, d, 0) for n, d in enumerate(ds))
            return 0, tile_at(pos[2], lax.rem(pos[2] + d, blocks), pos, maps, place)

        part = [pl.BlockSpec((TILE, depth), lambda z, pos, maps, place: (tile_at(pos[1], pos[2], pos, maps, place), 0))]
        return tile_call(
            functools.partial(pick_kernel, td, cd, len(ds)), (len(ds),), heads, (block, own) if extra else (block,),
            [pl.BlockSpec((width, TILE), column)] + part * extra,
            [jax.ShapeDtypeStruct(code, jnp.int16)] * len(ds) + [jax.ShapeDtypeStruct((TILE, depth), own.dtype)] * extra,
            [pl.BlockSpec(code, lambda z, *_: (0, 0, 0))] * len(ds)
            + [pl.BlockSpec((TILE, depth), lambda z, *_: (0, 0))] * extra,
            "pick", scratch=[pltpu.VMEM(code, jnp.int16)],
        )

    order = sorted(range(1, blocks), key=lambda d: -min(d, blocks - d))
    (x,) = pick(order[:1], False)
    *rest, part = pick(order[1:], True)
    raw = [None] * blocks
    for d, x in zip(order, [x] + rest):
        raw[d] = shift(x, "col", d)
    raw[0] = tile_call(
        column_kernel, (1,), heads, (block,),
        [pl.BlockSpec((width, TILE), lambda z, pos, maps, place: (0, tile_at(pos[2], pos[2], pos, maps, place)))],
        jax.ShapeDtypeStruct((td, TILE, TILE), F32), pl.BlockSpec((td, TILE, TILE), lambda z, *_: (0, 0, 0)), "column",
    )

    smem = pl.BlockSpec(memory_space=pltpu.SMEM)
    dims = (td, cd, rd, chips, blocks, cores, rown)
    sizes = [(chips + 2,), (chips, blocks), (8, 4), (7, cd), (5, rd * cd)]
    rowt, fac, diagt, stript, fint = pl.pallas_call(
        functools.partial(plan_kernel, dims),
        in_specs=[smem] * 4, out_specs=[smem] * 5, name="plan",
        out_shape=[jax.ShapeDtypeStruct(z, i32) for z in sizes],
        scratch_shapes=[pltpu.SMEM((2, slots_n), i32)],
    )(pos, child_maps, parent_place, child_patterns)

    partner = panel_gather(part)
    diag_part = tile_call(
        diag_kernel, (3,), (diagt,), (block, parent_front, own, partner),
        [
            pl.BlockSpec((TILE, TILE), lambda k, t: (t[0, k], t[1, k])),
            pl.BlockSpec((TILE, TILE), lambda k, t: (t[2, k], t[3, k])),
            pl.BlockSpec((TILE, depth), lambda k, t: (t[0, k], 0)),
            pl.BlockSpec((1, TILE, depth), lambda k, t: (t[7, k], 0, 0)),
        ],
        jax.ShapeDtypeStruct((3 * TILE, TILE), F32),
        pl.BlockSpec((TILE, TILE), lambda k, t: (k, 0)), "diag",
    )
    diag_part = sum_plane(diag_part)
    diag_part, raw = lax.optimization_barrier((diag_part, raw))
    diagonal, strip_rows, coded = update_call(rowt, fac, diag_part, own, partner, raw)
    pieces = (cores, chips, share + META, 2 * TILE)
    strips = tile_call(
        strip_kernel, (1,), (stript,), (strip_rows, parent_front, parent_front),
        [
            pl.BlockSpec(strip_rows.shape, lambda k, t: (0, 0, 0)),
            pl.BlockSpec((TILE, cd * TILE), lambda k, t: (t[0, 0], 0)),
            pl.BlockSpec((TILE, cd * TILE), lambda k, t: (t[0, 1], 0)),
        ],
        jax.ShapeDtypeStruct(pieces, jnp.int16),
        pl.BlockSpec(pieces, lambda k, t: (0, 0, 0, 0)), "strip",
        scratch=[pltpu.VMEM((cd * TILE, 2 * TILE), F32)],
    )
    acc, wc, wr = front_call(parent_place, fint, diagonal, strips, parent_front, coded)

    per = 2
    return tile_call(
        final_kernel, (rd, cd // per), (fint,), (acc, wr, wc),
        [
            pl.BlockSpec((TILE, per * TILE), lambda i, j, t: (i, j)),
            pl.BlockSpec(wr.shape, lambda i, j, t: (0, 0, 0)),
            pl.BlockSpec(wc.shape, lambda i, j, t: (0, 0, 0)),
        ],
        jax.ShapeDtypeStruct(parent_front.shape, F32),
        pl.BlockSpec((TILE, per * TILE), lambda i, j, t: (i, j)), "final",
        scratch=[pltpu.VMEM((n * TILE, 6 * TILE), BF16) for n in (rd, cd)],
    )


def solution(mesh):
    child, row, col = mesh.devices.shape
    cores = child * row // col
    fine = Mesh(mesh.devices.reshape(child, row // cores, cores, col), ("child", "rx", "core", "col"))
    return jax.shard_map(
        body,
        mesh=fine,
        in_specs=(
            P("child", ("rx", "core"), "col"),
            P("child", ("rx", "core"), None),
            P(),
            P(),
            P(),
            P(("child", "rx", "core"), "col"),
        ),
        out_specs=P(("child", "rx", "core"), "col"),
        check_vma=False,
    )
```

```python
import functools
import math

import jax
import jax.numpy as jnp
from jax import lax
from jax.experimental import pallas as pl
from jax.experimental.pallas import tpu as pltpu
from jax.sharding import Mesh, PartitionSpec as P

TILE = 256
F32 = jnp.float32
BF16 = jnp.bfloat16
META = 16
CODED = TILE + META
FULL = 32767.0
NT = (((1,), (1,)), ((), ()))
NN = (((1,), (0,)), ((), ()))


def dot(a, b, dims):
    return lax.dot_general(a, b, dims, preferred_element_type=F32)


def split(x):
    hi = x.astype(BF16)
    return hi, (x - hi.astype(F32)).astype(BF16)


def tile_call(kernel, grid, tables, operands, in_specs, out_shape, out_spec, name, cost=None, scratch=()):
    return pl.pallas_call(
        kernel,
        grid_spec=pltpu.PrefetchScalarGridSpec(
            num_scalar_prefetch=len(tables), grid=grid, in_specs=in_specs, out_specs=out_spec,
            scratch_shapes=list(scratch),
        ),
        out_shape=out_shape,
        name=name,
        cost_estimate=cost,
    )(*tables, *operands)


def powers(k):
    h = jnp.floor(k * 0.5)
    return jnp.exp2(h), jnp.exp2(k - h)


def encode(x):
    top = jnp.maximum(jnp.max(jnp.abs(x), axis=0, keepdims=True), 1e-30)
    k = jnp.ceil(jnp.log2(top) + 1e-3)
    p, r = powers(-k)
    part = jnp.clip(jnp.ceil(top * p * r * FULL), 1.0, FULL)
    q = jnp.floor(x * ((FULL * FULL / part) * p * r) + 0.5).astype(jnp.int32)
    ids = lax.broadcasted_iota(jnp.int32, (META, x.shape[1]), 0)
    meta = jnp.where(ids == 0, k.astype(jnp.int32), jnp.where(ids == 1, part.astype(jnp.int32), 0))
    return q.astype(jnp.int16), meta.astype(jnp.int16)


def decode(code):
    n = code.shape[0] - META
    meta = code[n:, :].astype(jnp.int32).astype(F32)
    p, r = powers(meta[0:1, :])
    return code[:n, :].astype(jnp.int32).astype(F32) * (meta[1:2, :] * (1.0 / (FULL * FULL)) * p * r)


def find(maps, place, child, block, group, td, width):
    at = jnp.int32(0)
    ok = jnp.int32(0)
    for t in range(td):
        hit = place[maps[child, block * td + t]] // width == group
        at = jnp.where(hit, t, at)
        ok = jnp.where(hit, 1, ok)
    return at, ok


def pick_kernel(td, cd, count, pos, maps, place, src, *refs):
    z = pl.program_id(0)
    tmp = refs[-1]
    for r in range(td):
        q, meta = encode(src[r * TILE : (r + 1) * TILE, :])
        tmp[r, :TILE, :] = q
        tmp[r, TILE:, :] = meta
    outs = refs[-1 - count : -1] if len(refs) == count + 1 else refs[1 : 1 + count]
    for d, out in enumerate(outs):

        @pl.when(z == d)
        def _(out=out):
            out[...] = tmp[...]

    if len(refs) > count + 1:
        panel, part = refs[0], refs[-2]

        @pl.when(z == 0)
        def _():
            ok = find(maps, place, pos[0], pos[1], pos[2], td, cd)[1]
            part[...] = jnp.where(ok != 0, panel[...], jnp.zeros_like(panel))


def plan_kernel(dims, pos, maps, place, pat, rowt, fac, diagt, stript, fint, inv):
    td, cd, rd, chips, blocks, cores, rown = dims
    ci, row, col, core = pos[0], pos[1], pos[2], pos[3]
    group = ci * rown + row
    chip = pos[6]
    rxn = chips // 2
    slots_n, tiles_n = place.shape[0], maps.shape[1]

    @pl.loop(0, slots_n)
    def _(k):
        inv[0, k] = -1
        inv[1, k] = -1

    @pl.loop(0, tiles_n)
    def _(k):
        inv[0, place[maps[0, k]]] = k
        inv[1, place[maps[1, k]]] = k

    from_col = [lax.rem(col + blocks - d, blocks) for d in range(blocks)]
    cols = [find(maps, place, ci, b, col, td, cd) for b in from_col]
    for d in range(chips):
        at, ok = find(maps, place, ci, row, lax.rem(chip + d, chips), td, cd)
        rowt[d] = at
        for n, (b, (tile, good)) in enumerate(zip(from_col, cols)):
            fac[d, n] = pat[ci, row * td + at, b * td + tile] * ok * good
    e = (place[0], place[1])
    ie = (inv[ci, e[0]], inv[ci, e[1]])
    le = [jnp.maximum(i, 0) for i in ie]
    own = [((ie[a] >= 0) & (le[a] // td == row)).astype(jnp.int32) for a in range(2)]
    for a in range(2):
        rowt[chips + a] = jnp.where(own[a] != 0, lax.rem(e[a] // cd + chips - chip, chips), -1)
        for b in range(a + 1):
            k = a + b
            live = own[a] * (ie[b] >= 0).astype(jnp.int32) * pat[ci, le[a], le[b]]
            diagt[0, k] = le[a] % td
            diagt[1, k] = le[b] % td
            diagt[2, k] = e[a] % rd
            diagt[3, k] = e[b] % cd
            diagt[4, k] = live * (le[b] // td == col).astype(jnp.int32)
            diagt[5, k] = ((e[a] // rd == group) & (e[b] // cd == col)).astype(jnp.int32)
            diagt[6, k] = live * (e[b] // cd == col).astype(jnp.int32)
            diagt[7, k] = le[b] // td
        stript[0, a] = e[a] % rd

        for q in range(cd):
            slot = col * cd + q
            iq = inv[ci, slot]
            free = ((slot != e[0]) & (slot != e[1])).astype(jnp.int32)
            stript[1 + a, q] = jnp.maximum(iq, 0) // td
            stript[3 + a, q] = own[a] * free * (iq >= 0).astype(jnp.int32)
            stript[5 + a, q] = free * (e[a] // rd == group).astype(jnp.int32)
    for k in range(2, cd):
        stript[0, k] = 0

    @pl.loop(0, rd * cd)
    def _(k):
        slot = col * cd + k % cd
        for c in range(2):
            r, t = inv[c, group * rd + k // cd], inv[c, slot]
            ok = ((r >= 0) & (t >= 0)).astype(jnp.int32)
            source = jnp.maximum(r, 0) // td
            far = (source % cores != core).astype(jnp.int32)
            turn = far * chips + lax.rem(chip + chips - (c * rxn + source // cores), chips)
            fint[2 * c, k] = turn * blocks + jnp.maximum(t, 0) // td
            fint[2 * c + 1, k] = ok
        fint[4, k] = jnp.where(slot == e[0], 1, jnp.where(slot == e[1], 2, 0))


def diag_kernel(t, blk, front, ea, eb, out):
    k = pl.program_id(0)
    x = jnp.where(t[4, k] != 0, blk[...], 0.0) + jnp.where(t[5, k] != 0, front[...], 0.0)
    out[...] = x - jnp.where(t[6, k] != 0, dot(ea[...], eb[0], NT), 0.0)


def column_kernel(pos, maps, place, src, out):
    for r in range(out.shape[0]):
        out[r] = src[r * TILE : (r + 1) * TILE, :]


def strip_kernel(t, upd, f0, f1, out, g):
    cd = t.shape[1]
    some = sum(t[n, q] for n in range(3, 7) for q in range(cd))

    @pl.when(some == 0)
    def _():
        out[...] = jnp.zeros_like(out)

    @pl.when(some != 0)
    def _():
        g[...] = jnp.zeros_like(g)
        for q in range(cd):
            for a, f in enumerate((f0, f1)):

                @pl.when(t[3 + a, q] + t[5 + a, q] != 0)
                def _(q=q, a=a, f=f):
                    at = pl.ds(pl.multiple_of(t[1 + a, q] * TILE, TILE), TILE)
                    x = jnp.where(t[3 + a, q] != 0, upd[a, :, at], 0.0)
                    x = x + jnp.where(t[5 + a, q] != 0, f[:, q * TILE : (q + 1) * TILE], 0.0)
                    g[q * TILE : (q + 1) * TILE, a * TILE : (a + 1) * TILE] = x.T

        n = out.shape[2] - META
        for p in range(out.shape[1]):
            for k in range(out.shape[0]):
                m = p * out.shape[0] + k
                code, meta = encode(g[m * n : (m + 1) * n, :])
                out[k, p, :n, :] = code
                out[k, p, n:, :] = meta


def final_kernel(t, front, wr, wc, out, rows, cols):
    i, j = pl.program_id(0), pl.program_id(1)
    per = out.shape[1] // TILE
    base = (i * pl.num_programs(1) + j) * per
    width = 2 * TILE

    @pl.when(base == 0)
    def _():
        for src, dst, low in ((wr, rows, 2), (wc, cols, 1)):
            n = src.shape[1] - META
            for p in range(src.shape[0]):
                at = pl.ds(p * n, n)
                hi, lo = split(decode(src[p]))
                for m in range(3):
                    dst[at, m * width : (m + 1) * width] = lo if m == low else hi

    ri = pl.ds(pl.multiple_of(i * TILE, TILE), TILE)
    cj = pl.ds(pl.multiple_of(j * TILE * per, TILE), TILE * per)
    out[...] = front[...] - dot(rows[ri, :], cols[cj, :], NT)
    for m in range(per):
        at = slice(m * TILE, (m + 1) * TILE)
        for n in range(2):

            @pl.when(t[4, base + m] == n + 1)
            def _(n=n, at=at):
                hi = rows[ri, n * TILE : (n + 1) * TILE]
                lo = rows[ri, 2 * width + n * TILE : 2 * width + (n + 1) * TILE]
                out[:, at] = hi.astype(F32) + lo.astype(F32)


MESH = pl.DeviceIdType.MESH


class Spot:
    def __init__(self):
        self.ci, self.rx = lax.axis_index("child"), lax.axis_index("rx")
        self.core, self.col = lax.axis_index("core"), lax.axis_index("col")
        self.rxn, self.cores, self.cols = lax.axis_size("rx"), lax.axis_size("core"), lax.axis_size("col")
        self.chips = lax.axis_size("child") * self.rxn
        self.chip = self.ci * self.rxn + self.rx
        self.other = {"core": 1 - self.core}

    def id(self, chip, core=None):
        core = self.core if core is None else core
        return {"child": chip // self.rxn, "rx": lax.rem(chip, self.rxn), "core": core}

    def turn(self, at, d, n):
        return lax.rem(at + (d % n), n)


def greet(ids):
    bar = pltpu.get_barrier_semaphore()
    for i in ids:
        pl.semaphore_signal(bar, inc=1, device_id=i, device_id_type=MESH)
    pl.semaphore_wait(bar, len(ids))


def push(src, dst, send, recv, to):
    cp = pltpu.make_async_remote_copy(
        src_ref=src, dst_ref=dst, send_sem=send, recv_sem=recv, device_id=to, device_id_type=MESH
    )
    cp.start()
    return cp


def remote_call(kernel, operands, out_shape, out_specs, scratch, cid, name, flops=0):
    return pl.pallas_call(
        kernel,
        out_shape=out_shape,
        in_specs=[pl.BlockSpec(memory_space=pltpu.VMEM)] * len(operands),
        out_specs=out_specs,
        scratch_shapes=scratch,
        compiler_params=pltpu.CompilerParams(collective_id=cid, has_side_effects=True),
        cost_estimate=pl.CostEstimate(flops=flops, bytes_accessed=1 << 20, transcendentals=0),
        name=name,
    )(*operands)


ANY = pl.BlockSpec(memory_space=pl.ANY)
IN_VMEM = pl.BlockSpec(memory_space=pltpu.VMEM)


def panel_kernel(x, out, loc, ss, rs, fs, fr):
    s = Spot()
    n = s.rxn
    me = s.rx * s.cores + s.core
    peers = [{"rx": s.turn(s.rx, d, n)} for d in range(1, n)]
    greet(peers + [s.other])
    keep = pltpu.make_async_copy(x, out.at[me], loc)
    keep.start()
    cps = [push(x, out.at[me], ss.at[d], rs.at[d], to) for d, to in enumerate(peers, 1)]
    fwd = [push(x, out.at[me], fs.at[0], fr.at[0], s.other)]
    for d, cp in enumerate(cps, 1):
        cp.wait_recv()
        at = s.turn(s.rx, -d, n) * s.cores + s.core
        fwd.append(push(out.at[at], out.at[at], fs.at[d], fr.at[d], s.other))
    keep.wait()
    for cp in cps:
        cp.wait_send()
    for cp in fwd:
        cp.wait()


def panel_gather(x):
    n = lax.axis_size("rx")
    shape = (n * lax.axis_size("core"),) + x.shape
    dma = pltpu.SemaphoreType.DMA
    return remote_call(
        panel_kernel, (x,), jax.ShapeDtypeStruct(shape, x.dtype), ANY,
        [dma, dma((n,)), dma((n,)), dma((n,)), dma((n,))], 0, "panels",
    )


def sum_kernel(x, part, half, mine, got, ss0, rs0, ss1, rs1):
    s = Spot()
    nc = s.chips
    chips = [s.turn(s.chip, d, nc) for d in range(1, nc)]
    greet([s.other] + [s.id(t) for t in chips])
    cp = push(x.at[1 - s.core], half, ss0, rs0, s.other)
    cp.wait()
    mine[...] = x[s.core] + half[...]
    cps = [push(mine.at[t], got.at[d], ss1.at[d], rs1.at[d], s.id(t)) for d, t in enumerate(chips)]
    for cp in cps:
        cp.wait()
    total = mine[s.chip]
    for d in range(nc - 1):
        total = total + got[d]
    part[...] = total


def sum_plane(x):
    nc, nz = lax.axis_size(("child", "rx")), lax.axis_size("col")
    part = (nz, x.shape[0] // (2 * nc * nz), x.shape[1])
    half = (nc,) + part
    dma = pltpu.SemaphoreType.DMA
    vm = [pltpu.VMEM(z, F32) for z in (half, half, (nc - 1,) + part)]
    return remote_call(
        sum_kernel, (x.reshape((2,) + half),), jax.ShapeDtypeStruct(part, F32), IN_VMEM,
        vm + [dma, dma, dma((nc,)), dma((nc,))], 1, "total"
    )


def update_kernel(rowt, fac, part, own, partner, raw0, *refs):
    s = Spot()
    nc, nz = s.chips, s.cols
    raws = refs[: nz - 1]
    out, strip, coded, zgot, ss2, rs2, ss3, rs3, ss4, rs4, ss5, rs5 = refs[nz - 1 :]
    chips = [s.turn(s.chip, d, nc) for d in range(1, nc)]
    cols = [s.turn(s.col, d, nz) for d in range(1, nz)]

    def one(p, carry):
        r = rowt[p]
        panel = own[r]
        for d in range(nz):
            b = s.turn(s.col, -d, nz)
            at = pl.ds(pl.multiple_of(b * TILE, TILE), TILE)
            u = (decode(raws[d - 1][r]) if d else raw0[r]) - dot(panel, partner[b], NT)
            u = jnp.where(fac[p, d] != 0, u, 0.0)
            for a in range(2):
                strip[a, :, at] = jnp.where(rowt[nc + a] == p, u, strip[a, :, at])
            q, meta = encode(u)
            coded[p, b, :TILE, :] = q
            coded[p, b, TILE:, :] = meta
        return carry

    def work(n):
        lax.fori_loop(nc * n // 4, nc * (n + 1) // 4, one, 0)

    greet([s.other] + [s.id(t) for t in chips] + [{"col": t} for t in cols])
    cps = [push(part.at[t], zgot.at[d], ss2.at[d], rs2.at[d], {"col": t}) for d, t in enumerate(cols)]
    strip[...] = jnp.zeros_like(strip)
    work(0)
    for cp in cps:
        cp.wait()
    total = part[s.col]
    for d in range(nz - 1):
        total = total + zgot[d]
    out[s.core, s.chip, s.col] = total

    def send_z(d, t):
        own = out.at[s.core, s.chip, s.col]
        return push(own, own, ss3.at[d], rs3.at[d], {"col": t})

    def send_xy(z, n):
        own = out.at[s.core, s.chip, z]
        return [push(own, own, ss4.at[n, d], rs4.at[n, d], s.id(t)) for d, t in enumerate(chips)]

    def send_core(c, z, n, m):
        own = out.at[s.core, c, z]
        return push(own, own, ss5.at[n, m], rs5.at[n, m], s.other)

    zc = [send_z(d, t) for d, t in enumerate(cols)]
    xy = [send_xy(s.col, 0)]
    cc = [send_core(s.chip, s.col, 0, 0)]
    work(1)
    for n in range(1, nz):
        z = s.turn(s.col, -n, nz)
        zc[n - 1].wait_recv()
        xy.append(send_xy(z, n))
        cc.append(send_core(s.chip, z, n, 0))
    work(2)
    for n in range(nz):
        for d in range(nc - 1):
            xy[n][d].wait_recv()
            cc.append(send_core(s.turn(s.chip, -(d + 1), nc), s.turn(s.col, -n, nz), n, d + 1))
    work(3)
    for cp in zc + [x for row in xy for x in row]:
        cp.wait_send()
    for cp in cc:
        cp.wait()


def update_call(rowt, fac, part, own, partner, raw):
    nc, nz = lax.axis_size(("child", "rx")), lax.axis_size("col")
    dma, vm, smem = pltpu.SemaphoreType.DMA, IN_VMEM, pl.BlockSpec(memory_space=pltpu.SMEM)
    out, strip, coded = pl.pallas_call(
        update_kernel,
        out_shape=[
            jax.ShapeDtypeStruct((2, nc) + part.shape, F32),
            jax.ShapeDtypeStruct((2, TILE, nz * TILE), F32),
            jax.ShapeDtypeStruct((nc, nz, CODED, TILE), jnp.int16),
        ],
        in_specs=[smem, smem] + [vm] * (3 + nz),
        out_specs=[vm] * 3,
        scratch_shapes=[pltpu.VMEM((nz - 1,) + part.shape[1:], F32)] + [dma((nz,))] * 4 + [dma((nz, nc))] * 4,
        compiler_params=pltpu.CompilerParams(collective_id=2, has_side_effects=True),
        name="update",
    )(rowt, fac, part, own.reshape((-1, TILE) + own.shape[1:]), partner, *raw)
    return out.reshape(-1, TILE), strip, coded


BASE = 128
WIDE = 8


def base_inverse(a_ref, d_ref, x_ref):
    n, step = a_ref.shape[0], 8
    ids = lax.broadcasted_iota(jnp.int32, (step, n), 0)
    lanes = lax.broadcasted_iota(jnp.int32, (step, n), 1)
    a = [a_ref[i * step : (i + 1) * step, :] for i in range(n // step)]
    x = [(lanes == ids + i * step).astype(F32) for i in range(n // step)]
    for j in range(0, n, WIDE):
        c0 = j // step
        chunks = range(c0, n // step)
        cols = [[jnp.broadcast_to(a[i][:, j + t : j + t + 1], (step, n)) for i in chunks] for t in range(WIDE)]
        at = [j + t - c0 * step for t in range(WIDE)]
        rows = [a[c0][p : p + 1, :] for p in at]
        xrows = [x[c0][p : p + 1, :] for p in at]
        for t in range(WIDE):
            pivot = cols[t][0][at[t] : at[t] + 1, :]
            d_ref[j + t : j + t + 1, :] = pivot
            inv = 1.0 / pivot
            low = [c * inv for c in cols[t]]
            low[0] = jnp.where(ids > at[t], low[0], 0.0)
            for s in range(t + 1, WIDE):
                f = cols[t][0][at[s] : at[s] + 1, :]
                g = f * inv
                cols[s] = [c - l * f for c, l in zip(cols[s], low)]
                rows[s] = rows[s] - g * rows[t]
                xrows[s] = xrows[s] - g * xrows[t]
            for n_, i in enumerate(chunks):
                a[i] = a[i] - low[n_] * rows[t]
                x[i] = x[i] - low[n_] * xrows[t]
    for i in range(n // step):
        x_ref[i * step : (i + 1) * step, :] = x[i] * (1.0 / jnp.sqrt(d_ref[i * step : (i + 1) * step, :]))


def factor_steps(a_in, y, full, a, blk, piv, inv):
    n = a.shape[0]
    high = functools.partial(lax.dot_general, precision=lax.Precision.HIGHEST, preferred_element_type=F32)
    ids = lax.broadcasted_iota(jnp.int32, (n, n), 0)
    a[:TILE, :TILE] = a_in[:TILE, :]
    a[TILE:, :TILE] = a_in[TILE : 2 * TILE, :]
    a[:TILE, TILE:] = a_in[TILE : 2 * TILE, :].T
    a[TILE:, TILE:] = a_in[2 * TILE :, :]
    full[...] = a[...]
    y[...] = (ids == lax.broadcasted_iota(jnp.int32, (n, n), 1)).astype(F32)

    for k in range(0, n, BASE):
        at, end = slice(k, k + BASE), k + BASE
        blk[...] = a[at, at]
        base_inverse(blk, piv, inv)
        yk = high(inv[...], y[at, :end], NN)
        y[at, :end] = yk
        if end < n:
            low = high(a[end:, at], inv[...], NT)
            a[end:, end:] = a[end:, end:] - high(low, low, NT)
            y[end:, :end] = y[end:, :end] - high(low, yk, NN)


def front_kernel(
    place, tab, diag, x, coded, base, *refs
):
    s = Spot()
    nc, nz = s.chips, s.cols
    acc, wc, wr = refs[:3]
    c0, far = coded.at[0], [coded.at[d] for d in range(1, nc)]
    blocks = coded.shape[1]
    (y, full, a, blk, piv, inv, half_in, mine, got, piece, zbuf, buf, sums,
     load, store, loc, keep_sem, hs, hr, cs, cr, bs, br, es, er, zs, zr, ps, pr, fs, fr, ws, wx, wl) = refs[3:]
    half = wr.shape[0]
    n = piece.shape[0] - META
    me = s.chip * s.cores + s.core
    slot = lax.rem(me, half)
    count = nc * s.cores
    chips = [s.turn(s.chip, d, nc) for d in range(1, nc)]
    plane = [s.turn(me, d, count) for d in range(1, count)]
    greet([s.id(t // s.cores, lax.rem(t, s.cores)) for t in plane] + [{"col": s.turn(s.col, d, nz)} for d in range(1, nz)])

    def spot(n):
        return buf.at[pl.ds(n * blocks, blocks)]

    pairs = [push(x.at[1 - s.core, t], half_in.at[d], hs.at[d], hr.at[d], s.other) for d, t in enumerate(chips + [s.chip])]
    fetch = pltpu.make_async_copy(base, sums, load)
    fetch.start()
    keep0 = pltpu.make_async_copy(c0, spot(0), keep_sem)
    keep0.start()

    def send_bulk(d):
        return push(far[d - 1], spot(d), bs.at[d], br.at[d], s.id(chips[d - 1]))

    bulk = [send_bulk(1)]
    sent = []
    for d, t in enumerate(chips + [s.chip]):
        pairs[d].wait_recv()
        q, meta = encode(decode(x[s.core, t]) + decode(half_in[d]))
        mine[d, :n, :] = q
        mine[d, n:, :] = meta
        if d < nc - 1:
            sent.append(push(mine.at[d], got.at[d], cs.at[d], cr.at[d], s.id(t)))
    bulk += [send_bulk(d) for d in range(2, nc)]
    echo = [push(c0, spot(nc), es.at[0], er.at[0], s.other)]

    factor_steps(diag, y, full, a, blk, piv, inv)

    g = decode(mine[nc - 1])
    for d, cp in enumerate(sent):
        cp.wait_recv()
        g = g + decode(got[d])
    unit = math.gcd(n, TILE)
    rows = []
    for u in range(n // unit):
        first = me * n + u * unit
        z = g[u * unit : (u + 1) * unit, :]
        for k in range(2):
            own = full[pl.ds(pl.multiple_of(k * TILE + lax.rem(first, TILE), unit), unit), :]
            z = jnp.where(s.col * (count * n // TILE) + first // TILE == place[k], own, z)
        rows.append(z)
    g = jnp.concatenate(rows, axis=0)
    w = lax.dot_general(g, y[...], NT, precision=lax.Precision.HIGHEST, preferred_element_type=F32)
    q, meta = encode(w)
    piece[:n, :] = q
    piece[n:, :] = meta
    x = piece

    def hand(src, z, d):
        here = jnp.logical_and(z == s.chip, s.ci == s.core)

        @pl.when(here)
        def _():
            pltpu.make_async_copy(src, wr.at[slot], wl).start()

        @pl.when(jnp.logical_not(here))
        def _():
            push(src, wr.at[slot], ws.at[d], wx.at[slot], s.id(z, s.ci))

    def handed(src, z, d):
        here = jnp.logical_and(z == s.chip, s.ci == s.core)

        @pl.when(here)
        def _():
            pltpu.make_async_copy(src, wr.at[slot], wl).wait()

        @pl.when(jnp.logical_not(here))
        def _():
            pltpu.make_async_remote_copy(
                src_ref=src, dst_ref=wr.at[slot], send_sem=ws.at[d], recv_sem=wx.at[slot],
                device_id=s.id(z, s.ci), device_id_type=MESH,
            ).wait_send()

    def hop(src, z, way, d):
        to = s.col + way

        @pl.when(jnp.logical_and(to >= 0, to < nz))
        def _():
            push(src, zbuf.at[z], zs.at[d], zr.at[z], {"col": to})

    def hopped(src, z, way, d):
        to = s.col + way

        @pl.when(jnp.logical_and(to >= 0, to < nz))
        def _():
            pltpu.make_async_remote_copy(
                src_ref=src, dst_ref=zbuf.at[z], send_sem=zs.at[d], recv_sem=zr.at[z],
                device_id={"col": to}, device_id_type=MESH,
            ).wait_send()

    hop(x, s.col, 1, 0)
    hop(x, s.col, -1, 1)
    hand(x, s.col, 0)
    keep = pltpu.make_async_copy(x, wc.at[me], loc)
    keep.start()
    pc = [push(x, wc.at[me], ps.at[d], pr.at[d], s.id(t)) for d, t in enumerate(chips, 1)]
    fc = [push(x, wc.at[me], fs.at[0], fr.at[0], s.other)]

    def moved(d, way):
        z = s.col - way * d
        n = 2 * d + (way < 0)

        @pl.when(jnp.logical_and(z >= 0, z < nz))
        def _():
            src = zbuf.at[z]
            pltpu.make_async_remote_copy(
                src_ref=src, dst_ref=src, send_sem=zs.at[n], recv_sem=zr.at[z],
                device_id=s.other, device_id_type=MESH,
            ).wait_recv()
            hop(src, z, way, n)
            hand(src, z, n)

    def done(d, way):
        z = s.col - way * d
        n = 2 * d + (way < 0)

        @pl.when(jnp.logical_and(z >= 0, z < nz))
        def _():
            hopped(zbuf.at[z], z, way, n)
            handed(zbuf.at[z], z, n)

    rd, cd = base.shape[0] // TILE, base.shape[1] // TILE
    for d in range(1, nc):
        bulk[d - 1].wait_recv()
        echo.append(push(spot(d), spot(nc + d), es.at[d], er.at[d], s.other))

    def place_rows(i):
        def one(j, carry):
            k = i * cd + j
            at = pl.ds(pl.multiple_of(j * TILE, TILE), TILE)
            z = sums[i * TILE : (i + 1) * TILE, at]
            for c in range(2):
                z = z + jnp.where(tab[2 * c + 1, k] != 0, decode(buf[tab[2 * c, k]]), 0.0)
            sums[i * TILE : (i + 1) * TILE, at] = z
            return carry

        lax.fori_loop(0, cd, one, 0)
        rows = pl.ds(i * TILE, TILE)
        cp = pltpu.make_async_copy(sums.at[rows], acc.at[rows], store.at[i])
        cp.start()
        return cp

    steps = max(nz, nc, 2)
    stores = []
    for d in range(1, steps):
        if d < nz:
            moved(d, 1)
            moved(d, -1)
        if d < nc:
            pc[d - 1].wait_recv()
            at = s.turn(s.chip, -d, nc) * s.cores + s.core
            fc.append(push(wc.at[at], wc.at[at], fs.at[d], fr.at[d], s.other))
        if d == 1:
            fetch.wait()
            keep0.wait()
            for cp in echo:
                cp.wait_recv()
        stores += [place_rows(i) for i in range(rd) if i % (steps - 1) == d - 1]
    hopped(x, s.col, 1, 0)
    hopped(x, s.col, -1, 1)
    handed(x, s.col, 0)
    for d in range(1, nz):
        done(d, 1)
        done(d, -1)
    for j in range(half):

        @pl.when(jnp.logical_or(s.ci != s.core, slot != j))
        def _(j=j):
            pltpu.make_async_remote_copy(
                src_ref=wr.at[j], dst_ref=wr.at[j], send_sem=ws.at[0], recv_sem=wx.at[j],
                device_id=s.other, device_id_type=MESH,
            ).wait_recv()

    keep.wait()
    for cp in stores:
        cp.wait()
    for cp in pairs + sent + bulk + pc + echo:
        cp.wait_send()
    for cp in fc:
        cp.wait()


def front_call(place, t, diag, x, base, coded):
    nc, nz = lax.axis_size(("child", "rx")), lax.axis_size("col")
    n = 2 * TILE
    dma = pltpu.SemaphoreType.DMA
    vm, smem = IN_VMEM, pl.BlockSpec(memory_space=pltpu.SMEM)
    piece, code = x.shape[2:], coded.shape[1:]
    scratch = [pltpu.VMEM((n, n), F32)] * 3 + [pltpu.VMEM((BASE, BASE), F32)] * 3
    scratch += [pltpu.VMEM((k,) + piece, x.dtype) for k in (nc, nc, nc)]
    scratch += [pltpu.VMEM(piece, x.dtype), pltpu.VMEM((nz,) + piece, x.dtype)]
    scratch += [pltpu.VMEM((2 * nc * code[0],) + code[1:], x.dtype), pltpu.VMEM(base.shape, F32)]
    scratch += [dma, dma((base.shape[0] // TILE,)), dma, dma] + [dma((nc,))] * 8 + [dma((2 * nz,)), dma((nz,))] + [dma((nc,))] * 4
    scratch += [dma((2 * nz,)), dma((nc,)), dma]
    shapes = [(2 * nc,) + piece, (nc,) + piece]
    return pl.pallas_call(
        front_kernel,
        out_shape=[jax.ShapeDtypeStruct(base.shape, F32)] + [jax.ShapeDtypeStruct(k, x.dtype) for k in shapes],
        in_specs=[smem, smem, vm, vm, ANY, ANY],
        out_specs=[ANY] * 3,
        scratch_shapes=scratch,
        compiler_params=pltpu.CompilerParams(collective_id=3, has_side_effects=True),
        name="front",
    )(place, t, diag, x, coded, base)


def body(child_blocks, child_panels, child_patterns, child_maps, parent_place, parent_front):
    ci = lax.axis_index("child")
    rx = lax.axis_index("rx")
    core = lax.axis_index("core")
    col = lax.axis_index("col")
    cores = lax.axis_size("core")
    rxn = lax.axis_size("rx")
    row = rx * cores + core
    rown = rxn * cores
    chips = lax.axis_size("child") * rxn
    chip = ci * rxn + rx
    group = ci * rown + row
    block = child_blocks[0]
    own = child_panels[0]
    depth = own.shape[1]
    width = block.shape[0]
    td = width // TILE
    blocks = child_maps.shape[1] // td
    rd = parent_front.shape[0] // TILE
    cd = parent_front.shape[1] // TILE
    slots_n = parent_place.shape[0]
    i32 = jnp.int32

    share = cd * TILE // (chips * cores)
    me = chip * cores + core
    pos = jnp.stack([ci, row, col, core, me, col * cd, chip]).astype(i32)

    def tile_at(block, group, pos, maps, place):
        return find(maps, place, pos[0], block, group, td, cd)[0]

    def shift(x, axes, d):
        n = lax.axis_size(axes)
        return lax.ppermute(x, axes, [(k, (k + d) % n) for k in range(n)])

    code = (td, CODED, TILE)
    heads = (pos, child_maps, parent_place)

    def pick(ds, extra):
        def column(z, pos, maps, place):
            d = sum(jnp.where(z == n, d, 0) for n, d in enumerate(ds))
            return 0, tile_at(pos[2], lax.rem(pos[2] + d, blocks), pos, maps, place)

        part = [pl.BlockSpec((TILE, depth), lambda z, pos, maps, place: (tile_at(pos[1], pos[2], pos, maps, place), 0))]
        return tile_call(
            functools.partial(pick_kernel, td, cd, len(ds)), (len(ds),), heads, (block, own) if extra else (block,),
            [pl.BlockSpec((width, TILE), column)] + part * extra,
            [jax.ShapeDtypeStruct(code, jnp.int16)] * len(ds) + [jax.ShapeDtypeStruct((TILE, depth), own.dtype)] * extra,
            [pl.BlockSpec(code, lambda z, *_: (0, 0, 0))] * len(ds)
            + [pl.BlockSpec((TILE, depth), lambda z, *_: (0, 0))] * extra,
            "pick", scratch=[pltpu.VMEM(code, jnp.int16)],
        )

    order = sorted(range(1, blocks), key=lambda d: -min(d, blocks - d))
    (x,) = pick(order[:1], False)
    *rest, part = pick(order[1:], True)
    raw = [None] * blocks
    for d, x in zip(order, [x] + rest):
        raw[d] = shift(x, "col", d)
    raw[0] = tile_call(
        column_kernel, (1,), heads, (block,),
        [pl.BlockSpec((width, TILE), lambda z, pos, maps, place: (0, tile_at(pos[2], pos[2], pos, maps, place)))],
        jax.ShapeDtypeStruct((td, TILE, TILE), F32), pl.BlockSpec((td, TILE, TILE), lambda z, *_: (0, 0, 0)), "column",
    )

    smem = pl.BlockSpec(memory_space=pltpu.SMEM)
    dims = (td, cd, rd, chips, blocks, cores, rown)
    sizes = [(chips + 2,), (chips, blocks), (8, 4), (7, cd), (5, rd * cd)]
    rowt, fac, diagt, stript, fint = pl.pallas_call(
        functools.partial(plan_kernel, dims),
        in_specs=[smem] * 4, out_specs=[smem] * 5, name="plan",
        out_shape=[jax.ShapeDtypeStruct(z, i32) for z in sizes],
        scratch_shapes=[pltpu.SMEM((2, slots_n), i32)],
    )(pos, child_maps, parent_place, child_patterns)

    partner = panel_gather(part)
    diag_part = tile_call(
        diag_kernel, (3,), (diagt,), (block, parent_front, own, partner),
        [
            pl.BlockSpec((TILE, TILE), lambda k, t: (t[0, k], t[1, k])),
            pl.BlockSpec((TILE, TILE), lambda k, t: (t[2, k], t[3, k])),
            pl.BlockSpec((TILE, depth), lambda k, t: (t[0, k], 0)),
            pl.BlockSpec((1, TILE, depth), lambda k, t: (t[7, k], 0, 0)),
        ],
        jax.ShapeDtypeStruct((3 * TILE, TILE), F32),
        pl.BlockSpec((TILE, TILE), lambda k, t: (k, 0)), "diag",
    )
    diag_part = sum_plane(diag_part)
    diag_part, raw = lax.optimization_barrier((diag_part, raw))
    diagonal, strip_rows, coded = update_call(rowt, fac, diag_part, own, partner, raw)
    pieces = (cores, chips, share + META, 2 * TILE)
    strips = tile_call(
        strip_kernel, (1,), (stript,), (strip_rows, parent_front, parent_front),
        [
            pl.BlockSpec(strip_rows.shape, lambda k, t: (0, 0, 0)),
            pl.BlockSpec((TILE, cd * TILE), lambda k, t: (t[0, 0], 0)),
            pl.BlockSpec((TILE, cd * TILE), lambda k, t: (t[0, 1], 0)),
        ],
        jax.ShapeDtypeStruct(pieces, jnp.int16),
        pl.BlockSpec(pieces, lambda k, t: (0, 0, 0, 0)), "strip",
        scratch=[pltpu.VMEM((cd * TILE, 2 * TILE), F32)],
    )
    acc, wc, wr = front_call(parent_place, fint, diagonal, strips, parent_front, coded)

    per = 2
    return tile_call(
        final_kernel, (rd, cd // per), (fint,), (acc, wr, wc),
        [
            pl.BlockSpec((TILE, per * TILE), lambda i, j, t: (i, j)),
            pl.BlockSpec(wr.shape, lambda i, j, t: (0, 0, 0)),
            pl.BlockSpec(wc.shape, lambda i, j, t: (0, 0, 0)),
        ],
        jax.ShapeDtypeStruct(parent_front.shape, F32),
        pl.BlockSpec((TILE, per * TILE), lambda i, j, t: (i, j)), "final",
        scratch=[pltpu.VMEM((n * TILE, 6 * TILE), BF16) for n in (rd, cd)],
    )


def solution(mesh):
    child, row, col = mesh.devices.shape
    cores = child * row // col
    fine = Mesh(mesh.devices.reshape(child, row // cores, cores, col), ("child", "rx", "core", "col"))
    return jax.shard_map(
        body,
        mesh=fine,
        in_specs=(
            P("child", ("rx", "core"), "col"),
            P("child", ("rx", "core"), None),
            P(),
            P(),
            P(),
            P(("child", "rx", "core"), "col"),
        ),
        out_specs=P(("child", "rx", "core"), "col"),
        check_vma=False,
    )
```

```python
import functools
import math

import jax
import jax.numpy as jnp
from jax import lax
from jax.experimental import pallas as pl
from jax.experimental.pallas import tpu as pltpu
from jax.sharding import Mesh, PartitionSpec as P

TILE = 256
F32 = jnp.float32
BF16 = jnp.bfloat16
META = 16
CODED = TILE + META
FULL = 32767.0
NT = (((1,), (1,)), ((), ()))
NN = (((1,), (0,)), ((), ()))


def dot(a, b, dims):
    return lax.dot_general(a, b, dims, preferred_element_type=F32)


def split(x):
    hi = x.astype(BF16)
    return hi, (x - hi.astype(F32)).astype(BF16)


def tile_call(kernel, grid, tables, operands, in_specs, out_shape, out_spec, name, cost=None, scratch=()):
    return pl.pallas_call(
        kernel,
        grid_spec=pltpu.PrefetchScalarGridSpec(
            num_scalar_prefetch=len(tables), grid=grid, in_specs=in_specs, out_specs=out_spec,
            scratch_shapes=list(scratch),
        ),
        out_shape=out_shape,
        name=name,
        cost_estimate=cost,
    )(*tables, *operands)


def powers(k):
    h = jnp.floor(k * 0.5)
    return jnp.exp2(h), jnp.exp2(k - h)


def encode(x):
    top = jnp.maximum(jnp.max(jnp.abs(x), axis=0, keepdims=True), 1e-30)
    k = jnp.ceil(jnp.log2(top) + 1e-3)
    p, r = powers(-k)
    part = jnp.clip(jnp.ceil(top * p * r * FULL), 1.0, FULL)
    q = jnp.floor(x * ((FULL * FULL / part) * p * r) + 0.5).astype(jnp.int32)
    ids = lax.broadcasted_iota(jnp.int32, (META, x.shape[1]), 0)
    meta = jnp.where(ids == 0, k.astype(jnp.int32), jnp.where(ids == 1, part.astype(jnp.int32), 0))
    return q.astype(jnp.int16), meta.astype(jnp.int16)


def decode(code):
    n = code.shape[0] - META
    meta = code[n:, :].astype(jnp.int32).astype(F32)
    p, r = powers(meta[0:1, :])
    return code[:n, :].astype(jnp.int32).astype(F32) * (meta[1:2, :] * (1.0 / (FULL * FULL)) * p * r)


def find(maps, place, child, block, group, td, width):
    at = jnp.int32(0)
    ok = jnp.int32(0)
    for t in range(td):
        hit = place[maps[child, block * td + t]] // width == group
        at = jnp.where(hit, t, at)
        ok = jnp.where(hit, 1, ok)
    return at, ok


def pick_kernel(td, cd, count, pos, maps, place, src, *refs):
    z = pl.program_id(0)
    tmp = refs[-1]
    for r in range(td):
        q, meta = encode(src[r * TILE : (r + 1) * TILE, :])
        tmp[r, :TILE, :] = q
        tmp[r, TILE:, :] = meta
    outs = refs[-1 - count : -1] if len(refs) == count + 1 else refs[1 : 1 + count]
    for d, out in enumerate(outs):

        @pl.when(z == d)
        def _(out=out):
            out[...] = tmp[...]

    if len(refs) > count + 1:
        panel, part = refs[0], refs[-2]

        @pl.when(z == 0)
        def _():
            ok = find(maps, place, pos[0], pos[1], pos[2], td, cd)[1]
            part[...] = jnp.where(ok != 0, panel[...], jnp.zeros_like(panel))


def plan_kernel(dims, pos, maps, place, pat, rowt, fac, diagt, stript, fint, inv):
    td, cd, rd, chips, blocks, cores, rown = dims
    ci, row, col, core = pos[0], pos[1], pos[2], pos[3]
    group = ci * rown + row
    chip = pos[6]
    rxn = chips // 2
    slots_n, tiles_n = place.shape[0], maps.shape[1]

    @pl.loop(0, slots_n)
    def _(k):
        inv[0, k] = -1
        inv[1, k] = -1

    @pl.loop(0, tiles_n)
    def _(k):
        inv[0, place[maps[0, k]]] = k
        inv[1, place[maps[1, k]]] = k

    from_col = [lax.rem(col + blocks - d, blocks) for d in range(blocks)]
    cols = [find(maps, place, ci, b, col, td, cd) for b in from_col]
    for d in range(chips):
        at, ok = find(maps, place, ci, row, lax.rem(chip + d, chips), td, cd)
        rowt[d] = at
        for n, (b, (tile, good)) in enumerate(zip(from_col, cols)):
            fac[d, n] = pat[ci, row * td + at, b * td + tile] * ok * good
    e = (place[0], place[1])
    ie = (inv[ci, e[0]], inv[ci, e[1]])
    le = [jnp.maximum(i, 0) for i in ie]
    own = [((ie[a] >= 0) & (le[a] // td == row)).astype(jnp.int32) for a in range(2)]
    for a in range(2):
        rowt[chips + a] = jnp.where(own[a] != 0, lax.rem(e[a] // cd + chips - chip, chips), -1)
        for b in range(a + 1):
            k = a + b
            live = own[a] * (ie[b] >= 0).astype(jnp.int32) * pat[ci, le[a], le[b]]
            diagt[0, k] = le[a] % td
            diagt[1, k] = le[b] % td
            diagt[2, k] = e[a] % rd
            diagt[3, k] = e[b] % cd
            diagt[4, k] = live * (le[b] // td == col).astype(jnp.int32)
            diagt[5, k] = ((e[a] // rd == group) & (e[b] // cd == col)).astype(jnp.int32)
            diagt[6, k] = live * (e[b] // cd == col).astype(jnp.int32)
            diagt[7, k] = le[b] // td
        stript[0, a] = e[a] % rd

        for q in range(cd):
            slot = col * cd + q
            iq = inv[ci, slot]
            free = ((slot != e[0]) & (slot != e[1])).astype(jnp.int32)
            stript[1 + a, q] = jnp.maximum(iq, 0) // td
            stript[3 + a, q] = own[a] * free * (iq >= 0).astype(jnp.int32)
            stript[5 + a, q] = free * (e[a] // rd == group).astype(jnp.int32)
    for k in range(2, cd):
        stript[0, k] = 0

    @pl.loop(0, rd * cd)
    def _(k):
        slot = col * cd + k % cd
        for c in range(2):
            r, t = inv[c, group * rd + k // cd], inv[c, slot]
            ok = ((r >= 0) & (t >= 0)).astype(jnp.int32)
            source = jnp.maximum(r, 0) // td
            far = (source % cores != core).astype(jnp.int32)
            turn = far * chips + lax.rem(chip + chips - (c * rxn + source // cores), chips)
            fint[2 * c, k] = turn * blocks + jnp.maximum(t, 0) // td
            fint[2 * c + 1, k] = ok
        fint[4, k] = jnp.where(slot == e[0], 1, jnp.where(slot == e[1], 2, 0))


def diag_kernel(t, blk, front, ea, eb, out):
    k = pl.program_id(0)
    x = jnp.where(t[4, k] != 0, blk[...], 0.0) + jnp.where(t[5, k] != 0, front[...], 0.0)
    out[...] = x - jnp.where(t[6, k] != 0, dot(ea[...], eb[0], NT), 0.0)


def column_kernel(pos, maps, place, src, out):
    for r in range(out.shape[0]):
        out[r] = src[r * TILE : (r + 1) * TILE, :]


def strip_kernel(t, upd, f0, f1, out, g):
    cd = t.shape[1]
    some = sum(t[n, q] for n in range(3, 7) for q in range(cd))

    @pl.when(some == 0)
    def _():
        out[...] = jnp.zeros_like(out)

    @pl.when(some != 0)
    def _():
        g[...] = jnp.zeros_like(g)
        for q in range(cd):
            for a, f in enumerate((f0, f1)):

                @pl.when(t[3 + a, q] + t[5 + a, q] != 0)
                def _(q=q, a=a, f=f):
                    at = pl.ds(pl.multiple_of(t[1 + a, q] * TILE, TILE), TILE)
                    x = jnp.where(t[3 + a, q] != 0, upd[a, :, at], 0.0)
                    x = x + jnp.where(t[5 + a, q] != 0, f[:, q * TILE : (q + 1) * TILE], 0.0)
                    g[q * TILE : (q + 1) * TILE, a * TILE : (a + 1) * TILE] = x.T

        n = out.shape[2] - META
        for p in range(out.shape[1]):
            for k in range(out.shape[0]):
                m = p * out.shape[0] + k
                code, meta = encode(g[m * n : (m + 1) * n, :])
                out[k, p, :n, :] = code
                out[k, p, n:, :] = meta


def final_kernel(t, front, wr, wc, out, rows, cols):
    i, j = pl.program_id(0), pl.program_id(1)
    per = out.shape[1] // TILE
    base = (i * pl.num_programs(1) + j) * per
    width = 2 * TILE

    @pl.when(base == 0)
    def _():
        for src, dst, low in ((wr, rows, 2), (wc, cols, 1)):
            n = src.shape[1] - META
            for p in range(src.shape[0]):
                at = pl.ds(p * n, n)
                hi, lo = split(decode(src[p]))
                for m in range(3):
                    dst[at, m * width : (m + 1) * width] = lo if m == low else hi

    ri = pl.ds(pl.multiple_of(i * TILE, TILE), TILE)
    cj = pl.ds(pl.multiple_of(j * TILE * per, TILE), TILE * per)
    out[...] = front[...] - dot(rows[ri, :], cols[cj, :], NT)
    for m in range(per):
        at = slice(m * TILE, (m + 1) * TILE)
        for n in range(2):

            @pl.when(t[4, base + m] == n + 1)
            def _(n=n, at=at):
                hi = rows[ri, n * TILE : (n + 1) * TILE]
                lo = rows[ri, 2 * width + n * TILE : 2 * width + (n + 1) * TILE]
                out[:, at] = hi.astype(F32) + lo.astype(F32)


MESH = pl.DeviceIdType.MESH


class Spot:
    def __init__(self):
        self.ci, self.rx = lax.axis_index("child"), lax.axis_index("rx")
        self.core, self.col = lax.axis_index("core"), lax.axis_index("col")
        self.rxn, self.cores, self.cols = lax.axis_size("rx"), lax.axis_size("core"), lax.axis_size("col")
        self.chips = lax.axis_size("child") * self.rxn
        self.chip = self.ci * self.rxn + self.rx
        self.other = {"core": 1 - self.core}

    def id(self, chip, core=None):
        core = self.core if core is None else core
        return {"child": chip // self.rxn, "rx": lax.rem(chip, self.rxn), "core": core}

    def turn(self, at, d, n):
        return lax.rem(at + (d % n), n)


def greet(ids):
    bar = pltpu.get_barrier_semaphore()
    for i in ids:
        pl.semaphore_signal(bar, inc=1, device_id=i, device_id_type=MESH)
    pl.semaphore_wait(bar, len(ids))


def push(src, dst, send, recv, to):
    cp = pltpu.make_async_remote_copy(
        src_ref=src, dst_ref=dst, send_sem=send, recv_sem=recv, device_id=to, device_id_type=MESH
    )
    cp.start()
    return cp


def remote_call(kernel, operands, out_shape, out_specs, scratch, cid, name, flops=0):
    return pl.pallas_call(
        kernel,
        out_shape=out_shape,
        in_specs=[pl.BlockSpec(memory_space=pltpu.VMEM)] * len(operands),
        out_specs=out_specs,
        scratch_shapes=scratch,
        compiler_params=pltpu.CompilerParams(collective_id=cid, has_side_effects=True),
        cost_estimate=pl.CostEstimate(flops=flops, bytes_accessed=1 << 20, transcendentals=0),
        name=name,
    )(*operands)


ANY = pl.BlockSpec(memory_space=pl.ANY)
IN_VMEM = pl.BlockSpec(memory_space=pltpu.VMEM)


def panel_kernel(x, out, loc, ss, rs, fs, fr):
    s = Spot()
    n = s.rxn
    me = s.rx * s.cores + s.core
    peers = [{"rx": s.turn(s.rx, d, n)} for d in range(1, n)]
    greet(peers + [s.other])
    keep = pltpu.make_async_copy(x, out.at[me], loc)
    keep.start()
    cps = [push(x, out.at[me], ss.at[d], rs.at[d], to) for d, to in enumerate(peers, 1)]
    fwd = [push(x, out.at[me], fs.at[0], fr.at[0], s.other)]
    for d, cp in enumerate(cps, 1):
        cp.wait_recv()
        at = s.turn(s.rx, -d, n) * s.cores + s.core
        fwd.append(push(out.at[at], out.at[at], fs.at[d], fr.at[d], s.other))
    keep.wait()
    for cp in cps:
        cp.wait_send()
    for cp in fwd:
        cp.wait()


def panel_gather(x):
    n = lax.axis_size("rx")
    shape = (n * lax.axis_size("core"),) + x.shape
    dma = pltpu.SemaphoreType.DMA
    return remote_call(
        panel_kernel, (x,), jax.ShapeDtypeStruct(shape, x.dtype), ANY,
        [dma, dma((n,)), dma((n,)), dma((n,)), dma((n,))], 0, "panels",
    )


def sum_kernel(x, part, half, mine, got, ss0, rs0, ss1, rs1):
    s = Spot()
    nc = s.chips
    chips = [s.turn(s.chip, d, nc) for d in range(1, nc)]
    greet([s.other] + [s.id(t) for t in chips])
    cp = push(x.at[1 - s.core], half, ss0, rs0, s.other)
    cp.wait()
    mine[...] = x[s.core] + half[...]
    cps = [push(mine.at[t], got.at[d], ss1.at[d], rs1.at[d], s.id(t)) for d, t in enumerate(chips)]
    for cp in cps:
        cp.wait()
    total = mine[s.chip]
    for d in range(nc - 1):
        total = total + got[d]
    part[...] = total


def sum_plane(x):
    nc, nz = lax.axis_size(("child", "rx")), lax.axis_size("col")
    part = (nz, x.shape[0] // (2 * nc * nz), x.shape[1])
    half = (nc,) + part
    dma = pltpu.SemaphoreType.DMA
    vm = [pltpu.VMEM(z, F32) for z in (half, half, (nc - 1,) + part)]
    return remote_call(
        sum_kernel, (x.reshape((2,) + half),), jax.ShapeDtypeStruct(part, F32), IN_VMEM,
        vm + [dma, dma, dma((nc,)), dma((nc,))], 1, "total"
    )


def update_kernel(rowt, fac, part, own, partner, raw0, *refs):
    s = Spot()
    nc, nz = s.chips, s.cols
    raws = refs[: nz - 1]
    out, strip, coded, zgot, ss2, rs2, ss3, rs3, ss4, rs4, ss5, rs5 = refs[nz - 1 :]
    chips = [s.turn(s.chip, d, nc) for d in range(1, nc)]
    cols = [s.turn(s.col, d, nz) for d in range(1, nz)]

    def one(p, carry):
        r = rowt[p]
        panel = own[r]
        for d in range(nz):
            b = s.turn(s.col, -d, nz)
            at = pl.ds(pl.multiple_of(b * TILE, TILE), TILE)
            u = (decode(raws[d - 1][r]) if d else raw0[r]) - dot(panel, partner[b], NT)
            u = jnp.where(fac[p, d] != 0, u, 0.0)
            for a in range(2):
                strip[a, :, at] = jnp.where(rowt[nc + a] == p, u, strip[a, :, at])
            q, meta = encode(u)
            coded[p, b, :TILE, :] = q
            coded[p, b, TILE:, :] = meta
        return carry

    def work(n):
        lax.fori_loop(nc * n // 4, nc * (n + 1) // 4, one, 0)

    greet([s.other] + [s.id(t) for t in chips] + [{"col": t} for t in cols])
    cps = [push(part.at[t], zgot.at[d], ss2.at[d], rs2.at[d], {"col": t}) for d, t in enumerate(cols)]
    strip[...] = jnp.zeros_like(strip)
    work(0)
    for cp in cps:
        cp.wait()
    total = part[s.col]
    for d in range(nz - 1):
        total = total + zgot[d]
    out[s.core, s.chip, s.col] = total

    def send_z(d, t):
        own = out.at[s.core, s.chip, s.col]
        return push(own, own, ss3.at[d], rs3.at[d], {"col": t})

    def send_xy(z, n):
        own = out.at[s.core, s.chip, z]
        return [push(own, own, ss4.at[n, d], rs4.at[n, d], s.id(t)) for d, t in enumerate(chips)]

    def send_core(c, z, n, m):
        own = out.at[s.core, c, z]
        return push(own, own, ss5.at[n, m], rs5.at[n, m], s.other)

    zc = [send_z(d, t) for d, t in enumerate(cols)]
    xy = [send_xy(s.col, 0)]
    cc = [send_core(s.chip, s.col, 0, 0)]
    work(1)
    for n in range(1, nz):
        z = s.turn(s.col, -n, nz)
        zc[n - 1].wait_recv()
        xy.append(send_xy(z, n))
        cc.append(send_core(s.chip, z, n, 0))
    work(2)
    for n in range(nz):
        for d in range(nc - 1):
            xy[n][d].wait_recv()
            cc.append(send_core(s.turn(s.chip, -(d + 1), nc), s.turn(s.col, -n, nz), n, d + 1))
    work(3)
    for cp in zc + [x for row in xy for x in row]:
        cp.wait_send()
    for cp in cc:
        cp.wait()


def update_call(rowt, fac, part, own, partner, raw):
    nc, nz = lax.axis_size(("child", "rx")), lax.axis_size("col")
    dma, vm, smem = pltpu.SemaphoreType.DMA, IN_VMEM, pl.BlockSpec(memory_space=pltpu.SMEM)
    out, strip, coded = pl.pallas_call(
        update_kernel,
        out_shape=[
            jax.ShapeDtypeStruct((2, nc) + part.shape, F32),
            jax.ShapeDtypeStruct((2, TILE, nz * TILE), F32),
            jax.ShapeDtypeStruct((nc, nz, CODED, TILE), jnp.int16),
        ],
        in_specs=[smem, smem] + [vm] * (3 + nz),
        out_specs=[vm] * 3,
        scratch_shapes=[pltpu.VMEM((nz - 1,) + part.shape[1:], F32)] + [dma((nz,))] * 4 + [dma((nz, nc))] * 4,
        compiler_params=pltpu.CompilerParams(collective_id=2, has_side_effects=True),
        name="update",
    )(rowt, fac, part, own.reshape((-1, TILE) + own.shape[1:]), partner, *raw)
    return out.reshape(-1, TILE), strip, coded


BASE = 128
WIDE = 8


def base_inverse(a_ref, d_ref, x_ref):
    n, step = a_ref.shape[0], 8
    ids = lax.broadcasted_iota(jnp.int32, (step, n), 0)
    lanes = lax.broadcasted_iota(jnp.int32, (step, n), 1)
    a = [a_ref[i * step : (i + 1) * step, :] for i in range(n // step)]
    x = [(lanes == ids + i * step).astype(F32) for i in range(n // step)]
    for j in range(0, n, WIDE):
        c0 = j // step
        chunks = range(c0, n // step)
        cols = [[jnp.broadcast_to(a[i][:, j + t : j + t + 1], (step, n)) for i in chunks] for t in range(WIDE)]
        at = [j + t - c0 * step for t in range(WIDE)]
        rows = [a[c0][p : p + 1, :] for p in at]
        xrows = [x[c0][p : p + 1, :] for p in at]
        for t in range(WIDE):
            pivot = cols[t][0][at[t] : at[t] + 1, :]
            d_ref[j + t : j + t + 1, :] = pivot
            inv = 1.0 / pivot
            low = [c * inv for c in cols[t]]
            low[0] = jnp.where(ids > at[t], low[0], 0.0)
            for s in range(t + 1, WIDE):
                f = cols[t][0][at[s] : at[s] + 1, :]
                g = f * inv
                cols[s] = [c - l * f for c, l in zip(cols[s], low)]
                rows[s] = rows[s] - g * rows[t]
                xrows[s] = xrows[s] - g * xrows[t]
            for n_, i in enumerate(chunks):
                a[i] = a[i] - low[n_] * rows[t]
                x[i] = x[i] - low[n_] * xrows[t]
    for i in range(n // step):
        x_ref[i * step : (i + 1) * step, :] = x[i] * (1.0 / jnp.sqrt(d_ref[i * step : (i + 1) * step, :]))


def factor_steps(a_in, y, full, a, blk, piv, inv):
    n = a.shape[0]
    high = functools.partial(lax.dot_general, precision=lax.Precision.HIGHEST, preferred_element_type=F32)
    ids = lax.broadcasted_iota(jnp.int32, (n, n), 0)
    a[:TILE, :TILE] = a_in[:TILE, :]
    a[TILE:, :TILE] = a_in[TILE : 2 * TILE, :]
    a[:TILE, TILE:] = a_in[TILE : 2 * TILE, :].T
    a[TILE:, TILE:] = a_in[2 * TILE :, :]
    full[...] = a[...]
    y[...] = (ids == lax.broadcasted_iota(jnp.int32, (n, n), 1)).astype(F32)

    for k in range(0, n, BASE):
        at, end = slice(k, k + BASE), k + BASE
        blk[...] = a[at, at]
        base_inverse(blk, piv, inv)
        yk = high(inv[...], y[at, :end], NN)
        y[at, :end] = yk
        if end < n:
            low = high(a[end:, at], inv[...], NT)
            a[end:, end:] = a[end:, end:] - high(low, low, NT)
            y[end:, :end] = y[end:, :end] - high(low, yk, NN)


def front_kernel(
    place, tab, diag, x, coded, base, *refs
):
    s = Spot()
    nc, nz = s.chips, s.cols
    acc, wc, wr = refs[:3]
    c0, far = coded.at[0], [coded.at[d] for d in range(1, nc)]
    blocks = coded.shape[1]
    (y, full, a, blk, piv, inv, half_in, mine, got, piece, zbuf, buf, sums,
     load, store, loc, keep_sem, hs, hr, cs, cr, bs, br, es, er, zs, zr, ps, pr, fs, fr, ws, wx, wl) = refs[3:]
    half = wr.shape[0]
    n = piece.shape[0] - META
    me = s.chip * s.cores + s.core
    slot = lax.rem(me, half)
    count = nc * s.cores
    chips = [s.turn(s.chip, d, nc) for d in range(1, nc)]
    plane = [s.turn(me, d, count) for d in range(1, count)]
    greet([s.id(t // s.cores, lax.rem(t, s.cores)) for t in plane] + [{"col": s.turn(s.col, d, nz)} for d in range(1, nz)])

    def spot(n):
        return buf.at[pl.ds(n * blocks, blocks)]

    pairs = [push(x.at[1 - s.core, t], half_in.at[d], hs.at[d], hr.at[d], s.other) for d, t in enumerate(chips + [s.chip])]
    fetch = pltpu.make_async_copy(base, sums, load)
    fetch.start()
    keep0 = pltpu.make_async_copy(c0, spot(0), keep_sem)
    keep0.start()

    def send_bulk(d):
        return push(far[d - 1], spot(d), bs.at[d], br.at[d], s.id(chips[d - 1]))

    bulk = [send_bulk(1)]
    sent = []
    for d, t in enumerate(chips + [s.chip]):
        pairs[d].wait_recv()
        q, meta = encode(decode(x[s.core, t]) + decode(half_in[d]))
        mine[d, :n, :] = q
        mine[d, n:, :] = meta
        if d < nc - 1:
            sent.append(push(mine.at[d], got.at[d], cs.at[d], cr.at[d], s.id(t)))
    bulk += [send_bulk(d) for d in range(2, nc)]
    echo = [push(c0, spot(nc), es.at[0], er.at[0], s.other)]

    factor_steps(diag, y, full, a, blk, piv, inv)

    g = decode(mine[nc - 1])
    for d, cp in enumerate(sent):
        cp.wait_recv()
        g = g + decode(got[d])
    unit = math.gcd(n, TILE)
    rows = []
    for u in range(n // unit):
        first = me * n + u * unit
        z = g[u * unit : (u + 1) * unit, :]
        for k in range(2):
            own = full[pl.ds(pl.multiple_of(k * TILE + lax.rem(first, TILE), unit), unit), :]
            z = jnp.where(s.col * (count * n // TILE) + first // TILE == place[k], own, z)
        rows.append(z)
    g = jnp.concatenate(rows, axis=0)
    w = lax.dot_general(g, y[...], NT, precision=lax.Precision.HIGHEST, preferred_element_type=F32)
    q, meta = encode(w)
    piece[:n, :] = q
    piece[n:, :] = meta
    x = piece

    def hand(src, z, d):
        here = jnp.logical_and(z == s.chip, s.ci == s.core)

        @pl.when(here)
        def _():
            pltpu.make_async_copy(src, wr.at[slot], wl).start()

        @pl.when(jnp.logical_not(here))
        def _():
            push(src, wr.at[slot], ws.at[d], wx.at[slot], s.id(z, s.ci))

    def handed(src, z, d):
        here = jnp.logical_and(z == s.chip, s.ci == s.core)

        @pl.when(here)
        def _():
            pltpu.make_async_copy(src, wr.at[slot], wl).wait()

        @pl.when(jnp.logical_not(here))
        def _():
            pltpu.make_async_remote_copy(
                src_ref=src, dst_ref=wr.at[slot], send_sem=ws.at[d], recv_sem=wx.at[slot],
                device_id=s.id(z, s.ci), device_id_type=MESH,
            ).wait_send()

    def hop(src, z, way, d):
        to = s.col + way

        @pl.when(jnp.logical_and(to >= 0, to < nz))
        def _():
            push(src, zbuf.at[z], zs.at[d], zr.at[z], {"col": to})

    def hopped(src, z, way, d):
        to = s.col + way

        @pl.when(jnp.logical_and(to >= 0, to < nz))
        def _():
            pltpu.make_async_remote_copy(
                src_ref=src, dst_ref=zbuf.at[z], send_sem=zs.at[d], recv_sem=zr.at[z],
                device_id={"col": to}, device_id_type=MESH,
            ).wait_send()

    hop(x, s.col, 1, 0)
    hop(x, s.col, -1, 1)
    hand(x, s.col, 0)
    keep = pltpu.make_async_copy(x, wc.at[me], loc)
    keep.start()
    pc = [push(x, wc.at[me], ps.at[d], pr.at[d], s.id(t)) for d, t in enumerate(chips, 1)]
    fc = [push(x, wc.at[me], fs.at[0], fr.at[0], s.other)]

    def moved(d, way):
        z = s.col - way * d
        n = 2 * d + (way < 0)

        @pl.when(jnp.logical_and(z >= 0, z < nz))
        def _():
            src = zbuf.at[z]
            pltpu.make_async_remote_copy(
                src_ref=src, dst_ref=src, send_sem=zs.at[n], recv_sem=zr.at[z],
                device_id=s.other, device_id_type=MESH,
            ).wait_recv()
            hop(src, z, way, n)
            hand(src, z, n)

    def done(d, way):
        z = s.col - way * d
        n = 2 * d + (way < 0)

        @pl.when(jnp.logical_and(z >= 0, z < nz))
        def _():
            hopped(zbuf.at[z], z, way, n)
            handed(zbuf.at[z], z, n)

    rd, cd = base.shape[0] // TILE, base.shape[1] // TILE
    for d in range(1, nc):
        bulk[d - 1].wait_recv()
        echo.append(push(spot(d), spot(nc + d), es.at[d], er.at[d], s.other))

    def place_rows(i):
        def one(j, carry):
            k = i * cd + j
            at = pl.ds(pl.multiple_of(j * TILE, TILE), TILE)
            z = sums[i * TILE : (i + 1) * TILE, at]
            for c in range(2):
                z = z + jnp.where(tab[2 * c + 1, k] != 0, decode(buf[tab[2 * c, k]]), 0.0)
            sums[i * TILE : (i + 1) * TILE, at] = z
            return carry

        lax.fori_loop(0, cd, one, 0)
        rows = pl.ds(i * TILE, TILE)
        cp = pltpu.make_async_copy(sums.at[rows], acc.at[rows], store.at[i])
        cp.start()
        return cp

    steps = max(nz, nc, 2)
    stores = []
    for d in range(1, steps):
        if d < nz:
            moved(d, 1)
            moved(d, -1)
        if d < nc:
            pc[d - 1].wait_recv()
            at = s.turn(s.chip, -d, nc) * s.cores + s.core
            fc.append(push(wc.at[at], wc.at[at], fs.at[d], fr.at[d], s.other))
        if d == 1:
            fetch.wait()
            keep0.wait()
            for cp in echo:
                cp.wait_recv()
        stores += [place_rows(i) for i in range(rd) if i % (steps - 1) == d - 1]
    hopped(x, s.col, 1, 0)
    hopped(x, s.col, -1, 1)
    handed(x, s.col, 0)
    for d in range(1, nz):
        done(d, 1)
        done(d, -1)
    for j in range(half):

        @pl.when(jnp.logical_or(s.ci != s.core, slot != j))
        def _(j=j):
            pltpu.make_async_remote_copy(
                src_ref=wr.at[j], dst_ref=wr.at[j], send_sem=ws.at[0], recv_sem=wx.at[j],
                device_id=s.other, device_id_type=MESH,
            ).wait_recv()

    keep.wait()
    for cp in stores:
        cp.wait()
    for cp in pairs + sent + bulk + pc + echo:
        cp.wait_send()
    for cp in fc:
        cp.wait()


def front_call(place, t, diag, x, base, coded):
    nc, nz = lax.axis_size(("child", "rx")), lax.axis_size("col")
    n = 2 * TILE
    dma = pltpu.SemaphoreType.DMA
    vm, smem = IN_VMEM, pl.BlockSpec(memory_space=pltpu.SMEM)
    piece, code = x.shape[2:], coded.shape[1:]
    scratch = [pltpu.VMEM((n, n), F32)] * 3 + [pltpu.VMEM((BASE, BASE), F32)] * 3
    scratch += [pltpu.VMEM((k,) + piece, x.dtype) for k in (nc, nc, nc)]
    scratch += [pltpu.VMEM(piece, x.dtype), pltpu.VMEM((nz,) + piece, x.dtype)]
    scratch += [pltpu.VMEM((2 * nc * code[0],) + code[1:], x.dtype), pltpu.VMEM(base.shape, F32)]
    scratch += [dma, dma((base.shape[0] // TILE,)), dma, dma] + [dma((nc,))] * 8 + [dma((2 * nz,)), dma((nz,))] + [dma((nc,))] * 4
    scratch += [dma((2 * nz,)), dma((nc,)), dma]
    shapes = [(2 * nc,) + piece, (nc,) + piece]
    return pl.pallas_call(
        front_kernel,
        out_shape=[jax.ShapeDtypeStruct(base.shape, F32)] + [jax.ShapeDtypeStruct(k, x.dtype) for k in shapes],
        in_specs=[smem, smem, vm, vm, ANY, ANY],
        out_specs=[ANY] * 3,
        scratch_shapes=scratch,
        compiler_params=pltpu.CompilerParams(collective_id=3, has_side_effects=True),
        name="front",
    )(place, t, diag, x, coded, base)


def body(child_blocks, child_panels, child_patterns, child_maps, parent_place, parent_front):
    ci = lax.axis_index("child")
    rx = lax.axis_index("rx")
    core = lax.axis_index("core")
    col = lax.axis_index("col")
    cores = lax.axis_size("core")
    rxn = lax.axis_size("rx")
    row = rx * cores + core
    rown = rxn * cores
    chips = lax.axis_size("child") * rxn
    chip = ci * rxn + rx
    group = ci * rown + row
    block = child_blocks[0]
    own = child_panels[0]
    depth = own.shape[1]
    width = block.shape[0]
    td = width // TILE
    blocks = child_maps.shape[1] // td
    rd = parent_front.shape[0] // TILE
    cd = parent_front.shape[1] // TILE
    slots_n = parent_place.shape[0]
    i32 = jnp.int32

    share = cd * TILE // (chips * cores)
    me = chip * cores + core
    pos = jnp.stack([ci, row, col, core, me, col * cd, chip]).astype(i32)

    def tile_at(block, group, pos, maps, place):
        return find(maps, place, pos[0], block, group, td, cd)[0]

    def shift(x, axes, d):
        n = lax.axis_size(axes)
        return lax.ppermute(x, axes, [(k, (k + d) % n) for k in range(n)])

    code = (td, CODED, TILE)
    heads = (pos, child_maps, parent_place)

    def pick(ds, extra):
        def column(z, pos, maps, place):
            d = sum(jnp.where(z == n, d, 0) for n, d in enumerate(ds))
            return 0, tile_at(pos[2], lax.rem(pos[2] + d, blocks), pos, maps, place)

        part = [pl.BlockSpec((TILE, depth), lambda z, pos, maps, place: (tile_at(pos[1], pos[2], pos, maps, place), 0))]
        return tile_call(
            functools.partial(pick_kernel, td, cd, len(ds)), (len(ds),), heads, (block, own) if extra else (block,),
            [pl.BlockSpec((width, TILE), column)] + part * extra,
            [jax.ShapeDtypeStruct(code, jnp.int16)] * len(ds) + [jax.ShapeDtypeStruct((TILE, depth), own.dtype)] * extra,
            [pl.BlockSpec(code, lambda z, *_: (0, 0, 0))] * len(ds)
            + [pl.BlockSpec((TILE, depth), lambda z, *_: (0, 0))] * extra,
            "pick", scratch=[pltpu.VMEM(code, jnp.int16)],
        )

    order = sorted(range(1, blocks), key=lambda d: -min(d, blocks - d))
    (x,) = pick(order[:1], False)
    *rest, part = pick(order[1:], True)
    raw = [None] * blocks
    for d, x in zip(order, [x] + rest):
        raw[d] = shift(x, "col", d)
    raw[0] = tile_call(
        column_kernel, (1,), heads, (block,),
        [pl.BlockSpec((width, TILE), lambda z, pos, maps, place: (0, tile_at(pos[2], pos[2], pos, maps, place)))],
        jax.ShapeDtypeStruct((td, TILE, TILE), F32), pl.BlockSpec((td, TILE, TILE), lambda z, *_: (0, 0, 0)), "column",
    )

    smem = pl.BlockSpec(memory_space=pltpu.SMEM)
    dims = (td, cd, rd, chips, blocks, cores, rown)
    sizes = [(chips + 2,), (chips, blocks), (8, 4), (7, cd), (5, rd * cd)]
    rowt, fac, diagt, stript, fint = pl.pallas_call(
        functools.partial(plan_kernel, dims),
        in_specs=[smem] * 4, out_specs=[smem] * 5, name="plan",
        out_shape=[jax.ShapeDtypeStruct(z, i32) for z in sizes],
        scratch_shapes=[pltpu.SMEM((2, slots_n), i32)],
    )(pos, child_maps, parent_place, child_patterns)

    partner = panel_gather(part)
    diag_part = tile_call(
        diag_kernel, (3,), (diagt,), (block, parent_front, own, partner),
        [
            pl.BlockSpec((TILE, TILE), lambda k, t: (t[0, k], t[1, k])),
            pl.BlockSpec((TILE, TILE), lambda k, t: (t[2, k], t[3, k])),
            pl.BlockSpec((TILE, depth), lambda k, t: (t[0, k], 0)),
            pl.BlockSpec((1, TILE, depth), lambda k, t: (t[7, k], 0, 0)),
        ],
        jax.ShapeDtypeStruct((3 * TILE, TILE), F32),
        pl.BlockSpec((TILE, TILE), lambda k, t: (k, 0)), "diag",
    )
    diag_part = sum_plane(diag_part)
    diag_part, raw = lax.optimization_barrier((diag_part, raw))
    diagonal, strip_rows, coded = update_call(rowt, fac, diag_part, own, partner, raw)
    pieces = (cores, chips, share + META, 2 * TILE)
    strips = tile_call(
        strip_kernel, (1,), (stript,), (strip_rows, parent_front, parent_front),
        [
            pl.BlockSpec(strip_rows.shape, lambda k, t: (0, 0, 0)),
            pl.BlockSpec((TILE, cd * TILE), lambda k, t: (t[0, 0], 0)),
            pl.BlockSpec((TILE, cd * TILE), lambda k, t: (t[0, 1], 0)),
        ],
        jax.ShapeDtypeStruct(pieces, jnp.int16),
        pl.BlockSpec(pieces, lambda k, t: (0, 0, 0, 0)), "strip",
        scratch=[pltpu.VMEM((cd * TILE, 2 * TILE), F32)],
    )
    acc, wc, wr = front_call(parent_place, fint, diagonal, strips, parent_front, coded)

    per = 3
    return tile_call(
        final_kernel, (rd, cd // per), (fint,), (acc, wr, wc),
        [
            pl.BlockSpec((TILE, per * TILE), lambda i, j, t: (i, j)),
            pl.BlockSpec(wr.shape, lambda i, j, t: (0, 0, 0)),
            pl.BlockSpec(wc.shape, lambda i, j, t: (0, 0, 0)),
        ],
        jax.ShapeDtypeStruct(parent_front.shape, F32),
        pl.BlockSpec((TILE, per * TILE), lambda i, j, t: (i, j)), "final",
        scratch=[pltpu.VMEM((n * TILE, 6 * TILE), BF16) for n in (rd, cd)],
    )


def solution(mesh):
    child, row, col = mesh.devices.shape
    cores = child * row // col
    fine = Mesh(mesh.devices.reshape(child, row // cores, cores, col), ("child", "rx", "core", "col"))
    return jax.shard_map(
        body,
        mesh=fine,
        in_specs=(
            P("child", ("rx", "core"), "col"),
            P("child", ("rx", "core"), None),
            P(),
            P(),
            P(),
            P(("child", "rx", "core"), "col"),
        ),
        out_specs=P(("child", "rx", "core"), "col"),
        check_vma=False,
    )
```
